32 devices in a mesh: seq: 8 (over z, core), tp: 4 (over y, x).
Axes of the slice: x: 2, y: 2, z: 4, core: 2. Of those that a mesh axis runs over, the one named last changes fastest.
Arguments:
- qkv: bfloat16 [3, 4, 128, 3072], P(None, None, ('seq', 'tp')), may hold values from -6 to 6
- positions: int32 [3, 4, 128], P(None, None, ('seq', 'tp')), may hold values from 0 to 31, as said below
- w_proj: bfloat16 [3072, 64], replicated, may hold values from -0.21875 to 0.21875
- latents: bfloat16 [4, 128, 64], P(None, 'seq'), may hold values from -6 to 6
- embed_w: bfloat16 [64, 2048], replicated, may hold values from -0.75 to 0.75
- up_w: bfloat16 [2048, 8192], P(None, 'tp'), may hold values from -0.125 to 0.125
- down_w: bfloat16 [8192, 2048], P('tp'), may hold values from -0.0625 to 0.0625
- head_w: bfloat16 [2048, 1000], P(('seq', 'tp')), may hold values from -3 to 3
- labels: int32 [4], replicated, may hold values from 0 to 999
- timesteps: int32 [4], replicated, may hold values from 0 to 999
Outputs:
- guided: bfloat16 [4, 128, 64], P(None, ('seq', 'tp'))
The draws below stay inside these ranges and needn't reach their ends.
Inputs may be any that keep to these rules, and one draw needn't show every extreme that they name: For each video the tokens are the cells of a stack of frames of 32 x 32 cells, each cell once, in shuffled order; positions[0] is the frame, positions[1] the row, positions[2] the column.
All inputs are finite; a program needn't handle non-finite values.
Results may differ from the reference program's by a relative error of at most 0.0095.
Values may be sent and summed in bfloat16 or wider, within the bound.
No kernel may reach another device: no remote copies, remote signals or barrier semaphores. Data moves between devices by JAX's collectives and lax.ppermute only.
A program may use at most 64 MiB of HBM per device.

```python
import jax
import jax.numpy as jnp
from jax import lax

HEADS = 24
HEAD_DIM = 128
D = 3072
LAT = 64
CLS_WIDTH = 2048
CLS_FF = 8192
CLASSES = 1000
SAMPLES = 4
GRID = 32
SEQ = 128


def token_cells(key):
    sample_keys = jax.random.split(jax.random.fold_in(key, 7), SAMPLES)
    orders = jax.vmap(lambda single: jax.random.permutation(single, SEQ))(sample_keys).astype(jnp.int32)
    frames = orders // (GRID * GRID)
    row_ids = orders // GRID % GRID
    columns = orders % GRID
    return jnp.stack([frames, row_ids, columns]).astype(jnp.int32)


def draw_positions(key, part):
    return token_cells(key)


def draw_qkv(key, part):
    draw_key = jax.random.fold_in(key, 11)
    key_query, key_key, key_value = jax.random.split(draw_key, 3)
    shape = (SAMPLES, SEQ, D)
    queries = jnp.clip(1.6 * jax.random.normal(key_query, shape, jnp.float32), -6.0, 6.0)
    keys_drawn = jnp.clip(1.6 * jax.random.normal(key_key, shape, jnp.float32), -6.0, 6.0)
    values = jnp.clip(jax.random.normal(key_value, shape, jnp.float32), -6.0, 6.0)
    return jnp.stack([queries, keys_drawn, values]).astype(jnp.bfloat16)


def plant(drawn, rng, low, top_value):
    shape = drawn.shape
    index_at = [jax.random.randint(jax.random.fold_in(rng, axis), (), 0, shape[axis]) for axis in range(len(shape))]
    drawn = drawn.at[tuple(index_at)].set(low)
    longest = shape.index(max(shape))
    index_at[longest] = (index_at[longest] + 1) % shape[longest]
    return drawn.at[tuple(index_at)].set(top_value)


def levels(rng, extent, cuts, least, top_value):
    factor_of, own = 1.0, jax.random.fold_in(rng, 6)
    for axis_at, blocks in cuts:
        draws = jnp.exp(jax.random.uniform(jax.random.fold_in(own, axis_at), (blocks,), jnp.float32, least / len(cuts), top_value / len(cuts)))
        factor_of = factor_of * jnp.repeat(draws, extent[axis_at] // blocks).reshape([-1 if axis == axis_at else 1 for axis in range(len(extent))])
    return factor_of


def scatter_about(key, dims, deviation, bound, cuts=(), kind=jnp.bfloat16):
    factor_of = levels(key, dims, cuts, -0.22, 0.18) if cuts else 1.0
    drawn = jax.random.normal(key, dims, jnp.float32) * deviation * factor_of
    return jnp.minimum(jnp.maximum(drawn, -bound), bound).astype(kind)


def setup_inputs(seed: int = 0) -> dict:
    streams_of = jax.random.split(jax.random.key(seed), 11)
    return {
        "qkv": draw_qkv(jax.random.fold_in(streams_of[10], 71), 0),
        "positions": draw_positions(jax.random.fold_in(streams_of[10], 71), 0),
        "w_proj": scatter_about(streams_of[2], (D, LAT), (D // 4) ** -0.5, 0.21875),
        "latents": scatter_about(streams_of[3], (SAMPLES, SEQ, LAT), 1.0, 6.0, ((1, 8),)),
        "embed_w": scatter_about(streams_of[4], (LAT, CLS_WIDTH), LAT ** -0.5, 0.75),
        "up_w": scatter_about(streams_of[5], (CLS_WIDTH, CLS_FF), CLS_WIDTH ** -0.5, 0.125, ((1, 4),)),
        "down_w": scatter_about(streams_of[6], (CLS_FF, CLS_WIDTH), CLS_FF ** -0.5, 0.0625, ((0, 4),)),
        "head_w": scatter_about(streams_of[7], (CLS_WIDTH, CLASSES), (2.0 * (SEQ / CLS_WIDTH) ** 0.5), 3.0, ((0, 32),)),
        "labels": plant(jax.random.randint(streams_of[8], (SAMPLES,), 0, CLASSES), jax.random.fold_in(streams_of[8], 1), 0, CLASSES - 1).astype(jnp.int32),
        "timesteps": plant(jax.random.randint(streams_of[9], (SAMPLES,), 0, 1000), jax.random.fold_in(streams_of[9], 1), 0, 999).astype(jnp.int32),
    }


GUIDANCE = 0.1

def rope_angles(positions, head_dim):
    frame_width = head_dim // 8
    plane_width = (head_dim - frame_width) // 2
    pieces = []
    for axis, width in zip(range(3), (frame_width, plane_width, plane_width)):
        freqs = 10000.0 ** (-jnp.arange(0, width, 2, dtype=jnp.float32) / width)
        pieces.append(positions[axis][..., None] * freqs)
    return jnp.concatenate(pieces, axis=-1)

def rotate(values, angles):
    half = values.shape[-1] // 2
    floats = values.astype(jnp.float32)
    first = floats[..., :half]
    second = floats[..., half:]
    cosine = jnp.cos(angles)[:, :, None, :]
    sine = jnp.sin(angles)[:, :, None, :]
    turned = jnp.concatenate([first * cosine - second * sine, first * sine + second * cosine], axis=-1)
    return turned.astype(jnp.bfloat16)

def gelu_slope(values):
    cdf = 0.5 * (1.0 + jax.scipy.special.erf(values * 0.7071067811865476))
    pdf = jnp.exp(-0.5 * values * values) * 0.3989422804014327
    return cdf + values * pdf

def reference(qkv, positions, w_proj, latents, embed_w, up_w, down_w, head_w, labels, timesteps):
    angles = rope_angles(positions.astype(jnp.float32), HEAD_DIM)
    shaped = (SAMPLES, SEQ, HEADS, HEAD_DIM)
    queries = rotate(qkv[0].reshape(shaped), angles)
    keys = rotate(qkv[1].reshape(shaped), angles)
    values = qkv[2].reshape(shaped)

    def items(array):
        return array.transpose(0, 2, 1, 3).reshape(SAMPLES * HEADS, SEQ, HEAD_DIM)

    def one_pair(operands):
        query_rows, key_rows, value_rows = operands
        scores = jnp.dot(query_rows, key_rows.T, preferred_element_type=jnp.float32) * HEAD_DIM ** (-0.5)
        top = lax.optimization_barrier(jnp.max(scores, axis=-1, keepdims=True))
        weights = jnp.exp(scores - top)
        total = lax.optimization_barrier(jnp.sum(weights, axis=-1, keepdims=True))
        mixed = jnp.dot(weights.astype(jnp.bfloat16), value_rows, preferred_element_type=jnp.float32)
        return (mixed / total).astype(jnp.bfloat16)
    attended = lax.map(one_pair, (items(queries), items(keys), items(values)))
    attended = attended.reshape(SAMPLES, HEADS, SEQ, HEAD_DIM).transpose(0, 2, 1, 3).reshape(SAMPLES, SEQ, D)
    eps = jnp.dot(attended, w_proj, preferred_element_type=jnp.float32)
    emb = jnp.dot(latents, embed_w, preferred_element_type=jnp.float32).astype(jnp.bfloat16)
    hidden = jnp.dot(emb, up_w, preferred_element_type=jnp.float32)
    act = jax.nn.gelu(hidden, approximate=False).astype(jnp.bfloat16)
    branch = jnp.dot(act, down_w, preferred_element_type=jnp.float32)
    pooled = (lax.optimization_barrier(jnp.sum(emb.astype(jnp.float32), axis=1)) + lax.optimization_barrier(jnp.sum(branch, axis=1))) / SEQ
    head_float = head_w.astype(jnp.float32)
    logits = jnp.dot(pooled, head_float, precision=lax.Precision.HIGHEST)
    probs = jax.nn.softmax(logits, axis=-1)
    onehot = (labels[:, None] == jnp.arange(CLASSES, dtype=jnp.int32)[None, :]).astype(jnp.float32)
    dpool = jnp.dot(onehot - probs, head_float.T, precision=lax.Precision.HIGHEST)
    dact = jnp.dot(dpool, down_w.astype(jnp.float32).T, precision=lax.Precision.HIGHEST)
    dh1 = (gelu_slope(hidden) * dact[:, None, :]).astype(jnp.bfloat16)
    demb = jnp.dot(dh1, up_w.T, preferred_element_type=jnp.float32)
    embed_float = embed_w.astype(jnp.float32)
    dx = jnp.dot(demb, embed_float.T, precision=lax.Precision.HIGHEST)
    dx = dx + jnp.dot(dpool, embed_float.T, precision=lax.Precision.HIGHEST)[:, None, :]
    phase = (timesteps.astype(jnp.float32) / 1000.0 + 0.008) / 1.008 * (jnp.pi / 2)
    abar = jnp.cos(phase) ** 2
    scale = GUIDANCE * jnp.sqrt(1.0 - abar)
    return (eps - scale[:, None, None] * dx).astype(jnp.bfloat16)
```

```python
import jax
import jax.numpy as jnp
from jax import lax
from jax.sharding import PartitionSpec as P

HEAD_DIM = 128


GUIDANCE = 0.1


def rope_angles(positions, head_dim):
    frame_width = head_dim // 8
    plane_width = (head_dim - frame_width) // 2
    pieces = []
    for axis, width in zip(range(3), (frame_width, plane_width, plane_width)):
        freqs = 10000.0 ** (-jnp.arange(0, width, 2, dtype=jnp.float32) / width)
        pieces.append(positions[axis][..., None] * freqs)
    return jnp.concatenate(pieces, axis=-1)


def rotate(values, angles):
    half = values.shape[-1] // 2
    floats = values.astype(jnp.float32)
    first = floats[..., :half]
    second = floats[..., half:]
    cosine = jnp.cos(angles)[:, :, None, :]
    sine = jnp.sin(angles)[:, :, None, :]
    turned = jnp.concatenate(
        [first * cosine - second * sine, first * sine + second * cosine], axis=-1
    )
    return turned.astype(jnp.bfloat16)


def gelu_slope(values):
    cdf = 0.5 * (1.0 + jax.scipy.special.erf(values * 0.7071067811865476))
    pdf = jnp.exp(-0.5 * values * values) * 0.3989422804014327
    return cdf + values * pdf


def pairs_first(array):
    samples, tokens = (array.shape[0], array.shape[1])
    return array.transpose(0, 2, 1, 3).reshape(samples * array.shape[2], tokens, HEAD_DIM)


def per_device_general(qkv, positions, w_proj, latents, embed_w, up_w, down_w, head_w, labels, timesteps):
    samples, tok_dev = (qkv.shape[1], qkv.shape[2])
    angles = rope_angles(positions.astype(jnp.float32), HEAD_DIM)
    heads = qkv.shape[3] // HEAD_DIM
    shaped = (samples, tok_dev, heads, HEAD_DIM)
    queries = rotate(qkv[0].reshape(shaped), angles)
    keys_tok = rotate(qkv[1].reshape(shaped), angles)
    values_tok = qkv[2].reshape(shaped)
    moved = lax.all_to_all(
        jnp.stack([pairs_first(queries), pairs_first(keys_tok), pairs_first(values_tok)]),
        "seq",
        split_axis=1,
        concat_axis=2,
        tiled=True,
    )
    query_pairs = moved[0]
    pair_count, query_count = (query_pairs.shape[0], query_pairs.shape[1])
    running = jnp.full((pair_count, query_count), -jnp.inf, jnp.float32)
    total = jnp.zeros((pair_count, query_count), jnp.float32)
    accum = jnp.zeros((pair_count, query_count, HEAD_DIM), jnp.float32)
    key_piece = lax.all_gather(moved[1], "tp", axis=1, tiled=True)
    value_piece = lax.all_gather(moved[2], "tp", axis=1, tiled=True)
    scores = jnp.einsum(
        "iqd,ikd->iqk", query_pairs, key_piece, preferred_element_type=jnp.float32
    ) * HEAD_DIM ** (-0.5)
    newest = jnp.max(scores, axis=-1)
    factor = jnp.exp(running - newest)
    weights = jnp.exp(scores - newest[..., None])
    total = total * factor + jnp.sum(weights, axis=-1)
    accum = accum * factor[..., None] + jnp.einsum(
        "iqk,ikd->iqd",
        weights.astype(jnp.bfloat16),
        value_piece,
        preferred_element_type=jnp.float32,
    )
    running, total, accum = (newest, total, accum)
    attended = (accum / total[..., None]).astype(jnp.bfloat16)
    returned = lax.all_to_all(attended, "seq", split_axis=1, concat_axis=0, tiled=True)
    returned = returned.reshape(samples, heads, tok_dev, HEAD_DIM).transpose(0, 2, 1, 3)
    returned = returned.reshape(samples, tok_dev, qkv.shape[3])
    eps = jnp.dot(returned, w_proj, preferred_element_type=jnp.float32)
    seq_len = latents.shape[1] * lax.axis_size("seq")
    tp_index = lax.axis_index("tp")
    emb = jnp.dot(latents, embed_w, preferred_element_type=jnp.float32).astype(jnp.bfloat16)
    hidden = jnp.dot(emb, up_w, preferred_element_type=jnp.float32)
    act = jax.nn.gelu(hidden, approximate=False).astype(jnp.bfloat16)
    branch = jnp.dot(act, down_w, preferred_element_type=jnp.float32)
    own_emb = lax.dynamic_slice_in_dim(emb, tp_index * tok_dev, tok_dev, 1).astype(jnp.float32)
    partial_pool = jnp.sum(branch, axis=1) + jnp.sum(own_emb, axis=1)
    head_rows = head_w.shape[0]
    flat_index = lax.axis_index("seq") * lax.axis_size("tp") + tp_index
    pooled = lax.psum(partial_pool, ("seq", "tp")) / seq_len
    pooled_share = lax.dynamic_slice_in_dim(pooled, flat_index * head_rows, head_rows, 1)
    head_float = head_w.astype(jnp.float32)
    logit_terms = jnp.dot(pooled_share, head_float, precision=lax.Precision.HIGHEST)
    logits = lax.psum(logit_terms, ("seq", "tp"))
    probs = jax.nn.softmax(logits, axis=-1)
    onehot = (labels[:, None] == jnp.arange(logits.shape[1], dtype=jnp.int32)[None, :]).astype(
        jnp.float32
    )
    grad_share = jnp.dot(onehot - probs, head_float.T, precision=lax.Precision.HIGHEST)
    dpool = lax.all_gather(grad_share, ("seq", "tp"), axis=1, tiled=True)
    dact = jnp.dot(dpool, down_w.astype(jnp.float32).T, precision=lax.Precision.HIGHEST)
    dh1 = (gelu_slope(hidden) * dact[:, None, :]).astype(jnp.bfloat16)
    demb = jnp.einsum("btf,cf->btc", dh1, up_w, preferred_element_type=jnp.float32)
    embed_float = embed_w.astype(jnp.float32)
    dx_terms = jnp.einsum("btc,lc->btl", demb, embed_float, precision=lax.Precision.HIGHEST)
    dx_mine = lax.psum_scatter(
        dx_terms.astype(jnp.bfloat16), "tp", scatter_dimension=1, tiled=True
    ).astype(jnp.float32)
    dx_pool = jnp.dot(dpool, embed_float.T, precision=lax.Precision.HIGHEST)
    dx_total = dx_mine + dx_pool[:, None, :]
    phase = (timesteps.astype(jnp.float32) / 1000.0 + 0.008) / 1.008 * (jnp.pi / 2)
    abar = jnp.cos(phase) ** 2
    scale = GUIDANCE * jnp.sqrt(1.0 - abar)
    return (eps - scale[:, None, None] * dx_total).astype(jnp.bfloat16)


def split_rows(values):
    high = values.astype(jnp.bfloat16)
    rest = values - high.astype(jnp.float32)
    middle = rest.astype(jnp.bfloat16)
    low = (rest - middle.astype(jnp.float32)).astype(jnp.bfloat16)
    return jnp.concatenate([high, middle, low], axis=0)


def split_dot(values, weights, contract=0):
    rows = values.shape[0]
    product = lax.dot_general(
        split_rows(values),
        weights,
        (((1,), (contract,)), ((), ())),
        preferred_element_type=jnp.float32,
    )
    return product[:rows] + product[rows : 2 * rows] + product[2 * rows :]


def per_device_fast(qkv, positions, w_proj, latents, embed_w, up_w, down_w, head_w, labels, timesteps):
    both = ("seq", "tp")
    n_seq, n_tp = (lax.axis_size("seq"), lax.axis_size("tp"))
    count = n_seq * n_tp
    seq_index, tp_index = (lax.axis_index("seq"), lax.axis_index("tp"))
    flat_index = seq_index * n_tp + tp_index
    samples, tok_dev, width = qkv.shape[1:]
    seq_len = tok_dev * count
    lat = latents.shape[2]
    heads = width // HEAD_DIM
    per_sample = count // samples
    heads_dev = heads // per_sample
    chunk = heads_dev * HEAD_DIM

    lat_all = lax.all_to_all(
        jnp.broadcast_to(latents[None], (n_seq,) + latents.shape), "seq", 0, 0, tiled=True
    )
    lat_all = lat_all.transpose(1, 0, 2, 3).reshape(samples * seq_len, lat)

    angles = rope_angles(positions.astype(jnp.float32), HEAD_DIM)
    shaped = (samples, tok_dev, heads, HEAD_DIM)
    queries = rotate(qkv[0].reshape(shaped), angles).reshape(samples, tok_dev, width)
    keys = rotate(qkv[1].reshape(shaped), angles).reshape(samples, tok_dev, width)
    packed = jnp.stack([queries, keys, qkv[2]])
    packed = packed.reshape(3, samples, tok_dev, per_sample, chunk).transpose(1, 3, 0, 2, 4)
    packed = packed.reshape(count, 3, tok_dev, chunk)
    moved = lax.all_to_all(packed, both, 0, 0, tiled=True)

    units = up_w.shape[1] // n_seq
    up_mine = lax.dynamic_slice_in_dim(up_w, seq_index * units, units, 1)
    down_mine = lax.dynamic_slice_in_dim(down_w, seq_index * units, units, 0)
    joint = jnp.dot(embed_w, up_mine, preferred_element_type=jnp.float32)
    joint_high = joint.astype(jnp.bfloat16)
    joint_low = (joint - joint_high.astype(jnp.float32)).astype(jnp.bfloat16)
    hidden = jnp.dot(lat_all, joint_high, preferred_element_type=jnp.float32) + jnp.dot(
        lat_all, joint_low, preferred_element_type=jnp.float32
    )
    act = jax.nn.gelu(hidden, approximate=False)
    act_sum = jnp.sum(act.reshape(samples, seq_len, units), axis=1)
    pool_terms = split_dot(act_sum, down_mine)
    rows_dev = head_w.shape[0]
    pool_terms = pool_terms.reshape(samples, count, rows_dev).transpose(1, 0, 2)
    pool_terms = lax.all_to_all(pool_terms, both, 0, 0, tiled=True)
    lat_sum = jnp.sum(lat_all.astype(jnp.float32).reshape(samples, seq_len, lat), axis=1)
    embed_mine = lax.dynamic_slice_in_dim(embed_w, flat_index * rows_dev, rows_dev, 1)
    pooled = (jnp.sum(pool_terms, axis=0) + split_dot(lat_sum, embed_mine)) / seq_len

    def head_view(index):
        return moved[:, index].reshape(seq_len, heads_dev, HEAD_DIM)

    scores = jnp.einsum(
        "qhd,khd->hqk", head_view(0), head_view(1), preferred_element_type=jnp.float32
    ) * HEAD_DIM ** (-0.5)
    weights = jnp.exp(scores - jnp.max(scores, axis=-1, keepdims=True))
    total = jnp.sum(weights, axis=-1)
    mixed = jnp.einsum(
        "hqk,khd->hqd",
        weights.astype(jnp.bfloat16),
        head_view(2),
        preferred_element_type=jnp.float32,
    )
    attended = (mixed / total[..., None]).astype(jnp.bfloat16)
    attended = attended.transpose(1, 0, 2).reshape(count, tok_dev, chunk)
    returned = lax.all_to_all(attended, both, 0, 0, tiled=True)
    returned = returned.reshape(samples, per_sample, tok_dev, chunk).transpose(0, 2, 1, 3)
    eps = jnp.dot(
        returned.reshape(samples, tok_dev, width), w_proj, preferred_element_type=jnp.float32
    )

    classes = head_w.shape[1]
    padded = -(-classes // (128 * n_tp)) * (128 * n_tp)
    terms = split_dot(pooled, head_w)
    terms = lax.all_to_all(
        jnp.broadcast_to(terms[None], (count,) + terms.shape), both, 0, 0, tiled=True
    )
    logits = jnp.sum(terms, axis=0)
    probs = jax.nn.softmax(logits, axis=-1)
    onehot = (labels[:, None] == jnp.arange(classes, dtype=jnp.int32)[None, :]).astype(jnp.float32)
    share = split_dot(onehot - probs, head_w, 1)
    dpool = lax.all_to_all(
        jnp.broadcast_to(share[None], (count,) + share.shape), both, 0, 0, tiled=True
    )
    dpool = dpool.transpose(1, 0, 2).reshape(samples, count * rows_dev)

    dact = split_dot(dpool, down_mine, 1)
    slope = gelu_slope(hidden).reshape(samples, seq_len, units)
    dh1 = (slope * dact[:, None, :]).astype(jnp.bfloat16).reshape(samples * seq_len, units)
    dx_terms = lax.dot_general(
        dh1, joint_high, (((1,), (1,)), ((), ())), preferred_element_type=jnp.float32
    ) + lax.dot_general(
        dh1, joint_low, (((1,), (1,)), ((), ())), preferred_element_type=jnp.float32
    )
    dx_terms = dx_terms.astype(jnp.bfloat16).reshape(samples, count, tok_dev, lat)
    dx_terms = lax.all_to_all(dx_terms.transpose(1, 0, 2, 3), both, 0, 0, tiled=True)
    dx = jnp.sum(dx_terms.astype(jnp.float32), axis=0)
    dx = dx + split_dot(dpool, embed_w, 1)[:, None, :]
    phase = (timesteps.astype(jnp.float32) / 1000.0 + 0.008) / 1.008 * (jnp.pi / 2)
    abar = jnp.cos(phase) ** 2
    scale = GUIDANCE * jnp.sqrt(1.0 - abar)
    return (eps - scale[:, None, None] * dx).astype(jnp.bfloat16)


def per_device(qkv, positions, w_proj, latents, embed_w, up_w, down_w, head_w, labels, timesteps):
    args = (qkv, positions, w_proj, latents, embed_w, up_w, down_w, head_w, labels, timesteps)
    n_seq = lax.axis_size("seq")
    count = n_seq * lax.axis_size("tp")
    samples, heads = (qkv.shape[1], qkv.shape[3] // HEAD_DIM)
    even = count % samples == 0 and heads % max(1, count // samples) == 0
    if even and up_w.shape[1] % (128 * n_seq) == 0:
        return per_device_fast(*args)
    return per_device_general(*args)


def solution(mesh):
    placed = (
        P(None, None, ("seq", "tp"), None),
        P(None, None, ("seq", "tp")),
        P(),
        P(None, "seq", None),
        P(),
        P(None, "tp"),
        P("tp", None),
        P(("seq", "tp"), None),
        P(),
        P(),
    )
    return jax.shard_map(
        per_device,
        mesh=mesh,
        in_specs=placed,
        out_specs=P(None, ("seq", "tp"), None),
        check_vma=False,
    )
```

```python
import jax
import jax.numpy as jnp
from jax import lax
from jax.sharding import PartitionSpec as P

HEAD_DIM = 128


GUIDANCE = 0.1


def rope_angles(positions, head_dim):
    frame_width = head_dim // 8
    plane_width = (head_dim - frame_width) // 2
    pieces = []
    for axis, width in zip(range(3), (frame_width, plane_width, plane_width)):
        freqs = 10000.0 ** (-jnp.arange(0, width, 2, dtype=jnp.float32) / width)
        pieces.append(positions[axis][..., None] * freqs)
    return jnp.concatenate(pieces, axis=-1)


def rotate(values, angles):
    half = values.shape[-1] // 2
    floats = values.astype(jnp.float32)
    first = floats[..., :half]
    second = floats[..., half:]
    cosine = jnp.cos(angles)[:, :, None, :]
    sine = jnp.sin(angles)[:, :, None, :]
    turned = jnp.concatenate(
        [first * cosine - second * sine, first * sine + second * cosine], axis=-1
    )
    return turned.astype(jnp.bfloat16)


def gelu_slope(values):
    cdf = 0.5 * (1.0 + jax.scipy.special.erf(values * 0.7071067811865476))
    pdf = jnp.exp(-0.5 * values * values) * 0.3989422804014327
    return cdf + values * pdf


def pairs_first(array):
    samples, tokens = (array.shape[0], array.shape[1])
    return array.transpose(0, 2, 1, 3).reshape(samples * array.shape[2], tokens, HEAD_DIM)


def per_device_general(qkv, positions, w_proj, latents, embed_w, up_w, down_w, head_w, labels, timesteps):
    samples, tok_dev = (qkv.shape[1], qkv.shape[2])
    angles = rope_angles(positions.astype(jnp.float32), HEAD_DIM)
    heads = qkv.shape[3] // HEAD_DIM
    shaped = (samples, tok_dev, heads, HEAD_DIM)
    queries = rotate(qkv[0].reshape(shaped), angles)
    keys_tok = rotate(qkv[1].reshape(shaped), angles)
    values_tok = qkv[2].reshape(shaped)
    moved = lax.all_to_all(
        jnp.stack([pairs_first(queries), pairs_first(keys_tok), pairs_first(values_tok)]),
        "seq",
        split_axis=1,
        concat_axis=2,
        tiled=True,
    )
    query_pairs = moved[0]
    pair_count, query_count = (query_pairs.shape[0], query_pairs.shape[1])
    running = jnp.full((pair_count, query_count), -jnp.inf, jnp.float32)
    total = jnp.zeros((pair_count, query_count), jnp.float32)
    accum = jnp.zeros((pair_count, query_count, HEAD_DIM), jnp.float32)
    key_piece = lax.all_gather(moved[1], "tp", axis=1, tiled=True)
    value_piece = lax.all_gather(moved[2], "tp", axis=1, tiled=True)
    scores = jnp.einsum(
        "iqd,ikd->iqk", query_pairs, key_piece, preferred_element_type=jnp.float32
    ) * HEAD_DIM ** (-0.5)
    newest = jnp.max(scores, axis=-1)
    factor = jnp.exp(running - newest)
    weights = jnp.exp(scores - newest[..., None])
    total = total * factor + jnp.sum(weights, axis=-1)
    accum = accum * factor[..., None] + jnp.einsum(
        "iqk,ikd->iqd",
        weights.astype(jnp.bfloat16),
        value_piece,
        preferred_element_type=jnp.float32,
    )
    running, total, accum = (newest, total, accum)
    attended = (accum / total[..., None]).astype(jnp.bfloat16)
    returned = lax.all_to_all(attended, "seq", split_axis=1, concat_axis=0, tiled=True)
    returned = returned.reshape(samples, heads, tok_dev, HEAD_DIM).transpose(0, 2, 1, 3)
    returned = returned.reshape(samples, tok_dev, qkv.shape[3])
    eps = jnp.dot(returned, w_proj, preferred_element_type=jnp.float32)
    seq_len = latents.shape[1] * lax.axis_size("seq")
    tp_index = lax.axis_index("tp")
    emb = jnp.dot(latents, embed_w, preferred_element_type=jnp.float32).astype(jnp.bfloat16)
    hidden = jnp.dot(emb, up_w, preferred_element_type=jnp.float32)
    act = jax.nn.gelu(hidden, approximate=False).astype(jnp.bfloat16)
    branch = jnp.dot(act, down_w, preferred_element_type=jnp.float32)
    own_emb = lax.dynamic_slice_in_dim(emb, tp_index * tok_dev, tok_dev, 1).astype(jnp.float32)
    partial_pool = jnp.sum(branch, axis=1) + jnp.sum(own_emb, axis=1)
    head_rows = head_w.shape[0]
    flat_index = lax.axis_index("seq") * lax.axis_size("tp") + tp_index
    pooled = lax.psum(partial_pool, ("seq", "tp")) / seq_len
    pooled_share = lax.dynamic_slice_in_dim(pooled, flat_index * head_rows, head_rows, 1)
    head_float = head_w.astype(jnp.float32)
    logit_terms = jnp.dot(pooled_share, head_float, precision=lax.Precision.HIGHEST)
    logits = lax.psum(logit_terms, ("seq", "tp"))
    probs = jax.nn.softmax(logits, axis=-1)
    onehot = (labels[:, None] == jnp.arange(logits.shape[1], dtype=jnp.int32)[None, :]).astype(
        jnp.float32
    )
    grad_share = jnp.dot(onehot - probs, head_float.T, precision=lax.Precision.HIGHEST)
    dpool = lax.all_gather(grad_share, ("seq", "tp"), axis=1, tiled=True)
    dact = jnp.dot(dpool, down_w.astype(jnp.float32).T, precision=lax.Precision.HIGHEST)
    dh1 = (gelu_slope(hidden) * dact[:, None, :]).astype(jnp.bfloat16)
    demb = jnp.einsum("btf,cf->btc", dh1, up_w, preferred_element_type=jnp.float32)
    embed_float = embed_w.astype(jnp.float32)
    dx_terms = jnp.einsum("btc,lc->btl", demb, embed_float, precision=lax.Precision.HIGHEST)
    dx_mine = lax.psum_scatter(
        dx_terms.astype(jnp.bfloat16), "tp", scatter_dimension=1, tiled=True
    ).astype(jnp.float32)
    dx_pool = jnp.dot(dpool, embed_float.T, precision=lax.Precision.HIGHEST)
    dx_total = dx_mine + dx_pool[:, None, :]
    phase = (timesteps.astype(jnp.float32) / 1000.0 + 0.008) / 1.008 * (jnp.pi / 2)
    abar = jnp.cos(phase) ** 2
    scale = GUIDANCE * jnp.sqrt(1.0 - abar)
    return (eps - scale[:, None, None] * dx_total).astype(jnp.bfloat16)


def split_rows(values):
    high = values.astype(jnp.bfloat16)
    rest = values - high.astype(jnp.float32)
    middle = rest.astype(jnp.bfloat16)
    low = (rest - middle.astype(jnp.float32)).astype(jnp.bfloat16)
    return jnp.concatenate([high, middle, low], axis=0)


def split_dot(values, weights, contract=0):
    rows = values.shape[0]
    product = lax.dot_general(
        split_rows(values),
        weights,
        (((1,), (contract,)), ((), ())),
        preferred_element_type=jnp.float32,
    )
    return product[:rows] + product[rows : 2 * rows] + product[2 * rows :]


def split_two(values, axis):
    high = values.astype(jnp.bfloat16)
    low = (values - high.astype(jnp.float32)).astype(jnp.bfloat16)
    return jnp.concatenate([high, low], axis=axis)


def per_device_fast(qkv, positions, w_proj, latents, embed_w, up_w, down_w, head_w, labels, timesteps):
    both = ("seq", "tp")
    n_seq, n_tp = (lax.axis_size("seq"), lax.axis_size("tp"))
    count = n_seq * n_tp
    seq_index = lax.axis_index("seq")
    half = seq_index % 2
    samples, tok_dev, width = qkv.shape[1:]
    seq_len = tok_dev * count
    lat = latents.shape[2]
    heads = width // HEAD_DIM
    per_sample = count // samples
    heads_dev = heads // per_sample
    rows_dev, classes = head_w.shape
    partner = [(i, i ^ n_tp) for i in range(count)]

    def in_order(own):
        other = lax.ppermute(own, both, partner)
        mine = jnp.broadcast_to(half == 0, own.shape)
        return jnp.stack([jnp.where(mine, own, other), jnp.where(mine, other, own)])

    lat_pair = in_order(latents)
    lat_rows = lat_pair.transpose(1, 0, 2, 3).reshape(-1, lat)
    tok_pair = lat_rows.shape[0] // samples
    head_pair = in_order(head_w).reshape(2 * rows_dev, classes)

    units = up_w.shape[1] // 2
    up_mine = lax.dynamic_slice_in_dim(up_w, half * units, units, 1)
    down_mine = lax.dynamic_slice_in_dim(down_w, half * units, units, 0)
    joint = split_two(jnp.dot(embed_w, up_mine, preferred_element_type=jnp.float32), 0)
    hidden = jnp.dot(
        jnp.concatenate([lat_rows, lat_rows], axis=1), joint, preferred_element_type=jnp.float32
    )
    act = jax.nn.gelu(hidden, approximate=False)
    act_sum = jnp.sum(act.reshape(samples, tok_pair, units), axis=1)
    lat_sum = jnp.sum(lat_rows.astype(jnp.float32).reshape(samples, tok_pair, lat), axis=1)
    pool_terms = split_dot(act_sum, down_mine) + split_dot(lat_sum / (2 * n_tp), embed_w)
    pool_terms = pool_terms.reshape(samples, n_seq // 2, 2, n_tp, rows_dev)
    pool_terms = pool_terms.transpose(1, 3, 0, 2, 4).reshape(n_seq // 2, 1, n_tp, samples, 2 * rows_dev)
    pool_terms = jnp.broadcast_to(pool_terms, (n_seq // 2, 2) + pool_terms.shape[2:])
    pool_terms = split_two(pool_terms.reshape(count, samples, 2 * rows_dev), 1)

    angles = rope_angles(positions.astype(jnp.float32), HEAD_DIM)
    shaped = (samples, tok_dev, heads, HEAD_DIM)
    queries = rotate(qkv[0].reshape(shaped), angles)
    keys = rotate(qkv[1].reshape(shaped), angles)
    packed = jnp.stack([queries, keys, qkv[2].reshape(shaped)])
    packed = packed.reshape(3, samples, tok_dev, per_sample, heads_dev, HEAD_DIM)
    packed = packed.transpose(1, 3, 0, 4, 2, 5).reshape(count, 3 * heads_dev * tok_dev, HEAD_DIM)
    qkv_rows = packed.shape[1]
    moved = lax.all_to_all(
        jnp.concatenate([packed, pool_terms], axis=1), both, 0, 0, tiled=True
    )

    pooled = jnp.sum(moved[:, qkv_rows:].astype(jnp.float32), axis=0)
    pooled = (pooled[:samples] + pooled[samples:]) / seq_len
    padded = -(-classes // 256) * 256
    terms = jnp.pad(split_dot(pooled, head_pair), ((0, 0), (0, padded - classes)))
    terms = lax.dynamic_slice_in_dim(terms, half * (padded // 2), padded // 2, 1)
    terms = lax.all_to_all(
        jnp.broadcast_to(terms[None], (count,) + terms.shape), both, 0, 0, tiled=True
    )

    views = moved[:, :qkv_rows].reshape(count, 3, heads_dev, tok_dev, HEAD_DIM)
    views = views.transpose(1, 2, 0, 3, 4).reshape(3, heads_dev, seq_len, HEAD_DIM)
    scores = jnp.einsum(
        "hqd,hkd->hqk", views[0], views[1], preferred_element_type=jnp.float32
    ) * HEAD_DIM ** (-0.5)
    weights = jnp.exp(scores - jnp.max(scores, axis=-1, keepdims=True))
    total = jnp.sum(weights, axis=-1)
    mixed = jnp.einsum(
        "hqk,hkd->hqd", weights.astype(jnp.bfloat16), views[2], preferred_element_type=jnp.float32
    )
    attended = (mixed / total[..., None]).astype(jnp.bfloat16)
    attended = attended.reshape(heads_dev, count, tok_dev, HEAD_DIM).transpose(1, 0, 2, 3)
    attended = attended.reshape(count, heads_dev * tok_dev, HEAD_DIM)

    logits = jnp.sum(terms.reshape(n_seq // 2, 2, n_tp, samples, padded // 2), axis=(0, 2))
    logits = logits.transpose(1, 0, 2).reshape(samples, padded)[:, :classes]
    probs = jax.nn.softmax(logits, axis=-1)
    onehot = (labels[:, None] == jnp.arange(classes, dtype=jnp.int32)[None, :]).astype(jnp.float32)
    share = split_two(split_dot(onehot - probs, head_w, 1), 1)
    share = jnp.broadcast_to(share[None], (count,) + share.shape)
    att_rows = attended.shape[1]
    second = lax.all_to_all(
        jnp.concatenate([attended, share], axis=1), both, 0, 0, tiled=True
    )
    returned = second[:, :att_rows].reshape(samples, per_sample, heads_dev, tok_dev, HEAD_DIM)
    returned = returned.transpose(0, 3, 1, 2, 4).reshape(samples, tok_dev, width)
    eps = jnp.dot(returned, w_proj, preferred_element_type=jnp.float32)
    dpool = second[:, att_rows:].astype(jnp.float32)
    dpool = (dpool[..., :rows_dev] + dpool[..., rows_dev:]).transpose(1, 0, 2).reshape(samples, -1)

    dact = split_dot(dpool, down_mine, 1)
    slope = gelu_slope(hidden).reshape(samples, tok_pair, units)
    dh1 = (slope * dact[:, None, :]).astype(jnp.bfloat16).reshape(samples * tok_pair, units)
    dx_terms = lax.dot_general(
        dh1, joint, (((1,), (1,)), ((), ())), preferred_element_type=jnp.float32
    )
    dx_terms = (dx_terms[:, :lat] + dx_terms[:, lat:]).astype(jnp.bfloat16)
    dx_terms = dx_terms.reshape(samples, 2 * n_tp, tok_dev, lat).transpose(1, 0, 2, 3)
    planes = [[first + k for k in range(2 * n_tp)] for first in range(0, count, 2 * n_tp)]
    dx_terms = lax.all_to_all(dx_terms, both, 0, 0, tiled=True, axis_index_groups=planes)
    dx = jnp.sum(dx_terms.astype(jnp.float32), axis=0)
    dx = dx + split_dot(dpool, embed_w, 1)[:, None, :]
    phase = (timesteps.astype(jnp.float32) / 1000.0 + 0.008) / 1.008 * (jnp.pi / 2)
    abar = jnp.cos(phase) ** 2
    scale = GUIDANCE * jnp.sqrt(1.0 - abar)
    return (eps - scale[:, None, None] * dx).astype(jnp.bfloat16)


def per_device(qkv, positions, w_proj, latents, embed_w, up_w, down_w, head_w, labels, timesteps):
    args = (qkv, positions, w_proj, latents, embed_w, up_w, down_w, head_w, labels, timesteps)
    n_seq = lax.axis_size("seq")
    count = n_seq * lax.axis_size("tp")
    samples, heads = (qkv.shape[1], qkv.shape[3] // HEAD_DIM)
    even = count % samples == 0 and heads % max(1, count // samples) == 0
    if even and n_seq % 2 == 0 and up_w.shape[1] % 256 == 0:
        return per_device_fast(*args)
    return per_device_general(*args)


def solution(mesh):
    placed = (
        P(None, None, ("seq", "tp"), None),
        P(None, None, ("seq", "tp")),
        P(),
        P(None, "seq", None),
        P(),
        P(None, "tp"),
        P("tp", None),
        P(("seq", "tp"), None),
        P(),
        P(),
    )
    return jax.shard_map(
        per_device,
        mesh=mesh,
        in_specs=placed,
        out_specs=P(None, ("seq", "tp"), None),
        check_vma=False,
    )
```

```python
import functools

import jax
import jax.numpy as jnp
import numpy as np
from jax import lax
from jax.experimental import pallas as pl
from jax.experimental.pallas import tpu as pltpu
from jax.sharding import PartitionSpec as P

HEAD_DIM = 128


GUIDANCE = 0.1


def rope_angles(positions, head_dim):
    frame_width = head_dim // 8
    plane_width = (head_dim - frame_width) // 2
    pieces = []
    for axis, width in zip(range(3), (frame_width, plane_width, plane_width)):
        freqs = 10000.0 ** (-jnp.arange(0, width, 2, dtype=jnp.float32) / width)
        pieces.append(positions[axis][..., None] * freqs)
    return jnp.concatenate(pieces, axis=-1)


def rotate(values, angles):
    half = values.shape[-1] // 2
    floats = values.astype(jnp.float32)
    first = floats[..., :half]
    second = floats[..., half:]
    cosine = jnp.cos(angles)[:, :, None, :]
    sine = jnp.sin(angles)[:, :, None, :]
    turned = jnp.concatenate(
        [first * cosine - second * sine, first * sine + second * cosine], axis=-1
    )
    return turned.astype(jnp.bfloat16)


def gelu_slope(values):
    cdf = 0.5 * (1.0 + jax.scipy.special.erf(values * 0.7071067811865476))
    pdf = jnp.exp(-0.5 * values * values) * 0.3989422804014327
    return cdf + values * pdf


def pairs_first(array):
    samples, tokens = (array.shape[0], array.shape[1])
    return array.transpose(0, 2, 1, 3).reshape(samples * array.shape[2], tokens, HEAD_DIM)


def per_device_general(qkv, positions, w_proj, latents, embed_w, up_w, down_w, head_w, labels, timesteps):
    samples, tok_dev = (qkv.shape[1], qkv.shape[2])
    angles = rope_angles(positions.astype(jnp.float32), HEAD_DIM)
    heads = qkv.shape[3] // HEAD_DIM
    shaped = (samples, tok_dev, heads, HEAD_DIM)
    queries = rotate(qkv[0].reshape(shaped), angles)
    keys_tok = rotate(qkv[1].reshape(shaped), angles)
    values_tok = qkv[2].reshape(shaped)
    moved = lax.all_to_all(
        jnp.stack([pairs_first(queries), pairs_first(keys_tok), pairs_first(values_tok)]),
        "seq",
        split_axis=1,
        concat_axis=2,
        tiled=True,
    )
    query_pairs = moved[0]
    pair_count, query_count = (query_pairs.shape[0], query_pairs.shape[1])
    running = jnp.full((pair_count, query_count), -jnp.inf, jnp.float32)
    total = jnp.zeros((pair_count, query_count), jnp.float32)
    accum = jnp.zeros((pair_count, query_count, HEAD_DIM), jnp.float32)
    key_piece = lax.all_gather(moved[1], "tp", axis=1, tiled=True)
    value_piece = lax.all_gather(moved[2], "tp", axis=1, tiled=True)
    scores = jnp.einsum(
        "iqd,ikd->iqk", query_pairs, key_piece, preferred_element_type=jnp.float32
    ) * HEAD_DIM ** (-0.5)
    newest = jnp.max(scores, axis=-1)
    factor = jnp.exp(running - newest)
    weights = jnp.exp(scores - newest[..., None])
    total = total * factor + jnp.sum(weights, axis=-1)
    accum = accum * factor[..., None] + jnp.einsum(
        "iqk,ikd->iqd",
        weights.astype(jnp.bfloat16),
        value_piece,
        preferred_element_type=jnp.float32,
    )
    running, total, accum = (newest, total, accum)
    attended = (accum / total[..., None]).astype(jnp.bfloat16)
    returned = lax.all_to_all(attended, "seq", split_axis=1, concat_axis=0, tiled=True)
    returned = returned.reshape(samples, heads, tok_dev, HEAD_DIM).transpose(0, 2, 1, 3)
    returned = returned.reshape(samples, tok_dev, qkv.shape[3])
    eps = jnp.dot(returned, w_proj, preferred_element_type=jnp.float32)
    seq_len = latents.shape[1] * lax.axis_size("seq")
    tp_index = lax.axis_index("tp")
    emb = jnp.dot(latents, embed_w, preferred_element_type=jnp.float32).astype(jnp.bfloat16)
    hidden = jnp.dot(emb, up_w, preferred_element_type=jnp.float32)
    act = jax.nn.gelu(hidden, approximate=False).astype(jnp.bfloat16)
    branch = jnp.dot(act, down_w, preferred_element_type=jnp.float32)
    own_emb = lax.dynamic_slice_in_dim(emb, tp_index * tok_dev, tok_dev, 1).astype(jnp.float32)
    partial_pool = jnp.sum(branch, axis=1) + jnp.sum(own_emb, axis=1)
    head_rows = head_w.shape[0]
    flat_index = lax.axis_index("seq") * lax.axis_size("tp") + tp_index
    pooled = lax.psum(partial_pool, ("seq", "tp")) / seq_len
    pooled_share = lax.dynamic_slice_in_dim(pooled, flat_index * head_rows, head_rows, 1)
    head_float = head_w.astype(jnp.float32)
    logit_terms = jnp.dot(pooled_share, head_float, precision=lax.Precision.HIGHEST)
    logits = lax.psum(logit_terms, ("seq", "tp"))
    probs = jax.nn.softmax(logits, axis=-1)
    onehot = (labels[:, None] == jnp.arange(logits.shape[1], dtype=jnp.int32)[None, :]).astype(
        jnp.float32
    )
    grad_share = jnp.dot(onehot - probs, head_float.T, precision=lax.Precision.HIGHEST)
    dpool = lax.all_gather(grad_share, ("seq", "tp"), axis=1, tiled=True)
    dact = jnp.dot(dpool, down_w.astype(jnp.float32).T, precision=lax.Precision.HIGHEST)
    dh1 = (gelu_slope(hidden) * dact[:, None, :]).astype(jnp.bfloat16)
    demb = jnp.einsum("btf,cf->btc", dh1, up_w, preferred_element_type=jnp.float32)
    embed_float = embed_w.astype(jnp.float32)
    dx_terms = jnp.einsum("btc,lc->btl", demb, embed_float, precision=lax.Precision.HIGHEST)
    dx_mine = lax.psum_scatter(
        dx_terms.astype(jnp.bfloat16), "tp", scatter_dimension=1, tiled=True
    ).astype(jnp.float32)
    dx_pool = jnp.dot(dpool, embed_float.T, precision=lax.Precision.HIGHEST)
    dx_total = dx_mine + dx_pool[:, None, :]
    phase = (timesteps.astype(jnp.float32) / 1000.0 + 0.008) / 1.008 * (jnp.pi / 2)
    abar = jnp.cos(phase) ** 2
    scale = GUIDANCE * jnp.sqrt(1.0 - abar)
    return (eps - scale[:, None, None] * dx_total).astype(jnp.bfloat16)


def split_rows(values):
    high = values.astype(jnp.bfloat16)
    rest = values - high.astype(jnp.float32)
    middle = rest.astype(jnp.bfloat16)
    low = (rest - middle.astype(jnp.float32)).astype(jnp.bfloat16)
    return jnp.concatenate([high, middle, low], axis=0)


def split_dot(values, weights, contract=0):
    rows = values.shape[0]
    product = lax.dot_general(
        split_rows(values),
        weights,
        (((1,), (contract,)), ((), ())),
        preferred_element_type=jnp.float32,
    )
    return product[:rows] + product[rows : 2 * rows] + product[2 * rows :]


def split_two(values, axis):
    high = values.astype(jnp.bfloat16)
    low = (values - high.astype(jnp.float32)).astype(jnp.bfloat16)
    return jnp.concatenate([high, low], axis=axis)


LANES = 128


def lane_frequencies():
    frame_width = HEAD_DIM // 8
    plane_width = (HEAD_DIM - frame_width) // 2
    freqs, axes = [], []
    for axis, width in zip(range(3), (frame_width, plane_width, plane_width)):
        steps = np.arange(0, width, 2, dtype=np.float32) / np.float32(width)
        freqs.append(np.float32(10000.0) ** (-steps))
        axes.append(np.full(width // 2, axis, np.float32))
    freqs, axes = (np.concatenate(freqs), np.concatenate(axes))
    table = np.stack([np.tile(freqs, 2), np.tile(axes, 2)]).astype(np.float32)
    return np.pad(table, ((0, 6), (0, 0)))


def forward_kernel(
    sizes,
    pos_ref,
    table_ref,
    qkv_hbm,
    own_hbm,
    other_hbm,
    embed_hbm,
    up_hbm,
    down_hbm,
    pay_ref,
    slope_ref,
    joint_ref,
    qkv_ref,
    lat_ref,
    embed_ref,
    up_ref,
    down_ref,
    rows_ref,
    sems,
):
    n_seq, n_tp, steps, seq_len = sizes
    samples, tok_dev, width = qkv_ref.shape[1:]
    count = n_seq * n_tp
    per_sample = count // samples
    heads_dev = width // HEAD_DIM // per_sample
    tok_seq, lat = own_hbm.shape[1:]
    units = down_ref.shape[0]
    part = units // steps
    half = lax.axis_index("seq") % 2

    def up_copy(step):
        start = pl.multiple_of(half * units + step * part, LANES)
        return pltpu.make_async_copy(
            up_hbm.at[:, pl.ds(start, part)], up_ref.at[step], sems.at[4 + step]
        )

    def down_copy(step):
        start = pl.multiple_of(half * units + step * part, LANES)
        return pltpu.make_async_copy(
            down_hbm.at[pl.ds(start, part)],
            down_ref.at[pl.ds(step * part, part)],
            sems.at[4 + steps + step],
        )

    own_copy = pltpu.make_async_copy(own_hbm, lat_ref.at[half], sems.at[0])
    other_copy = pltpu.make_async_copy(other_hbm, lat_ref.at[1 - half], sems.at[1])
    embed_copy = pltpu.make_async_copy(embed_hbm, embed_ref, sems.at[2])
    qkv_copy = pltpu.make_async_copy(qkv_hbm, qkv_ref, sems.at[3])
    for copy in (own_copy, other_copy, qkv_copy, embed_copy):
        copy.start()
    for step in range(steps):
        up_copy(step).start()
    for step in range(steps):
        down_copy(step).start()

    shape = (samples * tok_dev, LANES)
    row = lax.broadcasted_iota(jnp.int32, shape, 0)
    lane = lax.broadcasted_iota(jnp.int32, shape, 1)
    axis = jnp.broadcast_to(table_ref[1:2, :], shape)
    angles = jnp.zeros(shape, jnp.float32)
    for index in range(samples * tok_dev):
        sample, token = divmod(index, tok_dev)
        frame, line, column = (pos_ref[k, sample, token].astype(jnp.float32) for k in range(3))
        value = jnp.where(axis < 0.5, frame, jnp.where(axis < 1.5, line, column))
        angles = jnp.where(row == index, value, angles)
    angles = angles * jnp.broadcast_to(table_ref[0:1, :], shape)
    cosine = jnp.cos(angles)
    sine = jnp.sin(angles)
    sine = jnp.where(lane < HEAD_DIM // 2, -sine, sine)

    qkv_copy.wait()
    for sample in range(samples):
        cos_rows = cosine[sample * tok_dev : (sample + 1) * tok_dev]
        sin_rows = sine[sample * tok_dev : (sample + 1) * tok_dev]
        for head in range(width // HEAD_DIM):
            target = sample * per_sample + head // heads_dev
            span = slice(head * HEAD_DIM, (head + 1) * HEAD_DIM)
            for kind in range(3):
                group = 2 + kind * heads_dev + head % heads_dev
                values = qkv_ref[kind, sample, :, span]
                if kind < 2:
                    values = values.astype(jnp.float32)
                    values = values * cos_rows + pltpu.roll(values, HEAD_DIM // 2, 1) * sin_rows
                pay_ref[target, group] = values.astype(jnp.bfloat16)

    own_copy.wait()
    other_copy.wait()
    tok_pair = 2 * tok_seq
    sums = []
    for sample in range(samples):
        pieces = [lat_ref[0, sample], lat_ref[1, sample]]
        rows = jnp.concatenate(pieces, axis=0)
        rows_ref[sample * tok_pair : (sample + 1) * tok_pair] = jnp.concatenate([rows, rows], axis=1)
        sums.append(jnp.sum(rows.astype(jnp.float32), axis=0, keepdims=True))
    lat_sum = jnp.concatenate(sums, axis=0) * (1.0 / (2 * n_tp))
    lat_high = lat_sum.astype(jnp.bfloat16)
    lat_low = (lat_sum - lat_high.astype(jnp.float32)).astype(jnp.bfloat16)
    lat_rows = rows_ref[...]

    embed_copy.wait()
    embed = embed_ref[...]
    total = jnp.dot(
        jnp.concatenate([lat_high, lat_low], axis=0), embed, preferred_element_type=jnp.float32
    )
    parts = []
    for step in range(steps):
        up_copy(step).wait()
        joint = jnp.dot(embed, up_ref[step], preferred_element_type=jnp.float32)
        high = joint.astype(jnp.bfloat16)
        low = (joint - high.astype(jnp.float32)).astype(jnp.bfloat16)
        joint = jnp.concatenate([high, low], axis=0)
        span = slice(step * part, (step + 1) * part)
        joint_ref[:, span] = joint
        hidden = jnp.dot(lat_rows, joint, preferred_element_type=jnp.float32)
        cdf = 0.5 * (1.0 + lax.erf(hidden * 0.7071067811865476))
        pdf = jnp.exp(-0.5 * hidden * hidden) * 0.3989422804014327
        slope_ref[:, span] = cdf + hidden * pdf
        act_sum = jnp.sum((hidden * cdf).reshape(samples, tok_pair, part), axis=1)
        high = act_sum.astype(jnp.bfloat16)
        low = (act_sum - high.astype(jnp.float32)).astype(jnp.bfloat16)
        parts.append(jnp.concatenate([high, low], axis=0))
    for step in range(steps):
        down_copy(step).wait()
        total = total + jnp.dot(
            parts[step],
            down_ref[step * part : (step + 1) * part],
            preferred_element_type=jnp.float32,
        )
    pool = (total[:samples] + total[samples:]) * (1.0 / seq_len)
    side = lax.broadcasted_iota(jnp.int32, (samples, LANES), 1) < LANES // 2
    for plane in range(n_seq // 2):
        for column in range(n_tp):
            first = (plane * 2 * n_tp + column) // 2
            second = (plane * 2 * n_tp + n_tp + column) // 2
            first = pool[:, first * LANES : (first + 1) * LANES]
            second = pool[:, second * LANES : (second + 1) * LANES]
            if column % 2 == 0:
                block = jnp.where(side, first, pltpu.roll(second, LANES // 2, 1))
            else:
                block = jnp.where(side, pltpu.roll(first, LANES // 2, 1), second)
            high = block.astype(jnp.bfloat16)
            low = (block - high.astype(jnp.float32)).astype(jnp.bfloat16)
            for core in range(2):
                target = (plane * 2 + core) * n_tp + column
                pay_ref[target, 0] = high
                pay_ref[target, 1] = low


def forward(qkv, positions, own, other, embed_w, up_w, down_w, n_seq, n_tp):
    samples, tok_dev, width = qkv.shape[1:]
    count = n_seq * n_tp
    groups = 2 + 3 * (width // HEAD_DIM // (count // samples))
    tok_seq, lat = own.shape[1:]
    units, features = (up_w.shape[1] // 2, up_w.shape[0])
    steps = units // 256
    rows = 2 * tok_seq * samples
    any_spec = pl.BlockSpec(memory_space=pl.ANY)
    hbm_spec = pl.BlockSpec(memory_space=pltpu.HBM)
    vmem_spec = pl.BlockSpec(memory_space=pltpu.VMEM)
    return pl.pallas_call(
        functools.partial(forward_kernel, (n_seq, n_tp, steps, tok_dev * count)),
        out_shape=(
            jax.ShapeDtypeStruct((count, groups, tok_dev, LANES), jnp.bfloat16),
            jax.ShapeDtypeStruct((rows, units), jnp.float32),
            jax.ShapeDtypeStruct((2 * lat, units), jnp.bfloat16),
        ),
        in_specs=[
            pl.BlockSpec(memory_space=pltpu.SMEM),
            vmem_spec,
            hbm_spec,
            any_spec,
            any_spec,
            hbm_spec,
            hbm_spec,
            hbm_spec,
        ],
        out_specs=(vmem_spec,) * 3,
        scratch_shapes=[
            pltpu.VMEM(qkv.shape, jnp.bfloat16),
            pltpu.VMEM((2,) + own.shape, jnp.bfloat16),
            pltpu.VMEM(embed_w.shape, jnp.bfloat16),
            pltpu.VMEM((steps, features, 256), jnp.bfloat16),
            pltpu.VMEM((units, features), jnp.bfloat16),
            pltpu.VMEM((rows, 2 * lat), jnp.bfloat16),
            pltpu.SemaphoreType.DMA((4 + 2 * steps,)),
        ],
        compiler_params=pltpu.CompilerParams(vmem_limit_bytes=52 << 20),
        cost_estimate=pl.CostEstimate(
            flops=4 * features * units * 64, bytes_accessed=4 * features * units, transcendentals=0
        ),
        name="forward",
    )(positions, jnp.asarray(lane_frequencies()), qkv, own, other, embed_w, up_w, down_w)


def backward_kernel(
    steps, second_ref, slope_ref, joint_ref, down_hbm, out_ref, dpool_ref, down_ref, sems
):
    count, groups, samples, _ = second_ref.shape
    units = down_ref.shape[0]
    part = units // steps
    half = lax.axis_index("seq") % 2

    def down_copy(step):
        start = pl.multiple_of(half * units + step * part, LANES)
        return pltpu.make_async_copy(
            down_hbm.at[pl.ds(start, part)],
            down_ref.at[pl.ds(step * part, part)],
            sems.at[step],
        )

    for step in range(steps):
        down_copy(step).start()
    rows = slope_ref.shape[0] // samples
    side = lax.broadcasted_iota(jnp.int32, (samples, LANES), 1) < LANES // 2
    for pair in range(count // 2):
        first = second_ref[2 * pair, groups - 1].astype(jnp.float32)
        second = second_ref[2 * pair + 1, groups - 1].astype(jnp.float32)
        first = first + pltpu.roll(first, LANES // 2, 1)
        second = second + pltpu.roll(second, LANES // 2, 1)
        block = jnp.where(side, first, second)
        high = block.astype(jnp.bfloat16)
        low = (block - high.astype(jnp.float32)).astype(jnp.bfloat16)
        dpool_ref[:, pair * LANES : (pair + 1) * LANES] = jnp.concatenate([high, low], axis=0)
    dpool = dpool_ref[...]
    pieces = []
    for step in range(steps):
        down_copy(step).wait()
        pieces.append(
            lax.dot_general(
                dpool,
                down_ref[step * part : (step + 1) * part],
                (((1,), (1,)), ((), ())),
                preferred_element_type=jnp.float32,
            )
        )
    dact = jnp.concatenate(pieces, axis=1)
    dact = dact[:samples] + dact[samples:]
    halves = []
    for sample in range(samples):
        dh1 = slope_ref[sample * rows : (sample + 1) * rows] * dact[sample : sample + 1]
        halves.append(dh1.astype(jnp.bfloat16))
    dx = lax.dot_general(
        jnp.concatenate(halves, axis=0),
        joint_ref[...],
        (((1,), (1,)), ((), ())),
        preferred_element_type=jnp.float32,
    )
    dx = dx + pltpu.roll(dx, LANES // 2, 1)
    side = lax.broadcasted_iota(jnp.int32, (rows, LANES), 1) < LANES // 2
    tok_dev = out_ref.shape[2]
    for pair in range(samples // 2):
        first = dx[2 * pair * rows : (2 * pair + 1) * rows]
        second = dx[(2 * pair + 1) * rows : (2 * pair + 2) * rows]
        both = jnp.where(side, first, second)
        for target in range(rows // tok_dev):
            out_ref[target, pair] = both[target * tok_dev : (target + 1) * tok_dev].astype(jnp.bfloat16)


def backward(second, slope, joint, down, tok_dev):
    samples = second.shape[2]
    targets = slope.shape[0] // samples // tok_dev
    units, steps = (slope.shape[1], slope.shape[1] // 256)
    vmem_spec = pl.BlockSpec(memory_space=pltpu.VMEM)
    return pl.pallas_call(
        functools.partial(backward_kernel, steps),
        out_shape=(
            jax.ShapeDtypeStruct((targets, samples // 2, tok_dev, LANES), jnp.bfloat16),
            jax.ShapeDtypeStruct((2 * samples, down.shape[1]), jnp.bfloat16),
        ),
        in_specs=[vmem_spec] * 3 + [pl.BlockSpec(memory_space=pltpu.HBM)],
        out_specs=(vmem_spec,) * 2,
        scratch_shapes=[
            pltpu.VMEM((units, down.shape[1]), jnp.bfloat16),
            pltpu.SemaphoreType.DMA((steps,)),
        ],
        compiler_params=pltpu.CompilerParams(vmem_limit_bytes=52 << 20),
        name="backward",
    )(second, slope, joint, down)


def per_device_fast(qkv, positions, w_proj, latents, embed_w, up_w, down_w, head_w, labels, timesteps):
    both = ("seq", "tp")
    n_seq, n_tp = (lax.axis_size("seq"), lax.axis_size("tp"))
    count = n_seq * n_tp
    seq_index = lax.axis_index("seq")
    half = seq_index % 2
    samples, tok_dev, width = qkv.shape[1:]
    seq_len = tok_dev * count
    lat = latents.shape[2]
    heads = width // HEAD_DIM
    per_sample = count // samples
    heads_dev = heads // per_sample
    rows_dev, classes = head_w.shape
    partner = [(i, i ^ n_tp) for i in range(count)]

    def in_order(own):
        other = lax.ppermute(own, both, partner)
        mine = jnp.broadcast_to(half == 0, own.shape)
        return jnp.stack([jnp.where(mine, own, other), jnp.where(mine, other, own)])

    other = lax.ppermute(latents, both, partner)
    head_pair = in_order(head_w).reshape(2 * rows_dev, classes)

    payload, slope, joint = forward(
        qkv, positions, latents, other, embed_w, up_w, down_w, n_seq, n_tp
    )
    moved = lax.all_to_all(payload, both, 0, 0, tiled=True)

    pooled = jnp.sum(moved[:, :2].astype(jnp.float32), axis=(0, 1))
    padded = -(-classes // 256) * 256
    terms = jnp.pad(split_dot(pooled, head_pair), ((0, 0), (0, padded - classes)))
    terms = lax.dynamic_slice_in_dim(terms, half * (padded // 2), padded // 2, 1)
    terms = lax.all_to_all(
        jnp.broadcast_to(terms[None], (count,) + terms.shape), both, 0, 0, tiled=True
    )

    views = moved[:, 2:].reshape(count, 3, heads_dev, tok_dev, HEAD_DIM)
    views = views.transpose(1, 2, 0, 3, 4).reshape(3, heads_dev, seq_len, HEAD_DIM)
    scores = jnp.einsum(
        "hqd,hkd->hqk", views[0], views[1], preferred_element_type=jnp.float32
    ) * HEAD_DIM ** (-0.5)
    weights = jnp.exp(scores - jnp.max(scores, axis=-1, keepdims=True))
    total = jnp.sum(weights, axis=-1)
    mixed = jnp.einsum(
        "hqk,hkd->hqd", weights.astype(jnp.bfloat16), views[2], preferred_element_type=jnp.float32
    )
    attended = (mixed / total[..., None]).astype(jnp.bfloat16)
    attended = attended.reshape(heads_dev, count, tok_dev, HEAD_DIM).transpose(1, 0, 2, 3)

    logits = jnp.sum(terms.reshape(n_seq // 2, 2, n_tp, samples, padded // 2), axis=(0, 2))
    logits = logits.transpose(1, 0, 2).reshape(samples, padded)[:, :classes]
    probs = jax.nn.softmax(logits, axis=-1)
    onehot = (labels[:, None] == jnp.arange(classes, dtype=jnp.int32)[None, :]).astype(jnp.float32)
    share = split_two(split_dot(onehot - probs, head_w, 1), 1)
    share = jnp.broadcast_to(share[None, None], (count, 1) + share.shape)
    second = lax.all_to_all(
        jnp.concatenate([attended, share], axis=1), both, 0, 0, tiled=True
    )
    returned = second[:, :heads_dev].reshape(samples, per_sample, heads_dev, tok_dev, HEAD_DIM)
    returned = returned.transpose(0, 3, 1, 2, 4).reshape(samples, tok_dev, width)
    eps = jnp.dot(returned, w_proj, preferred_element_type=jnp.float32)
    dx_terms, dpool = backward(second, slope, joint, down_w, tok_dev)
    planes = [[first + k for k in range(2 * n_tp)] for first in range(0, count, 2 * n_tp)]
    dx_terms = lax.all_to_all(dx_terms, both, 0, 0, tiled=True, axis_index_groups=planes)
    dx = jnp.sum(dx_terms.astype(jnp.float32), axis=0)
    dx = dx.reshape(samples // 2, tok_dev, 2, lat).transpose(0, 2, 1, 3)
    dx = dx.reshape(samples, tok_dev, lat)
    dx_pool = lax.dot_general(
        dpool, embed_w, (((1,), (1,)), ((), ())), preferred_element_type=jnp.float32
    )
    dx = dx + (dx_pool[:samples] + dx_pool[samples:])[:, None, :]
    phase = (timesteps.astype(jnp.float32) / 1000.0 + 0.008) / 1.008 * (jnp.pi / 2)
    abar = jnp.cos(phase) ** 2
    scale = GUIDANCE * jnp.sqrt(1.0 - abar)
    return (eps - scale[:, None, None] * dx).astype(jnp.bfloat16)


def per_device(qkv, positions, w_proj, latents, embed_w, up_w, down_w, head_w, labels, timesteps):
    args = (qkv, positions, w_proj, latents, embed_w, up_w, down_w, head_w, labels, timesteps)
    n_seq = lax.axis_size("seq")
    count = n_seq * lax.axis_size("tp")
    samples, heads = (qkv.shape[1], qkv.shape[3] // HEAD_DIM)
    tok_dev, tok_seq, lat = (qkv.shape[2], latents.shape[1], latents.shape[2])
    even = count % samples == 0 and heads % max(1, count // samples) == 0
    even = even and n_seq % 2 == 0 and count // n_seq % 2 == 0 and samples == 4 and tok_dev == 4
    even = even and lat == 64 and head_w.shape[0] == 64 and tok_seq % 16 == 0
    even = even and up_w.shape[1] % 512 == 0 and tok_seq == tok_dev * (count // n_seq)
    if even and count * head_w.shape[0] == up_w.shape[0]:
        return per_device_fast(*args)
    return per_device_general(*args)


def solution(mesh):
    placed = (
        P(None, None, ("seq", "tp"), None),
        P(None, None, ("seq", "tp")),
        P(),
        P(None, "seq", None),
        P(),
        P(None, "tp"),
        P("tp", None),
        P(("seq", "tp"), None),
        P(),
        P(),
    )
    return jax.shard_map(
        per_device,
        mesh=mesh,
        in_specs=placed,
        out_specs=P(None, ("seq", "tp"), None),
        check_vma=False,
    )
```

```python
import functools

import jax
import jax.numpy as jnp
import numpy as np
from jax import lax
from jax.experimental import pallas as pl
from jax.experimental.pallas import tpu as pltpu
from jax.sharding import PartitionSpec as P

HEAD_DIM = 128


GUIDANCE = 0.1


def rope_angles(positions, head_dim):
    frame_width = head_dim // 8
    plane_width = (head_dim - frame_width) // 2
    pieces = []
    for axis, width in zip(range(3), (frame_width, plane_width, plane_width)):
        freqs = 10000.0 ** (-jnp.arange(0, width, 2, dtype=jnp.float32) / width)
        pieces.append(positions[axis][..., None] * freqs)
    return jnp.concatenate(pieces, axis=-1)


def rotate(values, angles):
    half = values.shape[-1] // 2
    floats = values.astype(jnp.float32)
    first = floats[..., :half]
    second = floats[..., half:]
    cosine = jnp.cos(angles)[:, :, None, :]
    sine = jnp.sin(angles)[:, :, None, :]
    turned = jnp.concatenate(
        [first * cosine - second * sine, first * sine + second * cosine], axis=-1
    )
    return turned.astype(jnp.bfloat16)


def gelu_slope(values):
    cdf = 0.5 * (1.0 + jax.scipy.special.erf(values * 0.7071067811865476))
    pdf = jnp.exp(-0.5 * values * values) * 0.3989422804014327
    return cdf + values * pdf


def pairs_first(array):
    samples, tokens = (array.shape[0], array.shape[1])
    return array.transpose(0, 2, 1, 3).reshape(samples * array.shape[2], tokens, HEAD_DIM)


def per_device_general(qkv, positions, w_proj, latents, embed_w, up_w, down_w, head_w, labels, timesteps):
    samples, tok_dev = (qkv.shape[1], qkv.shape[2])
    angles = rope_angles(positions.astype(jnp.float32), HEAD_DIM)
    heads = qkv.shape[3] // HEAD_DIM
    shaped = (samples, tok_dev, heads, HEAD_DIM)
    queries = rotate(qkv[0].reshape(shaped), angles)
    keys_tok = rotate(qkv[1].reshape(shaped), angles)
    values_tok = qkv[2].reshape(shaped)
    moved = lax.all_to_all(
        jnp.stack([pairs_first(queries), pairs_first(keys_tok), pairs_first(values_tok)]),
        "seq",
        split_axis=1,
        concat_axis=2,
        tiled=True,
    )
    query_pairs = moved[0]
    pair_count, query_count = (query_pairs.shape[0], query_pairs.shape[1])
    running = jnp.full((pair_count, query_count), -jnp.inf, jnp.float32)
    total = jnp.zeros((pair_count, query_count), jnp.float32)
    accum = jnp.zeros((pair_count, query_count, HEAD_DIM), jnp.float32)
    key_piece = lax.all_gather(moved[1], "tp", axis=1, tiled=True)
    value_piece = lax.all_gather(moved[2], "tp", axis=1, tiled=True)
    scores = jnp.einsum(
        "iqd,ikd->iqk", query_pairs, key_piece, preferred_element_type=jnp.float32
    ) * HEAD_DIM ** (-0.5)
    newest = jnp.max(scores, axis=-1)
    factor = jnp.exp(running - newest)
    weights = jnp.exp(scores - newest[..., None])
    total = total * factor + jnp.sum(weights, axis=-1)
    accum = accum * factor[..., None] + jnp.einsum(
        "iqk,ikd->iqd",
        weights.astype(jnp.bfloat16),
        value_piece,
        preferred_element_type=jnp.float32,
    )
    running, total, accum = (newest, total, accum)
    attended = (accum / total[..., None]).astype(jnp.bfloat16)
    returned = lax.all_to_all(attended, "seq", split_axis=1, concat_axis=0, tiled=True)
    returned = returned.reshape(samples, heads, tok_dev, HEAD_DIM).transpose(0, 2, 1, 3)
    returned = returned.reshape(samples, tok_dev, qkv.shape[3])
    eps = jnp.dot(returned, w_proj, preferred_element_type=jnp.float32)
    seq_len = latents.shape[1] * lax.axis_size("seq")
    tp_index = lax.axis_index("tp")
    emb = jnp.dot(latents, embed_w, preferred_element_type=jnp.float32).astype(jnp.bfloat16)
    hidden = jnp.dot(emb, up_w, preferred_element_type=jnp.float32)
    act = jax.nn.gelu(hidden, approximate=False).astype(jnp.bfloat16)
    branch = jnp.dot(act, down_w, preferred_element_type=jnp.float32)
    own_emb = lax.dynamic_slice_in_dim(emb, tp_index * tok_dev, tok_dev, 1).astype(jnp.float32)
    partial_pool = jnp.sum(branch, axis=1) + jnp.sum(own_emb, axis=1)
    head_rows = head_w.shape[0]
    flat_index = lax.axis_index("seq") * lax.axis_size("tp") + tp_index
    pooled = lax.psum(partial_pool, ("seq", "tp")) / seq_len
    pooled_share = lax.dynamic_slice_in_dim(pooled, flat_index * head_rows, head_rows, 1)
    head_float = head_w.astype(jnp.float32)
    logit_terms = jnp.dot(pooled_share, head_float, precision=lax.Precision.HIGHEST)
    logits = lax.psum(logit_terms, ("seq", "tp"))
    probs = jax.nn.softmax(logits, axis=-1)
    onehot = (labels[:, None] == jnp.arange(logits.shape[1], dtype=jnp.int32)[None, :]).astype(
        jnp.float32
    )
    grad_share = jnp.dot(onehot - probs, head_float.T, precision=lax.Precision.HIGHEST)
    dpool = lax.all_gather(grad_share, ("seq", "tp"), axis=1, tiled=True)
    dact = jnp.dot(dpool, down_w.astype(jnp.float32).T, precision=lax.Precision.HIGHEST)
    dh1 = (gelu_slope(hidden) * dact[:, None, :]).astype(jnp.bfloat16)
    demb = jnp.einsum("btf,cf->btc", dh1, up_w, preferred_element_type=jnp.float32)
    embed_float = embed_w.astype(jnp.float32)
    dx_terms = jnp.einsum("btc,lc->btl", demb, embed_float, precision=lax.Precision.HIGHEST)
    dx_mine = lax.psum_scatter(
        dx_terms.astype(jnp.bfloat16), "tp", scatter_dimension=1, tiled=True
    ).astype(jnp.float32)
    dx_pool = jnp.dot(dpool, embed_float.T, precision=lax.Precision.HIGHEST)
    dx_total = dx_mine + dx_pool[:, None, :]
    phase = (timesteps.astype(jnp.float32) / 1000.0 + 0.008) / 1.008 * (jnp.pi / 2)
    abar = jnp.cos(phase) ** 2
    scale = GUIDANCE * jnp.sqrt(1.0 - abar)
    return (eps - scale[:, None, None] * dx_total).astype(jnp.bfloat16)


def split_rows(values):
    high = values.astype(jnp.bfloat16)
    rest = values - high.astype(jnp.float32)
    middle = rest.astype(jnp.bfloat16)
    low = (rest - middle.astype(jnp.float32)).astype(jnp.bfloat16)
    return jnp.concatenate([high, middle, low], axis=0)


def split_dot(values, weights, contract=0):
    rows = values.shape[0]
    product = lax.dot_general(
        split_rows(values),
        weights,
        (((1,), (contract,)), ((), ())),
        preferred_element_type=jnp.float32,
    )
    return product[:rows] + product[rows : 2 * rows] + product[2 * rows :]


def split_two(values, axis):
    high = values.astype(jnp.bfloat16)
    low = (values - high.astype(jnp.float32)).astype(jnp.bfloat16)
    return jnp.concatenate([high, low], axis=axis)


LANES = 128


KEPT = 1


def in_hbm(*arrays):
    return [pltpu.with_memory_space_constraint(array, pltpu.HBM) for array in arrays]


def lane_frequencies():
    frame_width = HEAD_DIM // 8
    plane_width = (HEAD_DIM - frame_width) // 2
    freqs, axes = [], []
    for axis, width in zip(range(3), (frame_width, plane_width, plane_width)):
        steps = np.arange(0, width, 2, dtype=np.float32) / np.float32(width)
        freqs.append(np.float32(10000.0) ** (-steps))
        axes.append(np.full(width // 2, axis, np.float32))
    freqs, axes = (np.concatenate(freqs), np.concatenate(axes))
    table = np.stack([np.tile(freqs, 2), np.tile(axes, 2)]).astype(np.float32)
    return np.pad(table, ((0, 6), (0, 0)))


def forward_kernel(
    sizes,
    pos_hbm,
    table_hbm,
    qkv_hbm,
    own_hbm,
    other_hbm,
    embed_hbm,
    up_hbm,
    down_hbm,
    pay_ref,
    slope_ref,
    joint_ref,
    keep_ref,
    pos_ref,
    table_ref,
    qkv_ref,
    lat_ref,
    embed_ref,
    up_ref,
    down_ref,
    rows_ref,
    sems,
):
    n_seq, n_tp, steps, seq_len = sizes
    samples, tok_dev, width = qkv_ref.shape[1:]
    count = n_seq * n_tp
    per_sample = count // samples
    heads_dev = width // HEAD_DIM // per_sample
    tok_seq, lat = own_hbm.shape[1:]
    units = slope_ref.shape[1]
    part = units // steps
    kept = keep_ref.shape[0] // part
    half = lax.axis_index("seq") % 2

    def up_copy(step):
        start = pl.multiple_of(half * units + step * part, LANES)
        return pltpu.make_async_copy(
            up_hbm.at[:, pl.ds(start, part)], up_ref.at[step], sems.at[6 + step]
        )

    def down_at(step):
        if step < kept:
            return keep_ref.at[pl.ds(step * part, part)]
        return down_ref.at[pl.ds((step - kept) * part, part)]

    def down_copy(step):
        start = pl.multiple_of(half * units + step * part, LANES)
        return pltpu.make_async_copy(
            down_hbm.at[pl.ds(start, part)],
            down_at(step),
            sems.at[6 + steps + step],
        )

    own_copy = pltpu.make_async_copy(own_hbm, lat_ref.at[half], sems.at[0])
    other_copy = pltpu.make_async_copy(other_hbm, lat_ref.at[1 - half], sems.at[1])
    embed_copy = pltpu.make_async_copy(embed_hbm, embed_ref, sems.at[2])
    qkv_copy = pltpu.make_async_copy(qkv_hbm, qkv_ref, sems.at[3])
    pos_copy = pltpu.make_async_copy(pos_hbm, pos_ref, sems.at[4])
    table_copy = pltpu.make_async_copy(table_hbm, table_ref, sems.at[5])
    for copy in (pos_copy, table_copy, own_copy, other_copy, qkv_copy, embed_copy):
        copy.start()
    for step in range(steps):
        up_copy(step).start()
    for step in range(steps):
        down_copy(step).start()

    pos_copy.wait()
    table_copy.wait()

    shape = (samples * tok_dev, LANES)
    row = lax.broadcasted_iota(jnp.int32, shape, 0)
    lane = lax.broadcasted_iota(jnp.int32, shape, 1)
    axis = jnp.broadcast_to(table_ref[1:2, :], shape)
    angles = jnp.zeros(shape, jnp.float32)
    for index in range(samples * tok_dev):
        sample, token = divmod(index, tok_dev)
        frame, line, column = (pos_ref[k, sample, token].astype(jnp.float32) for k in range(3))
        value = jnp.where(axis < 0.5, frame, jnp.where(axis < 1.5, line, column))
        angles = jnp.where(row == index, value, angles)
    angles = angles * jnp.broadcast_to(table_ref[0:1, :], shape)
    cosine = jnp.cos(angles)
    sine = jnp.sin(angles)
    sine = jnp.where(lane < HEAD_DIM // 2, -sine, sine)

    qkv_copy.wait()
    for sample in range(samples):
        cos_rows = cosine[sample * tok_dev : (sample + 1) * tok_dev]
        sin_rows = sine[sample * tok_dev : (sample + 1) * tok_dev]
        for head in range(width // HEAD_DIM):
            target = sample * per_sample + head // heads_dev
            span = slice(head * HEAD_DIM, (head + 1) * HEAD_DIM)
            for kind in range(3):
                group = 2 + kind * heads_dev + head % heads_dev
                values = qkv_ref[kind, sample, :, span]
                if kind < 2:
                    values = values.astype(jnp.float32)
                    values = values * cos_rows + pltpu.roll(values, HEAD_DIM // 2, 1) * sin_rows
                pay_ref[target, group] = values.astype(jnp.bfloat16)

    own_copy.wait()
    other_copy.wait()
    tok_pair = 2 * tok_seq
    sums = []
    for sample in range(samples):
        pieces = [lat_ref[0, sample], lat_ref[1, sample]]
        rows = jnp.concatenate(pieces, axis=0)
        rows_ref[sample * tok_pair : (sample + 1) * tok_pair] = jnp.concatenate([rows, rows], axis=1)
        sums.append(jnp.sum(rows.astype(jnp.float32), axis=0, keepdims=True))
    lat_sum = jnp.concatenate(sums, axis=0) * (1.0 / (2 * n_tp))
    lat_high = lat_sum.astype(jnp.bfloat16)
    lat_low = (lat_sum - lat_high.astype(jnp.float32)).astype(jnp.bfloat16)
    lat_rows = rows_ref[...]

    embed_copy.wait()
    embed = embed_ref[...]
    total = jnp.dot(
        jnp.concatenate([lat_high, lat_low], axis=0), embed, preferred_element_type=jnp.float32
    )
    parts = []
    for step in range(steps):
        up_copy(step).wait()
        joint = jnp.dot(embed, up_ref[step], preferred_element_type=jnp.float32)
        high = joint.astype(jnp.bfloat16)
        low = (joint - high.astype(jnp.float32)).astype(jnp.bfloat16)
        joint = jnp.concatenate([high, low], axis=0)
        span = slice(step * part, (step + 1) * part)
        joint_ref[:, span] = joint
        hidden = jnp.dot(lat_rows, joint, preferred_element_type=jnp.float32)
        cdf = 0.5 * (1.0 + lax.erf(hidden * 0.7071067811865476))
        pdf = jnp.exp(-0.5 * hidden * hidden) * 0.3989422804014327
        slope_ref[:, span] = cdf + hidden * pdf
        act_sum = jnp.sum((hidden * cdf).reshape(samples, tok_pair, part), axis=1)
        high = act_sum.astype(jnp.bfloat16)
        low = (act_sum - high.astype(jnp.float32)).astype(jnp.bfloat16)
        parts.append(jnp.concatenate([high, low], axis=0))
    for step in range(steps):
        down_copy(step).wait()
        total = total + jnp.dot(
            parts[step],
            down_at(step)[...],
            preferred_element_type=jnp.float32,
        )
    pool = (total[:samples] + total[samples:]) * (1.0 / seq_len)
    side = lax.broadcasted_iota(jnp.int32, (samples, LANES), 1) < LANES // 2
    for plane in range(n_seq // 2):
        for column in range(n_tp):
            first = (plane * 2 * n_tp + column) // 2
            second = (plane * 2 * n_tp + n_tp + column) // 2
            first = pool[:, first * LANES : (first + 1) * LANES]
            second = pool[:, second * LANES : (second + 1) * LANES]
            if column % 2 == 0:
                block = jnp.where(side, first, pltpu.roll(second, LANES // 2, 1))
            else:
                block = jnp.where(side, pltpu.roll(first, LANES // 2, 1), second)
            high = block.astype(jnp.bfloat16)
            low = (block - high.astype(jnp.float32)).astype(jnp.bfloat16)
            for core in range(2):
                target = (plane * 2 + core) * n_tp + column
                pay_ref[target, 0] = high
                pay_ref[target, 1] = low


def forward(qkv, positions, own, other, embed_w, up_w, down_w, n_seq, n_tp):
    samples, tok_dev, width = qkv.shape[1:]
    count = n_seq * n_tp
    groups = 2 + 3 * (width // HEAD_DIM // (count // samples))
    tok_seq, lat = own.shape[1:]
    units, features = (up_w.shape[1] // 2, up_w.shape[0])
    steps = units // 256
    rows = 2 * tok_seq * samples
    any_spec = pl.BlockSpec(memory_space=pl.ANY)
    vmem_spec = pl.BlockSpec(memory_space=pltpu.VMEM)
    return pl.pallas_call(
        functools.partial(forward_kernel, (n_seq, n_tp, steps, tok_dev * count)),
        out_shape=(
            jax.ShapeDtypeStruct((count, groups, tok_dev, LANES), jnp.bfloat16),
            jax.ShapeDtypeStruct((rows, units), jnp.float32),
            jax.ShapeDtypeStruct((2 * lat, units), jnp.bfloat16),
            jax.ShapeDtypeStruct((KEPT * 256, features), jnp.bfloat16),
        ),
        in_specs=[any_spec] * 8,
        out_specs=(vmem_spec,) * 4,
        scratch_shapes=[
            pltpu.SMEM(positions.shape, jnp.int32),
            pltpu.VMEM((8, LANES), jnp.float32),
            pltpu.VMEM(qkv.shape, jnp.bfloat16),
            pltpu.VMEM((2,) + own.shape, jnp.bfloat16),
            pltpu.VMEM(embed_w.shape, jnp.bfloat16),
            pltpu.VMEM((steps, features, 256), jnp.bfloat16),
            pltpu.VMEM((units - KEPT * 256, features), jnp.bfloat16),
            pltpu.VMEM((rows, 2 * lat), jnp.bfloat16),
            pltpu.SemaphoreType.DMA((6 + 2 * steps,)),
        ],
        compiler_params=pltpu.CompilerParams(vmem_limit_bytes=32 << 20),
        cost_estimate=pl.CostEstimate(
            flops=4 * features * units * 64, bytes_accessed=4 * features * units, transcendentals=0
        ),
        name="forward",
    )(*in_hbm(positions, jnp.asarray(lane_frequencies()), qkv, own), other, *in_hbm(embed_w, up_w, down_w))


def backward_kernel(
    steps, second_ref, slope_ref, joint_ref, keep_ref, down_hbm, out_ref, dpool_ref, down_ref, sems
):
    count, groups, samples, _ = second_ref.shape
    units = slope_ref.shape[1]
    part = units // steps
    kept = keep_ref.shape[0] // part
    half = lax.axis_index("seq") % 2

    def down_copy(step):
        start = pl.multiple_of(half * units + step * part, LANES)
        return pltpu.make_async_copy(
            down_hbm.at[pl.ds(start, part)],
            down_ref.at[pl.ds((step - kept) * part, part)],
            sems.at[step - kept],
        )

    for step in range(kept, steps):
        down_copy(step).start()
    rows = slope_ref.shape[0] // samples
    side = lax.broadcasted_iota(jnp.int32, (samples, LANES), 1) < LANES // 2
    for pair in range(count // 2):
        first = second_ref[2 * pair, groups - 1].astype(jnp.float32)
        second = second_ref[2 * pair + 1, groups - 1].astype(jnp.float32)
        first = first + pltpu.roll(first, LANES // 2, 1)
        second = second + pltpu.roll(second, LANES // 2, 1)
        block = jnp.where(side, first, second)
        high = block.astype(jnp.bfloat16)
        low = (block - high.astype(jnp.float32)).astype(jnp.bfloat16)
        dpool_ref[:, pair * LANES : (pair + 1) * LANES] = jnp.concatenate([high, low], axis=0)
    dpool = dpool_ref[...]
    across = (((1,), (1,)), ((), ()))
    dx = None
    for step in range(steps):
        if step < kept:
            weights = keep_ref[step * part : (step + 1) * part]
        else:
            down_copy(step).wait()
            weights = down_ref[(step - kept) * part : (step - kept + 1) * part]
        dact = lax.dot_general(dpool, weights, across, preferred_element_type=jnp.float32)
        dact = dact[:samples] + dact[samples:]
        span = slice(step * part, (step + 1) * part)
        slope = slope_ref[:, span].reshape(samples, rows, part)
        dh1 = (slope * dact[:, None, :]).reshape(samples * rows, part).astype(jnp.bfloat16)
        term = lax.dot_general(dh1, joint_ref[:, span], across, preferred_element_type=jnp.float32)
        dx = term if dx is None else dx + term
    dx = dx + pltpu.roll(dx, LANES // 2, 1)
    side = lax.broadcasted_iota(jnp.int32, (rows, LANES), 1) < LANES // 2
    tok_dev = out_ref.shape[2]
    for pair in range(samples // 2):
        first = dx[2 * pair * rows : (2 * pair + 1) * rows]
        second = dx[(2 * pair + 1) * rows : (2 * pair + 2) * rows]
        both = jnp.where(side, first, second)
        for target in range(rows // tok_dev):
            out_ref[target, pair] = both[target * tok_dev : (target + 1) * tok_dev].astype(jnp.bfloat16)


def backward(second, slope, joint, keep, down, tok_dev):
    samples = second.shape[2]
    targets = slope.shape[0] // samples // tok_dev
    units, steps = (slope.shape[1], slope.shape[1] // 256)
    vmem_spec = pl.BlockSpec(memory_space=pltpu.VMEM)
    return pl.pallas_call(
        functools.partial(backward_kernel, steps),
        out_shape=(
            jax.ShapeDtypeStruct((targets, samples // 2, tok_dev, LANES), jnp.bfloat16),
            jax.ShapeDtypeStruct((2 * samples, down.shape[1]), jnp.bfloat16),
        ),
        in_specs=[vmem_spec] * 4 + [pl.BlockSpec(memory_space=pl.ANY)],
        out_specs=(vmem_spec,) * 2,
        scratch_shapes=[
            pltpu.VMEM((units - keep.shape[0], down.shape[1]), jnp.bfloat16),
            pltpu.SemaphoreType.DMA((steps - KEPT,)),
        ],
        compiler_params=pltpu.CompilerParams(vmem_limit_bytes=32 << 20),
        name="backward",
    )(second, slope, joint, keep, *in_hbm(down))


def per_device_fast(qkv, positions, w_proj, latents, embed_w, up_w, down_w, head_w, labels, timesteps):
    both = ("seq", "tp")
    n_seq, n_tp = (lax.axis_size("seq"), lax.axis_size("tp"))
    count = n_seq * n_tp
    seq_index = lax.axis_index("seq")
    half = seq_index % 2
    samples, tok_dev, width = qkv.shape[1:]
    seq_len = tok_dev * count
    lat = latents.shape[2]
    heads = width // HEAD_DIM
    per_sample = count // samples
    heads_dev = heads // per_sample
    rows_dev, classes = head_w.shape
    partner = [(i, i ^ n_tp) for i in range(count)]

    def in_order(own):
        other = lax.ppermute(own, both, partner)
        mine = jnp.broadcast_to(half == 0, own.shape)
        return jnp.stack([jnp.where(mine, own, other), jnp.where(mine, other, own)])

    other = lax.ppermute(latents, both, partner)
    head_pair = in_order(head_w).reshape(2 * rows_dev, classes)

    payload, slope, joint, keep = forward(
        qkv, positions, latents, other, embed_w, up_w, down_w, n_seq, n_tp
    )
    moved = lax.all_to_all(payload, both, 0, 0, tiled=True)

    pooled = jnp.sum(moved[:, :2].astype(jnp.float32), axis=(0, 1))
    padded = -(-classes // 256) * 256
    terms = jnp.pad(split_dot(pooled, head_pair), ((0, 0), (0, padded - classes)))
    terms = lax.dynamic_slice_in_dim(terms, half * (padded // 2), padded // 2, 1)
    terms = lax.all_to_all(
        jnp.broadcast_to(terms.astype(jnp.bfloat16)[None], (count,) + terms.shape),
        both,
        0,
        0,
        tiled=True,
    )

    views = moved[:, 2:].reshape(count, 3, heads_dev, tok_dev, HEAD_DIM)
    views = views.transpose(1, 2, 0, 3, 4).reshape(3, heads_dev, seq_len, HEAD_DIM)
    scores = jnp.einsum(
        "hqd,hkd->hqk", views[0], views[1], preferred_element_type=jnp.float32
    ) * HEAD_DIM ** (-0.5)
    weights = jnp.exp(scores - jnp.max(scores, axis=-1, keepdims=True))
    total = jnp.sum(weights, axis=-1)
    mixed = jnp.einsum(
        "hqk,hkd->hqd", weights.astype(jnp.bfloat16), views[2], preferred_element_type=jnp.float32
    )
    attended = (mixed / total[..., None]).astype(jnp.bfloat16)
    attended = attended.reshape(heads_dev, count, tok_dev, HEAD_DIM).transpose(1, 0, 2, 3)

    terms = terms.astype(jnp.float32).reshape(n_seq // 2, 2, n_tp, samples, padded // 2)
    logits = jnp.sum(terms, axis=(0, 2))
    logits = logits.transpose(1, 0, 2).reshape(samples, padded)[:, :classes]
    probs = jax.nn.softmax(logits, axis=-1)
    onehot = (labels[:, None] == jnp.arange(classes, dtype=jnp.int32)[None, :]).astype(jnp.float32)
    share = split_two(split_dot(onehot - probs, head_w, 1), 1)
    share = jnp.broadcast_to(share[None, None], (count, 1) + share.shape)
    second = lax.all_to_all(
        jnp.concatenate([attended, share], axis=1), both, 0, 0, tiled=True
    )
    returned = second[:, :heads_dev].reshape(samples, per_sample, heads_dev, tok_dev, HEAD_DIM)
    returned = returned.transpose(0, 3, 1, 2, 4).reshape(samples, tok_dev, width)
    eps = jnp.dot(returned, w_proj, preferred_element_type=jnp.float32)
    eps = lax.optimization_barrier(eps)
    dx_terms, dpool = backward(second, slope, joint, keep, down_w, tok_dev)
    planes = [[first + k for k in range(2 * n_tp)] for first in range(0, count, 2 * n_tp)]
    dx_terms = lax.all_to_all(dx_terms, both, 0, 0, tiled=True, axis_index_groups=planes)
    dx = jnp.sum(dx_terms.astype(jnp.float32), axis=0)
    dx = dx.reshape(samples // 2, tok_dev, 2, lat).transpose(0, 2, 1, 3)
    dx = dx.reshape(samples, tok_dev, lat)
    dx_pool = lax.dot_general(
        dpool, embed_w, (((1,), (1,)), ((), ())), preferred_element_type=jnp.float32
    )
    dx = dx + (dx_pool[:samples] + dx_pool[samples:])[:, None, :]
    phase = (timesteps.astype(jnp.float32) / 1000.0 + 0.008) / 1.008 * (jnp.pi / 2)
    abar = jnp.cos(phase) ** 2
    scale = GUIDANCE * jnp.sqrt(1.0 - abar)
    return (eps - scale[:, None, None] * dx).astype(jnp.bfloat16)


def per_device(qkv, positions, w_proj, latents, embed_w, up_w, down_w, head_w, labels, timesteps):
    args = (qkv, positions, w_proj, latents, embed_w, up_w, down_w, head_w, labels, timesteps)
    n_seq = lax.axis_size("seq")
    count = n_seq * lax.axis_size("tp")
    samples, heads = (qkv.shape[1], qkv.shape[3] // HEAD_DIM)
    tok_dev, tok_seq, lat = (qkv.shape[2], latents.shape[1], latents.shape[2])
    even = count % samples == 0 and heads % max(1, count // samples) == 0
    even = even and n_seq % 2 == 0 and count // n_seq % 2 == 0 and samples == 4 and tok_dev == 4
    even = even and lat == 64 and head_w.shape[0] == 64 and tok_seq % 16 == 0
    even = even and up_w.shape[1] % 512 == 0 and tok_seq == tok_dev * (count // n_seq)
    if even and count * head_w.shape[0] == up_w.shape[0]:
        return per_device_fast(*args)
    return per_device_general(*args)


def solution(mesh):
    placed = (
        P(None, None, ("seq", "tp"), None),
        P(None, None, ("seq", "tp")),
        P(),
        P(None, "seq", None),
        P(),
        P(None, "tp"),
        P("tp", None),
        P(("seq", "tp"), None),
        P(),
        P(),
    )
    return jax.shard_map(
        per_device,
        mesh=mesh,
        in_specs=placed,
        out_specs=P(None, ("seq", "tp"), None),
        check_vma=False,
    )
```

```python
import functools

import jax
import jax.numpy as jnp
import numpy as np
from jax import lax
from jax.experimental import pallas as pl
from jax.experimental.pallas import tpu as pltpu
from jax.sharding import PartitionSpec as P

HEAD_DIM = 128


GUIDANCE = 0.1


def rope_angles(positions, head_dim):
    frame_width = head_dim // 8
    plane_width = (head_dim - frame_width) // 2
    pieces = []
    for axis, width in zip(range(3), (frame_width, plane_width, plane_width)):
        freqs = 10000.0 ** (-jnp.arange(0, width, 2, dtype=jnp.float32) / width)
        pieces.append(positions[axis][..., None] * freqs)
    return jnp.concatenate(pieces, axis=-1)


def rotate(values, angles):
    half = values.shape[-1] // 2
    floats = values.astype(jnp.float32)
    first = floats[..., :half]
    second = floats[..., half:]
    cosine = jnp.cos(angles)[:, :, None, :]
    sine = jnp.sin(angles)[:, :, None, :]
    turned = jnp.concatenate(
        [first * cosine - second * sine, first * sine + second * cosine], axis=-1
    )
    return turned.astype(jnp.bfloat16)


def gelu_slope(values):
    cdf = 0.5 * (1.0 + jax.scipy.special.erf(values * 0.7071067811865476))
    pdf = jnp.exp(-0.5 * values * values) * 0.3989422804014327
    return cdf + values * pdf


def pairs_first(array):
    samples, tokens = (array.shape[0], array.shape[1])
    return array.transpose(0, 2, 1, 3).reshape(samples * array.shape[2], tokens, HEAD_DIM)


def per_device_general(qkv, positions, w_proj, latents, embed_w, up_w, down_w, head_w, labels, timesteps):
    samples, tok_dev = (qkv.shape[1], qkv.shape[2])
    angles = rope_angles(positions.astype(jnp.float32), HEAD_DIM)
    heads = qkv.shape[3] // HEAD_DIM
    shaped = (samples, tok_dev, heads, HEAD_DIM)
    queries = rotate(qkv[0].reshape(shaped), angles)
    keys_tok = rotate(qkv[1].reshape(shaped), angles)
    values_tok = qkv[2].reshape(shaped)
    moved = lax.all_to_all(
        jnp.stack([pairs_first(queries), pairs_first(keys_tok), pairs_first(values_tok)]),
        "seq",
        split_axis=1,
        concat_axis=2,
        tiled=True,
    )
    query_pairs = moved[0]
    pair_count, query_count = (query_pairs.shape[0], query_pairs.shape[1])
    running = jnp.full((pair_count, query_count), -jnp.inf, jnp.float32)
    total = jnp.zeros((pair_count, query_count), jnp.float32)
    accum = jnp.zeros((pair_count, query_count, HEAD_DIM), jnp.float32)
    key_piece = lax.all_gather(moved[1], "tp", axis=1, tiled=True)
    value_piece = lax.all_gather(moved[2], "tp", axis=1, tiled=True)
    scores = jnp.einsum(
        "iqd,ikd->iqk", query_pairs, key_piece, preferred_element_type=jnp.float32
    ) * HEAD_DIM ** (-0.5)
    newest = jnp.max(scores, axis=-1)
    factor = jnp.exp(running - newest)
    weights = jnp.exp(scores - newest[..., None])
    total = total * factor + jnp.sum(weights, axis=-1)
    accum = accum * factor[..., None] + jnp.einsum(
        "iqk,ikd->iqd",
        weights.astype(jnp.bfloat16),
        value_piece,
        preferred_element_type=jnp.float32,
    )
    running, total, accum = (newest, total, accum)
    attended = (accum / total[..., None]).astype(jnp.bfloat16)
    returned = lax.all_to_all(attended, "seq", split_axis=1, concat_axis=0, tiled=True)
    returned = returned.reshape(samples, heads, tok_dev, HEAD_DIM).transpose(0, 2, 1, 3)
    returned = returned.reshape(samples, tok_dev, qkv.shape[3])
    eps = jnp.dot(returned, w_proj, preferred_element_type=jnp.float32)
    seq_len = latents.shape[1] * lax.axis_size("seq")
    tp_index = lax.axis_index("tp")
    emb = jnp.dot(latents, embed_w, preferred_element_type=jnp.float32).astype(jnp.bfloat16)
    hidden = jnp.dot(emb, up_w, preferred_element_type=jnp.float32)
    act = jax.nn.gelu(hidden, approximate=False).astype(jnp.bfloat16)
    branch = jnp.dot(act, down_w, preferred_element_type=jnp.float32)
    own_emb = lax.dynamic_slice_in_dim(emb, tp_index * tok_dev, tok_dev, 1).astype(jnp.float32)
    partial_pool = jnp.sum(branch, axis=1) + jnp.sum(own_emb, axis=1)
    head_rows = head_w.shape[0]
    flat_index = lax.axis_index("seq") * lax.axis_size("tp") + tp_index
    pooled = lax.psum(partial_pool, ("seq", "tp")) / seq_len
    pooled_share = lax.dynamic_slice_in_dim(pooled, flat_index * head_rows, head_rows, 1)
    head_float = head_w.astype(jnp.float32)
    logit_terms = jnp.dot(pooled_share, head_float, precision=lax.Precision.HIGHEST)
    logits = lax.psum(logit_terms, ("seq", "tp"))
    probs = jax.nn.softmax(logits, axis=-1)
    onehot = (labels[:, None] == jnp.arange(logits.shape[1], dtype=jnp.int32)[None, :]).astype(
        jnp.float32
    )
    grad_share = jnp.dot(onehot - probs, head_float.T, precision=lax.Precision.HIGHEST)
    dpool = lax.all_gather(grad_share, ("seq", "tp"), axis=1, tiled=True)
    dact = jnp.dot(dpool, down_w.astype(jnp.float32).T, precision=lax.Precision.HIGHEST)
    dh1 = (gelu_slope(hidden) * dact[:, None, :]).astype(jnp.bfloat16)
    demb = jnp.einsum("btf,cf->btc", dh1, up_w, preferred_element_type=jnp.float32)
    embed_float = embed_w.astype(jnp.float32)
    dx_terms = jnp.einsum("btc,lc->btl", demb, embed_float, precision=lax.Precision.HIGHEST)
    dx_mine = lax.psum_scatter(
        dx_terms.astype(jnp.bfloat16), "tp", scatter_dimension=1, tiled=True
    ).astype(jnp.float32)
    dx_pool = jnp.dot(dpool, embed_float.T, precision=lax.Precision.HIGHEST)
    dx_total = dx_mine + dx_pool[:, None, :]
    phase = (timesteps.astype(jnp.float32) / 1000.0 + 0.008) / 1.008 * (jnp.pi / 2)
    abar = jnp.cos(phase) ** 2
    scale = GUIDANCE * jnp.sqrt(1.0 - abar)
    return (eps - scale[:, None, None] * dx_total).astype(jnp.bfloat16)


def split_rows(values):
    high = values.astype(jnp.bfloat16)
    rest = values - high.astype(jnp.float32)
    middle = rest.astype(jnp.bfloat16)
    low = (rest - middle.astype(jnp.float32)).astype(jnp.bfloat16)
    return jnp.concatenate([high, middle, low], axis=0)


def split_dot(values, weights, contract=0):
    rows = values.shape[0]
    product = lax.dot_general(
        split_rows(values),
        weights,
        (((1,), (contract,)), ((), ())),
        preferred_element_type=jnp.float32,
    )
    return product[:rows] + product[rows : 2 * rows] + product[2 * rows :]


def split_two(values, axis):
    high = values.astype(jnp.bfloat16)
    low = (values - high.astype(jnp.float32)).astype(jnp.bfloat16)
    return jnp.concatenate([high, low], axis=axis)


LANES = 128


KEPT = 1


def in_hbm(*arrays):
    return [pltpu.with_memory_space_constraint(array, pltpu.HBM) for array in arrays]


def lane_frequencies():
    frame_width = HEAD_DIM // 8
    plane_width = (HEAD_DIM - frame_width) // 2
    freqs, axes = [], []
    for axis, width in zip(range(3), (frame_width, plane_width, plane_width)):
        steps = np.arange(0, width, 2, dtype=np.float32) / np.float32(width)
        freqs.append(np.float32(10000.0) ** (-steps))
        axes.append(np.full(width // 2, axis, np.float32))
    freqs, axes = (np.concatenate(freqs), np.concatenate(axes))
    table = np.stack([np.tile(freqs, 2), np.tile(axes, 2)]).astype(np.float32)
    return np.pad(table, ((0, 6), (0, 0)))


def forward_kernel(
    sizes,
    pos_hbm,
    table_hbm,
    qkv_hbm,
    own_hbm,
    other_hbm,
    embed_hbm,
    up_hbm,
    down_hbm,
    pay_ref,
    slope_ref,
    joint_ref,
    keep_ref,
    pos_ref,
    table_ref,
    qkv_ref,
    lat_ref,
    embed_ref,
    up_ref,
    down_ref,
    rows_ref,
    sems,
):
    n_seq, n_tp, steps, seq_len = sizes
    samples, tok_dev, width = qkv_ref.shape[1:]
    count = n_seq * n_tp
    per_sample = count // samples
    heads_dev = width // HEAD_DIM // per_sample
    tok_seq, lat = own_hbm.shape[1:]
    units = slope_ref.shape[1]
    part = units // steps
    kept = keep_ref.shape[0] // part
    half = lax.axis_index("seq") % 2

    def up_copy(step):
        start = pl.multiple_of(half * units + step * part, LANES)
        return pltpu.make_async_copy(
            up_hbm.at[:, pl.ds(start, part)], up_ref.at[step], sems.at[6 + step]
        )

    def down_at(step):
        if step < kept:
            return keep_ref.at[pl.ds(step * part, part)]
        return down_ref.at[pl.ds((step - kept) * part, part)]

    def down_copy(step):
        start = pl.multiple_of(half * units + step * part, LANES)
        return pltpu.make_async_copy(
            down_hbm.at[pl.ds(start, part)],
            down_at(step),
            sems.at[6 + steps + step],
        )

    own_copy = pltpu.make_async_copy(own_hbm, lat_ref.at[half], sems.at[0])
    other_copy = pltpu.make_async_copy(other_hbm, lat_ref.at[1 - half], sems.at[1])
    embed_copy = pltpu.make_async_copy(embed_hbm, embed_ref, sems.at[2])
    qkv_copy = pltpu.make_async_copy(qkv_hbm, qkv_ref, sems.at[3])
    pos_copy = pltpu.make_async_copy(pos_hbm, pos_ref, sems.at[4])
    table_copy = pltpu.make_async_copy(table_hbm, table_ref, sems.at[5])
    for copy in (pos_copy, table_copy, own_copy, other_copy, qkv_copy, embed_copy):
        copy.start()
    for step in range(steps):
        up_copy(step).start()
    for step in range(steps):
        down_copy(step).start()

    pos_copy.wait()
    table_copy.wait()

    shape = (samples * tok_dev, LANES)
    row = lax.broadcasted_iota(jnp.int32, shape, 0)
    lane = lax.broadcasted_iota(jnp.int32, shape, 1)
    axis = jnp.broadcast_to(table_ref[1:2, :], shape)
    angles = jnp.zeros(shape, jnp.float32)
    for index in range(samples * tok_dev):
        sample, token = divmod(index, tok_dev)
        frame, line, column = (pos_ref[k, sample, token].astype(jnp.float32) for k in range(3))
        value = jnp.where(axis < 0.5, frame, jnp.where(axis < 1.5, line, column))
        angles = jnp.where(row == index, value, angles)
    angles = angles * jnp.broadcast_to(table_ref[0:1, :], shape)
    cosine = jnp.cos(angles)
    sine = jnp.sin(angles)
    sine = jnp.where(lane < HEAD_DIM // 2, -sine, sine)

    qkv_copy.wait()
    for sample in range(samples):
        cos_rows = cosine[sample * tok_dev : (sample + 1) * tok_dev]
        sin_rows = sine[sample * tok_dev : (sample + 1) * tok_dev]
        for head in range(width // HEAD_DIM):
            target = sample * per_sample + head // heads_dev
            span = slice(head * HEAD_DIM, (head + 1) * HEAD_DIM)
            for kind in range(3):
                group = 2 + kind * heads_dev + head % heads_dev
                values = qkv_ref[kind, sample, :, span]
                if kind < 2:
                    values = values.astype(jnp.float32)
                    values = values * cos_rows + pltpu.roll(values, HEAD_DIM // 2, 1) * sin_rows
                pay_ref[target, group] = values.astype(jnp.bfloat16)

    own_copy.wait()
    other_copy.wait()
    tok_pair = 2 * tok_seq
    sums = []
    for sample in range(samples):
        pieces = [lat_ref[0, sample], lat_ref[1, sample]]
        rows = jnp.concatenate(pieces, axis=0)
        rows_ref[sample * tok_pair : (sample + 1) * tok_pair] = jnp.concatenate([rows, rows], axis=1)
        sums.append(jnp.sum(rows.astype(jnp.float32), axis=0, keepdims=True))
    lat_sum = jnp.concatenate(sums, axis=0) * (1.0 / (2 * n_tp))
    lat_high = lat_sum.astype(jnp.bfloat16)
    lat_low = (lat_sum - lat_high.astype(jnp.float32)).astype(jnp.bfloat16)
    lat_rows = rows_ref[...]

    embed_copy.wait()
    embed = embed_ref[...]
    total = jnp.dot(
        jnp.concatenate([lat_high, lat_low], axis=0), embed, preferred_element_type=jnp.float32
    )
    parts = []
    for step in range(steps):
        up_copy(step).wait()
        joint = jnp.dot(embed, up_ref[step], preferred_element_type=jnp.float32)
        high = joint.astype(jnp.bfloat16)
        low = (joint - high.astype(jnp.float32)).astype(jnp.bfloat16)
        joint = jnp.concatenate([high, low], axis=0)
        span = slice(step * part, (step + 1) * part)
        joint_ref[:, span] = joint
        hidden = jnp.dot(lat_rows, joint, preferred_element_type=jnp.float32)
        cdf = 0.5 * (1.0 + lax.erf(hidden * 0.7071067811865476))
        pdf = jnp.exp(-0.5 * hidden * hidden) * 0.3989422804014327
        slope_ref[:, span] = cdf + hidden * pdf
        act_sum = jnp.sum((hidden * cdf).reshape(samples, tok_pair, part), axis=1)
        high = act_sum.astype(jnp.bfloat16)
        low = (act_sum - high.astype(jnp.float32)).astype(jnp.bfloat16)
        parts.append(jnp.concatenate([high, low], axis=0))
    for step in range(steps):
        down_copy(step).wait()
        total = total + jnp.dot(
            parts[step],
            down_at(step)[...],
            preferred_element_type=jnp.float32,
        )
    pool = (total[:samples] + total[samples:]) * (1.0 / seq_len)
    side = lax.broadcasted_iota(jnp.int32, (samples, LANES), 1) < LANES // 2
    for plane in range(n_seq // 2):
        for column in range(n_tp):
            first = (plane * 2 * n_tp + column) // 2
            second = (plane * 2 * n_tp + n_tp + column) // 2
            first = pool[:, first * LANES : (first + 1) * LANES]
            second = pool[:, second * LANES : (second + 1) * LANES]
            if column % 2 == 0:
                block = jnp.where(side, first, pltpu.roll(second, LANES // 2, 1))
            else:
                block = jnp.where(side, pltpu.roll(first, LANES // 2, 1), second)
            high = block.astype(jnp.bfloat16)
            low = (block - high.astype(jnp.float32)).astype(jnp.bfloat16)
            for core in range(2):
                target = (plane * 2 + core) * n_tp + column
                pay_ref[target, 0] = high
                pay_ref[target, 1] = low


def forward(qkv, positions, own, other, embed_w, up_w, down_w, n_seq, n_tp):
    samples, tok_dev, width = qkv.shape[1:]
    count = n_seq * n_tp
    groups = 2 + 3 * (width // HEAD_DIM // (count // samples))
    tok_seq, lat = own.shape[1:]
    units, features = (up_w.shape[1] // 2, up_w.shape[0])
    steps = units // 256
    rows = 2 * tok_seq * samples
    any_spec = pl.BlockSpec(memory_space=pl.ANY)
    vmem_spec = pl.BlockSpec(memory_space=pltpu.VMEM)
    return pl.pallas_call(
        functools.partial(forward_kernel, (n_seq, n_tp, steps, tok_dev * count)),
        out_shape=(
            jax.ShapeDtypeStruct((count, groups, tok_dev, LANES), jnp.bfloat16),
            jax.ShapeDtypeStruct((rows, units), jnp.float32),
            jax.ShapeDtypeStruct((2 * lat, units), jnp.bfloat16),
            jax.ShapeDtypeStruct((KEPT * 256, features), jnp.bfloat16),
        ),
        in_specs=[any_spec] * 8,
        out_specs=(vmem_spec,) * 4,
        scratch_shapes=[
            pltpu.SMEM(positions.shape, jnp.int32),
            pltpu.VMEM((8, LANES), jnp.float32),
            pltpu.VMEM(qkv.shape, jnp.bfloat16),
            pltpu.VMEM((2,) + own.shape, jnp.bfloat16),
            pltpu.VMEM(embed_w.shape, jnp.bfloat16),
            pltpu.VMEM((steps, features, 256), jnp.bfloat16),
            pltpu.VMEM((units - KEPT * 256, features), jnp.bfloat16),
            pltpu.VMEM((rows, 2 * lat), jnp.bfloat16),
            pltpu.SemaphoreType.DMA((6 + 2 * steps,)),
        ],
        compiler_params=pltpu.CompilerParams(vmem_limit_bytes=32 << 20),
        cost_estimate=pl.CostEstimate(
            flops=4 * features * units * 64, bytes_accessed=4 * features * units, transcendentals=0
        ),
        name="forward",
    )(*in_hbm(positions, jnp.asarray(lane_frequencies()), qkv, own), other, *in_hbm(embed_w, up_w, down_w))


def backward_kernel(
    steps, second_ref, slope_ref, joint_ref, keep_ref, down_hbm, out_ref, dpool_ref, down_ref, sems
):
    count, groups, samples, _ = second_ref.shape
    units = slope_ref.shape[1]
    part = units // steps
    kept = keep_ref.shape[0] // part
    half = lax.axis_index("seq") % 2

    def down_copy(step):
        start = pl.multiple_of(half * units + step * part, LANES)
        return pltpu.make_async_copy(
            down_hbm.at[pl.ds(start, part)],
            down_ref.at[pl.ds((step - kept) * part, part)],
            sems.at[step - kept],
        )

    for step in range(kept, steps):
        down_copy(step).start()
    rows = slope_ref.shape[0] // samples
    side = lax.broadcasted_iota(jnp.int32, (samples, LANES), 1) < LANES // 2
    for pair in range(count // 2):
        first = second_ref[2 * pair, groups - 1].astype(jnp.float32)
        second = second_ref[2 * pair + 1, groups - 1].astype(jnp.float32)
        first = first + pltpu.roll(first, LANES // 2, 1)
        second = second + pltpu.roll(second, LANES // 2, 1)
        block = jnp.where(side, first, second)
        high = block.astype(jnp.bfloat16)
        low = (block - high.astype(jnp.float32)).astype(jnp.bfloat16)
        dpool_ref[:, pair * LANES : (pair + 1) * LANES] = jnp.concatenate([high, low], axis=0)
    dpool = dpool_ref[...]
    across = (((1,), (1,)), ((), ()))
    dx = None
    for step in range(steps):
        if step < kept:
            weights = keep_ref[step * part : (step + 1) * part]
        else:
            down_copy(step).wait()
            weights = down_ref[(step - kept) * part : (step - kept + 1) * part]
        dact = lax.dot_general(dpool, weights, across, preferred_element_type=jnp.float32)
        dact = dact[:samples] + dact[samples:]
        span = slice(step * part, (step + 1) * part)
        slope = slope_ref[:, span].reshape(samples, rows, part)
        dh1 = (slope * dact[:, None, :]).reshape(samples * rows, part).astype(jnp.bfloat16)
        term = lax.dot_general(dh1, joint_ref[:, span], across, preferred_element_type=jnp.float32)
        dx = term if dx is None else dx + term
    dx = dx + pltpu.roll(dx, LANES // 2, 1)
    side = lax.broadcasted_iota(jnp.int32, (rows, LANES), 1) < LANES // 2
    tok_dev = out_ref.shape[2]
    for pair in range(samples // 2):
        first = dx[2 * pair * rows : (2 * pair + 1) * rows]
        second = dx[(2 * pair + 1) * rows : (2 * pair + 2) * rows]
        both = jnp.where(side, first, second)
        for target in range(rows // tok_dev):
            out_ref[target, pair] = both[target * tok_dev : (target + 1) * tok_dev].astype(jnp.bfloat16)


def backward(second, slope, joint, keep, down, tok_dev):
    samples = second.shape[2]
    targets = slope.shape[0] // samples // tok_dev
    units, steps = (slope.shape[1], slope.shape[1] // 256)
    vmem_spec = pl.BlockSpec(memory_space=pltpu.VMEM)
    return pl.pallas_call(
        functools.partial(backward_kernel, steps),
        out_shape=(
            jax.ShapeDtypeStruct((targets, samples // 2, tok_dev, LANES), jnp.bfloat16),
            jax.ShapeDtypeStruct((2 * samples, down.shape[1]), jnp.bfloat16),
        ),
        in_specs=[vmem_spec] * 4 + [pl.BlockSpec(memory_space=pl.ANY)],
        out_specs=(vmem_spec,) * 2,
        scratch_shapes=[
            pltpu.VMEM((units - keep.shape[0], down.shape[1]), jnp.bfloat16),
            pltpu.SemaphoreType.DMA((steps - KEPT,)),
        ],
        compiler_params=pltpu.CompilerParams(vmem_limit_bytes=32 << 20),
        name="backward",
    )(second, slope, joint, keep, *in_hbm(down))


def per_device_fast(qkv, positions, w_proj, latents, embed_w, up_w, down_w, head_w, labels, timesteps):
    both = ("seq", "tp")
    n_seq, n_tp = (lax.axis_size("seq"), lax.axis_size("tp"))
    count = n_seq * n_tp
    seq_index = lax.axis_index("seq")
    half = seq_index % 2
    samples, tok_dev, width = qkv.shape[1:]
    seq_len = tok_dev * count
    lat = latents.shape[2]
    heads = width // HEAD_DIM
    per_sample = count // samples
    heads_dev = heads // per_sample
    rows_dev, classes = head_w.shape
    partner = [(i, i ^ n_tp) for i in range(count)]

    def in_order(own):
        other = lax.ppermute(own, both, partner)
        mine = jnp.broadcast_to(half == 0, own.shape)
        return jnp.stack([jnp.where(mine, own, other), jnp.where(mine, other, own)])

    other = lax.ppermute(latents, both, partner)
    head_pair = in_order(head_w).reshape(2 * rows_dev, classes)

    payload, slope, joint, keep = forward(
        qkv, positions, latents, other, embed_w, up_w, down_w, n_seq, n_tp
    )
    moved = lax.all_to_all(payload, both, 0, 0, tiled=True)

    pooled = jnp.sum(moved[:, :2].astype(jnp.float32), axis=(0, 1))
    padded = -(-classes // 256) * 256
    terms = jnp.pad(split_dot(pooled, head_pair), ((0, 0), (0, padded - classes)))
    terms = lax.dynamic_slice_in_dim(terms, half * (padded // 2), padded // 2, 1)
    terms = lax.all_to_all(
        jnp.broadcast_to(terms.astype(jnp.bfloat16)[None], (count,) + terms.shape),
        both,
        0,
        0,
        tiled=True,
    )

    views = moved[:, 2:].reshape(count, 3, heads_dev, tok_dev, HEAD_DIM)
    views = views.transpose(1, 2, 0, 3, 4).reshape(3, heads_dev, seq_len, HEAD_DIM)
    scores = jnp.einsum(
        "hqd,hkd->hqk", views[0], views[1], preferred_element_type=jnp.float32
    ) * HEAD_DIM ** (-0.5)
    weights = jnp.exp(scores - jnp.max(scores, axis=-1, keepdims=True))
    total = jnp.sum(weights, axis=-1)
    mixed = jnp.einsum(
        "hqk,hkd->hqd", weights.astype(jnp.bfloat16), views[2], preferred_element_type=jnp.float32
    )
    attended = (mixed / total[..., None]).astype(jnp.bfloat16)
    first_row = (seq_index * n_tp + lax.axis_index("tp")) % per_sample * heads_dev * HEAD_DIM
    proj_mine = lax.dynamic_slice_in_dim(w_proj, first_row, heads_dev * HEAD_DIM, 0)
    eps_terms = jnp.einsum(
        "hqd,hdl->ql",
        attended,
        proj_mine.reshape(heads_dev, HEAD_DIM, lat),
        preferred_element_type=jnp.float32,
    )
    eps_terms = split_two(eps_terms, 1).reshape(count, 1, tok_dev, 2 * lat)

    terms = terms.astype(jnp.float32).reshape(n_seq // 2, 2, n_tp, samples, padded // 2)
    logits = jnp.sum(terms, axis=(0, 2))
    logits = logits.transpose(1, 0, 2).reshape(samples, padded)[:, :classes]
    probs = jax.nn.softmax(logits, axis=-1)
    onehot = (labels[:, None] == jnp.arange(classes, dtype=jnp.int32)[None, :]).astype(jnp.float32)
    share = split_two(split_dot(onehot - probs, head_w, 1), 1)
    share = jnp.broadcast_to(share[None, None], (count, 1) + share.shape)
    second = lax.all_to_all(
        jnp.concatenate([eps_terms, share], axis=1), both, 0, 0, tiled=True
    )
    eps = second[:, 0].astype(jnp.float32).reshape(samples, per_sample, tok_dev, 2 * lat)
    eps = jnp.sum(eps, axis=1)
    eps = eps[..., :lat] + eps[..., lat:]
    eps = lax.optimization_barrier(eps)
    dx_terms, dpool = backward(second, slope, joint, keep, down_w, tok_dev)
    planes = [[first + k for k in range(2 * n_tp)] for first in range(0, count, 2 * n_tp)]
    dx_terms = lax.all_to_all(dx_terms, both, 0, 0, tiled=True, axis_index_groups=planes)
    dx = jnp.sum(dx_terms.astype(jnp.float32), axis=0)
    dx = dx.reshape(samples // 2, tok_dev, 2, lat).transpose(0, 2, 1, 3)
    dx = dx.reshape(samples, tok_dev, lat)
    dx_pool = lax.dot_general(
        dpool, embed_w, (((1,), (1,)), ((), ())), preferred_element_type=jnp.float32
    )
    dx = dx + (dx_pool[:samples] + dx_pool[samples:])[:, None, :]
    phase = (timesteps.astype(jnp.float32) / 1000.0 + 0.008) / 1.008 * (jnp.pi / 2)
    abar = jnp.cos(phase) ** 2
    scale = GUIDANCE * jnp.sqrt(1.0 - abar)
    return (eps - scale[:, None, None] * dx).astype(jnp.bfloat16)


def per_device(qkv, positions, w_proj, latents, embed_w, up_w, down_w, head_w, labels, timesteps):
    args = (qkv, positions, w_proj, latents, embed_w, up_w, down_w, head_w, labels, timesteps)
    n_seq = lax.axis_size("seq")
    count = n_seq * lax.axis_size("tp")
    samples, heads = (qkv.shape[1], qkv.shape[3] // HEAD_DIM)
    tok_dev, tok_seq, lat = (qkv.shape[2], latents.shape[1], latents.shape[2])
    even = count % samples == 0 and heads % max(1, count // samples) == 0
    even = even and n_seq % 2 == 0 and count // n_seq % 2 == 0 and samples == 4 and tok_dev == 4
    even = even and lat == 64 and head_w.shape[0] == 64 and tok_seq % 16 == 0
    even = even and up_w.shape[1] % 512 == 0 and tok_seq == tok_dev * (count // n_seq)
    if even and count * head_w.shape[0] == up_w.shape[0]:
        return per_device_fast(*args)
    return per_device_general(*args)


def solution(mesh):
    placed = (
        P(None, None, ("seq", "tp"), None),
        P(None, None, ("seq", "tp")),
        P(),
        P(None, "seq", None),
        P(),
        P(None, "tp"),
        P("tp", None),
        P(("seq", "tp"), None),
        P(),
        P(),
    )
    return jax.shard_map(
        per_device,
        mesh=mesh,
        in_specs=placed,
        out_specs=P(None, ("seq", "tp"), None),
        check_vma=False,
    )
```

```python
import functools

import jax
import jax.numpy as jnp
import numpy as np
from jax import lax
from jax.experimental import pallas as pl
from jax.experimental.pallas import tpu as pltpu
from jax.sharding import PartitionSpec as P

HEAD_DIM = 128


GUIDANCE = 0.1


def rope_angles(positions, head_dim):
    frame_width = head_dim // 8
    plane_width = (head_dim - frame_width) // 2
    pieces = []
    for axis, width in zip(range(3), (frame_width, plane_width, plane_width)):
        freqs = 10000.0 ** (-jnp.arange(0, width, 2, dtype=jnp.float32) / width)
        pieces.append(positions[axis][..., None] * freqs)
    return jnp.concatenate(pieces, axis=-1)


def rotate(values, angles):
    half = values.shape[-1] // 2
    floats = values.astype(jnp.float32)
    first = floats[..., :half]
    second = floats[..., half:]
    cosine = jnp.cos(angles)[:, :, None, :]
    sine = jnp.sin(angles)[:, :, None, :]
    turned = jnp.concatenate(
        [first * cosine - second * sine, first * sine + second * cosine], axis=-1
    )
    return turned.astype(jnp.bfloat16)


def gelu_slope(values):
    cdf = 0.5 * (1.0 + jax.scipy.special.erf(values * 0.7071067811865476))
    pdf = jnp.exp(-0.5 * values * values) * 0.3989422804014327
    return cdf + values * pdf


def pairs_first(array):
    samples, tokens = (array.shape[0], array.shape[1])
    return array.transpose(0, 2, 1, 3).reshape(samples * array.shape[2], tokens, HEAD_DIM)


def per_device_general(qkv, positions, w_proj, latents, embed_w, up_w, down_w, head_w, labels, timesteps):
    samples, tok_dev = (qkv.shape[1], qkv.shape[2])
    angles = rope_angles(positions.astype(jnp.float32), HEAD_DIM)
    heads = qkv.shape[3] // HEAD_DIM
    shaped = (samples, tok_dev, heads, HEAD_DIM)
    queries = rotate(qkv[0].reshape(shaped), angles)
    keys_tok = rotate(qkv[1].reshape(shaped), angles)
    values_tok = qkv[2].reshape(shaped)
    moved = lax.all_to_all(
        jnp.stack([pairs_first(queries), pairs_first(keys_tok), pairs_first(values_tok)]),
        "seq",
        split_axis=1,
        concat_axis=2,
        tiled=True,
    )
    query_pairs = moved[0]
    pair_count, query_count = (query_pairs.shape[0], query_pairs.shape[1])
    running = jnp.full((pair_count, query_count), -jnp.inf, jnp.float32)
    total = jnp.zeros((pair_count, query_count), jnp.float32)
    accum = jnp.zeros((pair_count, query_count, HEAD_DIM), jnp.float32)
    key_piece = lax.all_gather(moved[1], "tp", axis=1, tiled=True)
    value_piece = lax.all_gather(moved[2], "tp", axis=1, tiled=True)
    scores = jnp.einsum(
        "iqd,ikd->iqk", query_pairs, key_piece, preferred_element_type=jnp.float32
    ) * HEAD_DIM ** (-0.5)
    newest = jnp.max(scores, axis=-1)
    factor = jnp.exp(running - newest)
    weights = jnp.exp(scores - newest[..., None])
    total = total * factor + jnp.sum(weights, axis=-1)
    accum = accum * factor[..., None] + jnp.einsum(
        "iqk,ikd->iqd",
        weights.astype(jnp.bfloat16),
        value_piece,
        preferred_element_type=jnp.float32,
    )
    running, total, accum = (newest, total, accum)
    attended = (accum / total[..., None]).astype(jnp.bfloat16)
    returned = lax.all_to_all(attended, "seq", split_axis=1, concat_axis=0, tiled=True)
    returned = returned.reshape(samples, heads, tok_dev, HEAD_DIM).transpose(0, 2, 1, 3)
    returned = returned.reshape(samples, tok_dev, qkv.shape[3])
    eps = jnp.dot(returned, w_proj, preferred_element_type=jnp.float32)
    seq_len = latents.shape[1] * lax.axis_size("seq")
    tp_index = lax.axis_index("tp")
    emb = jnp.dot(latents, embed_w, preferred_element_type=jnp.float32).astype(jnp.bfloat16)
    hidden = jnp.dot(emb, up_w, preferred_element_type=jnp.float32)
    act = jax.nn.gelu(hidden, approximate=False).astype(jnp.bfloat16)
    branch = jnp.dot(act, down_w, preferred_element_type=jnp.float32)
    own_emb = lax.dynamic_slice_in_dim(emb, tp_index * tok_dev, tok_dev, 1).astype(jnp.float32)
    partial_pool = jnp.sum(branch, axis=1) + jnp.sum(own_emb, axis=1)
    head_rows = head_w.shape[0]
    flat_index = lax.axis_index("seq") * lax.axis_size("tp") + tp_index
    pooled = lax.psum(partial_pool, ("seq", "tp")) / seq_len
    pooled_share = lax.dynamic_slice_in_dim(pooled, flat_index * head_rows, head_rows, 1)
    head_float = head_w.astype(jnp.float32)
    logit_terms = jnp.dot(pooled_share, head_float, precision=lax.Precision.HIGHEST)
    logits = lax.psum(logit_terms, ("seq", "tp"))
    probs = jax.nn.softmax(logits, axis=-1)
    onehot = (labels[:, None] == jnp.arange(logits.shape[1], dtype=jnp.int32)[None, :]).astype(
        jnp.float32
    )
    grad_share = jnp.dot(onehot - probs, head_float.T, precision=lax.Precision.HIGHEST)
    dpool = lax.all_gather(grad_share, ("seq", "tp"), axis=1, tiled=True)
    dact = jnp.dot(dpool, down_w.astype(jnp.float32).T, precision=lax.Precision.HIGHEST)
    dh1 = (gelu_slope(hidden) * dact[:, None, :]).astype(jnp.bfloat16)
    demb = jnp.einsum("btf,cf->btc", dh1, up_w, preferred_element_type=jnp.float32)
    embed_float = embed_w.astype(jnp.float32)
    dx_terms = jnp.einsum("btc,lc->btl", demb, embed_float, precision=lax.Precision.HIGHEST)
    dx_mine = lax.psum_scatter(
        dx_terms.astype(jnp.bfloat16), "tp", scatter_dimension=1, tiled=True
    ).astype(jnp.float32)
    dx_pool = jnp.dot(dpool, embed_float.T, precision=lax.Precision.HIGHEST)
    dx_total = dx_mine + dx_pool[:, None, :]
    phase = (timesteps.astype(jnp.float32) / 1000.0 + 0.008) / 1.008 * (jnp.pi / 2)
    abar = jnp.cos(phase) ** 2
    scale = GUIDANCE * jnp.sqrt(1.0 - abar)
    return (eps - scale[:, None, None] * dx_total).astype(jnp.bfloat16)


def rounded(values):
    return lax.reduce_precision(values, exponent_bits=8, mantissa_bits=7)


def split_rows(values):
    high = rounded(values)
    middle = rounded(values - high)
    low = values - high - middle
    return jnp.concatenate([high, middle, low], axis=0).astype(jnp.bfloat16)


def split_dot(values, weights, contract=0):
    rows = values.shape[0]
    product = lax.dot_general(
        split_rows(values),
        weights,
        (((1,), (contract,)), ((), ())),
        preferred_element_type=jnp.float32,
    )
    return product[:rows] + product[rows : 2 * rows] + product[2 * rows :]


def split_two(values, axis):
    high = rounded(values)
    return jnp.concatenate([high, values - high], axis=axis).astype(jnp.bfloat16)


LANES = 128


KEPT = 2


def in_hbm(*arrays):
    return [pltpu.with_memory_space_constraint(array, pltpu.HBM) for array in arrays]


def lane_frequencies():
    frame_width = HEAD_DIM // 8
    plane_width = (HEAD_DIM - frame_width) // 2
    freqs, axes = [], []
    for axis, width in zip(range(3), (frame_width, plane_width, plane_width)):
        steps = np.arange(0, width, 2, dtype=np.float32) / np.float32(width)
        freqs.append(np.float32(10000.0) ** (-steps))
        axes.append(np.full(width // 2, axis, np.float32))
    freqs, axes = (np.concatenate(freqs), np.concatenate(axes))
    table = np.stack([np.tile(freqs, 2), np.tile(axes, 2)]).astype(np.float32)
    return np.pad(table, ((0, 6), (0, 0)))


def forward_kernel(
    sizes,
    pos_hbm,
    table_hbm,
    qkv_hbm,
    own_hbm,
    other_hbm,
    embed_hbm,
    up_hbm,
    down_hbm,
    proj_hbm,
    pay_ref,
    slope_ref,
    joint_ref,
    keep_ref,
    proj_ref,
    pos_ref,
    table_ref,
    qkv_ref,
    lat_ref,
    embed_ref,
    up_ref,
    down_ref,
    rows_ref,
    sems,
):
    n_seq, n_tp, steps, seq_len = sizes
    samples, tok_dev, width = qkv_ref.shape[1:]
    count = n_seq * n_tp
    per_sample = count // samples
    heads_dev = width // HEAD_DIM // per_sample
    tok_seq, lat = own_hbm.shape[1:]
    units = slope_ref.shape[1]
    part = units // steps
    kept = keep_ref.shape[0] // part
    half = lax.axis_index("seq") % 2

    def up_copy(step):
        start = pl.multiple_of(half * units + step * part, LANES)
        return pltpu.make_async_copy(
            up_hbm.at[:, pl.ds(start, part)], up_ref.at[step], sems.at[6 + step]
        )

    def down_at(step):
        if step < kept:
            return keep_ref.at[pl.ds(step * part, part)]
        return down_ref.at[pl.ds((step - kept) * part, part)]

    def down_copy(step):
        start = pl.multiple_of(half * units + step * part, LANES)
        return pltpu.make_async_copy(
            down_hbm.at[pl.ds(start, part)],
            down_at(step),
            sems.at[6 + steps + step],
        )

    own_copy = pltpu.make_async_copy(own_hbm, lat_ref.at[half], sems.at[0])
    other_copy = pltpu.make_async_copy(other_hbm, lat_ref.at[1 - half], sems.at[1])
    embed_copy = pltpu.make_async_copy(embed_hbm, embed_ref, sems.at[2])
    qkv_copy = pltpu.make_async_copy(qkv_hbm, qkv_ref, sems.at[3])
    chunk = proj_ref.shape[1]
    flat = lax.axis_index("seq") * n_tp + lax.axis_index("tp")
    first_column = pl.multiple_of(lax.rem(flat, per_sample) * chunk, chunk)
    proj_copy = pltpu.make_async_copy(
        proj_hbm.at[:, pl.ds(first_column, chunk)], proj_ref, sems.at[6 + 2 * steps]
    )
    pos_copy = pltpu.make_async_copy(pos_hbm, pos_ref, sems.at[4])
    table_copy = pltpu.make_async_copy(table_hbm, table_ref, sems.at[5])
    for copy in (pos_copy, table_copy, own_copy, other_copy, qkv_copy, embed_copy):
        copy.start()
    for step in range(steps):
        up_copy(step).start()
    for step in range(steps):
        down_copy(step).start()
    proj_copy.start()

    pos_copy.wait()
    table_copy.wait()

    shape = (samples * tok_dev, LANES)
    row = lax.broadcasted_iota(jnp.int32, shape, 0)
    lane = lax.broadcasted_iota(jnp.int32, shape, 1)
    axis = jnp.broadcast_to(table_ref[1:2, :], shape)
    angles = jnp.zeros(shape, jnp.float32)
    for index in range(samples * tok_dev):
        sample, token = divmod(index, tok_dev)
        frame, line, column = (pos_ref[k, sample, token].astype(jnp.float32) for k in range(3))
        value = jnp.where(axis < 0.5, frame, jnp.where(axis < 1.5, line, column))
        angles = jnp.where(row == index, value, angles)
    angles = angles * jnp.broadcast_to(table_ref[0:1, :], shape)
    cosine = jnp.cos(angles)
    sine = jnp.sin(angles)
    sine = jnp.where(lane < HEAD_DIM // 2, -sine, sine)

    qkv_copy.wait()
    for sample in range(samples):
        cos_rows = cosine[sample * tok_dev : (sample + 1) * tok_dev]
        sin_rows = sine[sample * tok_dev : (sample + 1) * tok_dev]
        for head in range(width // HEAD_DIM):
            target = sample * per_sample + head // heads_dev
            span = slice(head * HEAD_DIM, (head + 1) * HEAD_DIM)
            for kind in range(3):
                group = 1 + kind * heads_dev + head % heads_dev
                values = qkv_ref[kind, sample, :, span]
                if kind < 2:
                    values = values.astype(jnp.float32)
                    values = values * cos_rows + pltpu.roll(values, HEAD_DIM // 2, 1) * sin_rows
                pay_ref[target, group] = values.astype(jnp.bfloat16)

    own_copy.wait()
    other_copy.wait()
    tok_pair = 2 * tok_seq
    sums = []
    for sample in range(samples):
        pieces = [lat_ref[0, sample], lat_ref[1, sample]]
        rows = jnp.concatenate(pieces, axis=0)
        rows_ref[sample * tok_pair : (sample + 1) * tok_pair] = jnp.concatenate([rows, rows], axis=1)
        sums.append(jnp.sum(rows.astype(jnp.float32), axis=0, keepdims=True))
    lat_sum = jnp.concatenate(sums, axis=0) * (1.0 / (2 * n_tp))
    lat_high = lat_sum.astype(jnp.bfloat16)
    lat_low = (lat_sum - lat_high.astype(jnp.float32)).astype(jnp.bfloat16)
    lat_rows = rows_ref[...]

    embed_copy.wait()
    embed = embed_ref[...]
    total = jnp.dot(
        jnp.concatenate([lat_high, lat_low], axis=0), embed, preferred_element_type=jnp.float32
    )
    parts = []
    for step in range(steps):
        up_copy(step).wait()
        joint = jnp.dot(embed, up_ref[step], preferred_element_type=jnp.float32)
        high = joint.astype(jnp.bfloat16)
        low = (joint - high.astype(jnp.float32)).astype(jnp.bfloat16)
        joint = jnp.concatenate([high, low], axis=0)
        span = slice(step * part, (step + 1) * part)
        joint_ref[:, span] = joint
        hidden = jnp.dot(lat_rows, joint, preferred_element_type=jnp.float32)
        cdf = 0.5 * (1.0 + lax.erf(hidden * 0.7071067811865476))
        pdf = jnp.exp(-0.5 * hidden * hidden) * 0.3989422804014327
        slope_ref[:, span] = (cdf + hidden * pdf).astype(jnp.bfloat16)
        act_sum = jnp.sum((hidden * cdf).reshape(samples, tok_pair, part), axis=1)
        high = act_sum.astype(jnp.bfloat16)
        low = (act_sum - high.astype(jnp.float32)).astype(jnp.bfloat16)
        parts.append(jnp.concatenate([high, low], axis=0))
    for step in range(steps):
        down_copy(step).wait()
        total = total + jnp.dot(
            parts[step],
            down_at(step)[...],
            preferred_element_type=jnp.float32,
        )
    proj_copy.wait()
    pool = (total[:samples] + total[samples:]) * (1.0 / seq_len)
    side = lax.broadcasted_iota(jnp.int32, (samples, LANES), 1) < LANES // 2
    for plane in range(n_seq // 2):
        for column in range(n_tp):
            first = (plane * 2 * n_tp + column) // 2
            second = (plane * 2 * n_tp + n_tp + column) // 2
            first = pool[:, first * LANES : (first + 1) * LANES]
            second = pool[:, second * LANES : (second + 1) * LANES]
            if column % 2 == 0:
                block = jnp.where(side, first, pltpu.roll(second, LANES // 2, 1))
            else:
                block = jnp.where(side, pltpu.roll(first, LANES // 2, 1), second)
            for core in range(2):
                target = (plane * 2 + core) * n_tp + column
                pay_ref[target, 0] = block.astype(jnp.bfloat16)


def forward(qkv, positions, own, other, embed_w, up_w, down_w, w_proj, n_seq, n_tp):
    samples, tok_dev, width = qkv.shape[1:]
    count = n_seq * n_tp
    groups = 1 + 3 * (width // HEAD_DIM // (count // samples))
    tok_seq, lat = own.shape[1:]
    units, features = (up_w.shape[1] // 2, up_w.shape[0])
    steps = units // 256
    rows = 2 * tok_seq * samples
    any_spec = pl.BlockSpec(memory_space=pl.ANY)
    vmem_spec = pl.BlockSpec(memory_space=pltpu.VMEM)
    return pl.pallas_call(
        functools.partial(forward_kernel, (n_seq, n_tp, steps, tok_dev * count)),
        out_shape=(
            jax.ShapeDtypeStruct((count, groups, tok_dev, LANES), jnp.bfloat16),
            jax.ShapeDtypeStruct((rows, units), jnp.bfloat16),
            jax.ShapeDtypeStruct((2 * lat, units), jnp.bfloat16),
            jax.ShapeDtypeStruct((KEPT * 256, features), jnp.bfloat16),
            jax.ShapeDtypeStruct((lat, width * samples // count), jnp.bfloat16),
        ),
        in_specs=[any_spec] * 9,
        out_specs=(vmem_spec,) * 5,
        scratch_shapes=[
            pltpu.SMEM(positions.shape, jnp.int32),
            pltpu.VMEM((8, LANES), jnp.float32),
            pltpu.VMEM(qkv.shape, jnp.bfloat16),
            pltpu.VMEM((2,) + own.shape, jnp.bfloat16),
            pltpu.VMEM(embed_w.shape, jnp.bfloat16),
            pltpu.VMEM((steps, features, 256), jnp.bfloat16),
            pltpu.VMEM((units - KEPT * 256, features), jnp.bfloat16),
            pltpu.VMEM((rows, 2 * lat), jnp.bfloat16),
            pltpu.SemaphoreType.DMA((7 + 2 * steps,)),
        ],
        compiler_params=pltpu.CompilerParams(vmem_limit_bytes=32 << 20),
        cost_estimate=pl.CostEstimate(
            flops=4 * features * units * 64, bytes_accessed=4 * features * units, transcendentals=0
        ),
        name="forward",
    )(*in_hbm(positions, jnp.asarray(lane_frequencies()), qkv, own), other, *in_hbm(embed_w, up_w, down_w, w_proj))


def backward_kernel(
    steps, second_ref, slope_ref, joint_ref, keep_ref, down_hbm, out_ref, dpool_ref, down_ref, sems
):
    count, groups, samples, _ = second_ref.shape
    units = slope_ref.shape[1]
    part = units // steps
    kept = keep_ref.shape[0] // part
    half = lax.axis_index("seq") % 2

    def down_copy(step):
        start = pl.multiple_of(half * units + step * part, LANES)
        return pltpu.make_async_copy(
            down_hbm.at[pl.ds(start, part)],
            down_ref.at[pl.ds((step - kept) * part, part)],
            sems.at[step - kept],
        )

    for step in range(kept, steps):
        down_copy(step).start()
    rows = slope_ref.shape[0] // samples
    side = lax.broadcasted_iota(jnp.int32, (samples, LANES), 1) < LANES // 2
    for pair in range(count // 2):
        first = second_ref[2 * pair, groups - 1].astype(jnp.float32)
        second = second_ref[2 * pair + 1, groups - 1].astype(jnp.float32)
        first = first + pltpu.roll(first, LANES // 2, 1)
        second = second + pltpu.roll(second, LANES // 2, 1)
        block = jnp.where(side, first, second)
        high = block.astype(jnp.bfloat16)
        low = (block - high.astype(jnp.float32)).astype(jnp.bfloat16)
        dpool_ref[:, pair * LANES : (pair + 1) * LANES] = jnp.concatenate([high, low], axis=0)
    dpool = dpool_ref[...]
    across = (((1,), (1,)), ((), ()))
    dx = None
    for step in range(steps):
        if step < kept:
            weights = keep_ref[step * part : (step + 1) * part]
        else:
            down_copy(step).wait()
            weights = down_ref[(step - kept) * part : (step - kept + 1) * part]
        dact = lax.dot_general(dpool, weights, across, preferred_element_type=jnp.float32)
        dact = dact[:samples] + dact[samples:]
        span = slice(step * part, (step + 1) * part)
        slope = slope_ref[:, span].astype(jnp.float32).reshape(samples, rows, part)
        dh1 = (slope * dact[:, None, :]).reshape(samples * rows, part).astype(jnp.bfloat16)
        term = lax.dot_general(dh1, joint_ref[:, span], across, preferred_element_type=jnp.float32)
        dx = term if dx is None else dx + term
    dx = dx + pltpu.roll(dx, LANES // 2, 1)
    side = lax.broadcasted_iota(jnp.int32, (rows, LANES), 1) < LANES // 2
    tok_dev = out_ref.shape[2]
    for pair in range(samples // 2):
        first = dx[2 * pair * rows : (2 * pair + 1) * rows]
        second = dx[(2 * pair + 1) * rows : (2 * pair + 2) * rows]
        both = jnp.where(side, first, second)
        for target in range(rows // tok_dev):
            out_ref[target, pair] = both[target * tok_dev : (target + 1) * tok_dev].astype(jnp.bfloat16)


def backward(second, slope, joint, keep, down, tok_dev):
    samples = second.shape[2]
    targets = slope.shape[0] // samples // tok_dev
    units, steps = (slope.shape[1], slope.shape[1] // 256)
    vmem_spec = pl.BlockSpec(memory_space=pltpu.VMEM)
    return pl.pallas_call(
        functools.partial(backward_kernel, steps),
        out_shape=(
            jax.ShapeDtypeStruct((targets, samples // 2, tok_dev, LANES), jnp.bfloat16),
            jax.ShapeDtypeStruct((2 * samples, down.shape[1]), jnp.bfloat16),
        ),
        in_specs=[vmem_spec] * 4 + [pl.BlockSpec(memory_space=pl.ANY)],
        out_specs=(vmem_spec,) * 2,
        scratch_shapes=[
            pltpu.VMEM((units - keep.shape[0], down.shape[1]), jnp.bfloat16),
            pltpu.SemaphoreType.DMA((steps - KEPT,)),
        ],
        compiler_params=pltpu.CompilerParams(vmem_limit_bytes=32 << 20),
        name="backward",
    )(second, slope, joint, keep, *in_hbm(down))


def per_device_fast(qkv, positions, w_proj, latents, embed_w, up_w, down_w, head_w, labels, timesteps):
    both = ("seq", "tp")
    n_seq, n_tp = (lax.axis_size("seq"), lax.axis_size("tp"))
    count = n_seq * n_tp
    seq_index = lax.axis_index("seq")
    half = seq_index % 2
    samples, tok_dev, width = qkv.shape[1:]
    seq_len = tok_dev * count
    lat = latents.shape[2]
    heads = width // HEAD_DIM
    per_sample = count // samples
    heads_dev = heads // per_sample
    rows_dev, classes = head_w.shape
    partner = [(i, i ^ n_tp) for i in range(count)]

    def in_order(own):
        other = lax.ppermute(own, both, partner)
        mine = jnp.broadcast_to(half == 0, own.shape)
        return jnp.stack([jnp.where(mine, own, other), jnp.where(mine, other, own)])

    other = lax.ppermute(latents, both, partner)
    head_pair = in_order(head_w).reshape(2 * rows_dev, classes)

    payload, slope, joint, keep, proj_mine = forward(
        qkv, positions, latents, other, embed_w, up_w, down_w, w_proj.T, n_seq, n_tp
    )
    moved = lax.all_to_all(payload, both, 0, 0, tiled=True)

    pooled = jnp.sum(moved[:, 0].astype(jnp.float32), axis=0)
    padded = -(-classes // 256) * 256
    terms = jnp.pad(split_dot(pooled, head_pair), ((0, 0), (0, padded - classes)))
    terms = lax.dynamic_slice_in_dim(terms, half * (padded // 2), padded // 2, 1)
    terms = jnp.broadcast_to(terms.astype(jnp.bfloat16)[None], (count,) + terms.shape)
    terms, moved = lax.optimization_barrier((terms, moved))
    terms = lax.all_to_all(terms, both, 0, 0, tiled=True)

    views = moved[:, 1:].reshape(count, 3, heads_dev, tok_dev, HEAD_DIM)
    views = views.transpose(1, 2, 0, 3, 4).reshape(3, heads_dev, seq_len, HEAD_DIM)
    scores = jnp.einsum(
        "hqd,hkd->hqk", views[0], views[1], preferred_element_type=jnp.float32
    ) * HEAD_DIM ** (-0.5)
    weights = jnp.exp(scores - jnp.max(scores, axis=-1, keepdims=True))
    total = jnp.sum(weights, axis=-1)
    mixed = jnp.einsum(
        "hqk,hkd->hqd", weights.astype(jnp.bfloat16), views[2], preferred_element_type=jnp.float32
    )
    attended = (mixed / total[..., None]).astype(jnp.bfloat16)
    eps_terms = jnp.einsum(
        "hqd,lhd->ql",
        attended,
        proj_mine.reshape(lat, heads_dev, HEAD_DIM),
        preferred_element_type=jnp.float32,
    )
    eps_terms = split_two(eps_terms, 1).reshape(count, 1, tok_dev, 2 * lat)

    terms = terms.astype(jnp.float32).reshape(n_seq // 2, 2, n_tp, samples, padded // 2)
    logits = jnp.sum(terms, axis=(0, 2))
    logits = logits.transpose(1, 0, 2).reshape(samples, padded)[:, :classes]
    probs = jax.nn.softmax(logits, axis=-1)
    onehot = (labels[:, None] == jnp.arange(classes, dtype=jnp.int32)[None, :]).astype(jnp.float32)
    share = split_two(split_dot(onehot - probs, head_w, 1), 1)
    share = jnp.broadcast_to(share[None, None], (count, 1) + share.shape)
    second = lax.all_to_all(
        jnp.concatenate([eps_terms, share], axis=1), both, 0, 0, tiled=True
    )
    eps = second[:, 0].astype(jnp.float32).reshape(samples, per_sample, tok_dev, 2 * lat)
    eps = jnp.sum(eps, axis=1)
    eps = eps[..., :lat] + eps[..., lat:]
    eps = lax.optimization_barrier(eps)
    dx_terms, dpool = backward(second, slope, joint, keep, down_w, tok_dev)
    planes = [[first + k for k in range(2 * n_tp)] for first in range(0, count, 2 * n_tp)]
    dx_terms = lax.all_to_all(dx_terms, both, 0, 0, tiled=True, axis_index_groups=planes)
    dx = jnp.sum(dx_terms.astype(jnp.float32), axis=0)
    dx = dx.reshape(samples // 2, tok_dev, 2, lat).transpose(0, 2, 1, 3)
    dx = dx.reshape(samples, tok_dev, lat)
    dx_pool = lax.dot_general(
        dpool, embed_w, (((1,), (1,)), ((), ())), preferred_element_type=jnp.float32
    )
    dx = dx + (dx_pool[:samples] + dx_pool[samples:])[:, None, :]
    phase = (timesteps.astype(jnp.float32) / 1000.0 + 0.008) / 1.008 * (jnp.pi / 2)
    abar = jnp.cos(phase) ** 2
    scale = GUIDANCE * jnp.sqrt(1.0 - abar)
    return (eps - scale[:, None, None] * dx).astype(jnp.bfloat16)


def per_device(qkv, positions, w_proj, latents, embed_w, up_w, down_w, head_w, labels, timesteps):
    args = (qkv, positions, w_proj, latents, embed_w, up_w, down_w, head_w, labels, timesteps)
    n_seq = lax.axis_size("seq")
    count = n_seq * lax.axis_size("tp")
    samples, heads = (qkv.shape[1], qkv.shape[3] // HEAD_DIM)
    tok_dev, tok_seq, lat = (qkv.shape[2], latents.shape[1], latents.shape[2])
    even = count % samples == 0 and heads % max(1, count // samples) == 0
    even = even and n_seq % 2 == 0 and count // n_seq % 2 == 0 and samples == 4 and tok_dev == 4
    even = even and lat == 64 and head_w.shape[0] == 64 and tok_seq % 16 == 0
    even = even and up_w.shape[1] % 512 == 0 and tok_seq == tok_dev * (count // n_seq)
    if even and count * head_w.shape[0] == up_w.shape[0]:
        return per_device_fast(*args)
    return per_device_general(*args)


def solution(mesh):
    placed = (
        P(None, None, ("seq", "tp"), None),
        P(None, None, ("seq", "tp")),
        P(),
        P(None, "seq", None),
        P(),
        P(None, "tp"),
        P("tp", None),
        P(("seq", "tp"), None),
        P(),
        P(),
    )
    return jax.shard_map(
        per_device,
        mesh=mesh,
        in_specs=placed,
        out_specs=P(None, ("seq", "tp"), None),
        check_vma=False,
    )
```

```python
import functools

import jax
import jax.numpy as jnp
import numpy as np
from jax import lax
from jax.experimental import pallas as pl
from jax.experimental.pallas import tpu as pltpu
from jax.sharding import PartitionSpec as P

HEAD_DIM = 128


GUIDANCE = 0.1


def rope_angles(positions, head_dim):
    frame_width = head_dim // 8
    plane_width = (head_dim - frame_width) // 2
    pieces = []
    for axis, width in zip(range(3), (frame_width, plane_width, plane_width)):
        freqs = 10000.0 ** (-jnp.arange(0, width, 2, dtype=jnp.float32) / width)
        pieces.append(positions[axis][..., None] * freqs)
    return jnp.concatenate(pieces, axis=-1)


def rotate(values, angles):
    half = values.shape[-1] // 2
    floats = values.astype(jnp.float32)
    first = floats[..., :half]
    second = floats[..., half:]
    cosine = jnp.cos(angles)[:, :, None, :]
    sine = jnp.sin(angles)[:, :, None, :]
    turned = jnp.concatenate(
        [first * cosine - second * sine, first * sine + second * cosine], axis=-1
    )
    return turned.astype(jnp.bfloat16)


def gelu_slope(values):
    cdf = 0.5 * (1.0 + jax.scipy.special.erf(values * 0.7071067811865476))
    pdf = jnp.exp(-0.5 * values * values) * 0.3989422804014327
    return cdf + values * pdf


def pairs_first(array):
    samples, tokens = (array.shape[0], array.shape[1])
    return array.transpose(0, 2, 1, 3).reshape(samples * array.shape[2], tokens, HEAD_DIM)


def per_device_general(qkv, positions, w_proj, latents, embed_w, up_w, down_w, head_w, labels, timesteps):
    samples, tok_dev = (qkv.shape[1], qkv.shape[2])
    angles = rope_angles(positions.astype(jnp.float32), HEAD_DIM)
    heads = qkv.shape[3] // HEAD_DIM
    shaped = (samples, tok_dev, heads, HEAD_DIM)
    queries = rotate(qkv[0].reshape(shaped), angles)
    keys_tok = rotate(qkv[1].reshape(shaped), angles)
    values_tok = qkv[2].reshape(shaped)
    moved = lax.all_to_all(
        jnp.stack([pairs_first(queries), pairs_first(keys_tok), pairs_first(values_tok)]),
        "seq",
        split_axis=1,
        concat_axis=2,
        tiled=True,
    )
    query_pairs = moved[0]
    pair_count, query_count = (query_pairs.shape[0], query_pairs.shape[1])
    running = jnp.full((pair_count, query_count), -jnp.inf, jnp.float32)
    total = jnp.zeros((pair_count, query_count), jnp.float32)
    accum = jnp.zeros((pair_count, query_count, HEAD_DIM), jnp.float32)
    key_piece = lax.all_gather(moved[1], "tp", axis=1, tiled=True)
    value_piece = lax.all_gather(moved[2], "tp", axis=1, tiled=True)
    scores = jnp.einsum(
        "iqd,ikd->iqk", query_pairs, key_piece, preferred_element_type=jnp.float32
    ) * HEAD_DIM ** (-0.5)
    newest = jnp.max(scores, axis=-1)
    factor = jnp.exp(running - newest)
    weights = jnp.exp(scores - newest[..., None])
    total = total * factor + jnp.sum(weights, axis=-1)
    accum = accum * factor[..., None] + jnp.einsum(
        "iqk,ikd->iqd",
        weights.astype(jnp.bfloat16),
        value_piece,
        preferred_element_type=jnp.float32,
    )
    running, total, accum = (newest, total, accum)
    attended = (accum / total[..., None]).astype(jnp.bfloat16)
    returned = lax.all_to_all(attended, "seq", split_axis=1, concat_axis=0, tiled=True)
    returned = returned.reshape(samples, heads, tok_dev, HEAD_DIM).transpose(0, 2, 1, 3)
    returned = returned.reshape(samples, tok_dev, qkv.shape[3])
    eps = jnp.dot(returned, w_proj, preferred_element_type=jnp.float32)
    seq_len = latents.shape[1] * lax.axis_size("seq")
    tp_index = lax.axis_index("tp")
    emb = jnp.dot(latents, embed_w, preferred_element_type=jnp.float32).astype(jnp.bfloat16)
    hidden = jnp.dot(emb, up_w, preferred_element_type=jnp.float32)
    act = jax.nn.gelu(hidden, approximate=False).astype(jnp.bfloat16)
    branch = jnp.dot(act, down_w, preferred_element_type=jnp.float32)
    own_emb = lax.dynamic_slice_in_dim(emb, tp_index * tok_dev, tok_dev, 1).astype(jnp.float32)
    partial_pool = jnp.sum(branch, axis=1) + jnp.sum(own_emb, axis=1)
    head_rows = head_w.shape[0]
    flat_index = lax.axis_index("seq") * lax.axis_size("tp") + tp_index
    pooled = lax.psum(partial_pool, ("seq", "tp")) / seq_len
    pooled_share = lax.dynamic_slice_in_dim(pooled, flat_index * head_rows, head_rows, 1)
    head_float = head_w.astype(jnp.float32)
    logit_terms = jnp.dot(pooled_share, head_float, precision=lax.Precision.HIGHEST)
    logits = lax.psum(logit_terms, ("seq", "tp"))
    probs = jax.nn.softmax(logits, axis=-1)
    onehot = (labels[:, None] == jnp.arange(logits.shape[1], dtype=jnp.int32)[None, :]).astype(
        jnp.float32
    )
    grad_share = jnp.dot(onehot - probs, head_float.T, precision=lax.Precision.HIGHEST)
    dpool = lax.all_gather(grad_share, ("seq", "tp"), axis=1, tiled=True)
    dact = jnp.dot(dpool, down_w.astype(jnp.float32).T, precision=lax.Precision.HIGHEST)
    dh1 = (gelu_slope(hidden) * dact[:, None, :]).astype(jnp.bfloat16)
    demb = jnp.einsum("btf,cf->btc", dh1, up_w, preferred_element_type=jnp.float32)
    embed_float = embed_w.astype(jnp.float32)
    dx_terms = jnp.einsum("btc,lc->btl", demb, embed_float, precision=lax.Precision.HIGHEST)
    dx_mine = lax.psum_scatter(
        dx_terms.astype(jnp.bfloat16), "tp", scatter_dimension=1, tiled=True
    ).astype(jnp.float32)
    dx_pool = jnp.dot(dpool, embed_float.T, precision=lax.Precision.HIGHEST)
    dx_total = dx_mine + dx_pool[:, None, :]
    phase = (timesteps.astype(jnp.float32) / 1000.0 + 0.008) / 1.008 * (jnp.pi / 2)
    abar = jnp.cos(phase) ** 2
    scale = GUIDANCE * jnp.sqrt(1.0 - abar)
    return (eps - scale[:, None, None] * dx_total).astype(jnp.bfloat16)


def rounded(values):
    return lax.reduce_precision(values, exponent_bits=8, mantissa_bits=7)


def split_rows(values):
    high = rounded(values)
    middle = rounded(values - high)
    low = values - high - middle
    return jnp.concatenate([high, middle, low], axis=0).astype(jnp.bfloat16)


def split_dot(values, weights, contract=0):
    rows = values.shape[0]
    product = lax.dot_general(
        split_rows(values),
        weights,
        (((1,), (contract,)), ((), ())),
        preferred_element_type=jnp.float32,
    )
    return product[:rows] + product[rows : 2 * rows] + product[2 * rows :]


def split_two(values, axis):
    high = rounded(values)
    return jnp.concatenate([high, values - high], axis=axis).astype(jnp.bfloat16)


LANES = 128


KEPT = 2


def in_hbm(*arrays):
    return [pltpu.with_memory_space_constraint(array, pltpu.HBM) for array in arrays]


def lane_frequencies():
    frame_width = HEAD_DIM // 8
    plane_width = (HEAD_DIM - frame_width) // 2
    freqs, axes = [], []
    for axis, width in zip(range(3), (frame_width, plane_width, plane_width)):
        steps = np.arange(0, width, 2, dtype=np.float32) / np.float32(width)
        freqs.append(np.float32(10000.0) ** (-steps))
        axes.append(np.full(width // 2, axis, np.float32))
    freqs, axes = (np.concatenate(freqs), np.concatenate(axes))
    table = np.stack([np.tile(freqs, 2), np.tile(axes, 2)]).astype(np.float32)
    return np.pad(table, ((0, 6), (0, 0)))


def forward_kernel(
    sizes,
    pos_hbm,
    table_hbm,
    qkv_hbm,
    own_hbm,
    other_hbm,
    embed_hbm,
    up_hbm,
    down_hbm,
    proj_hbm,
    pay_ref,
    slope_ref,
    joint_ref,
    keep_ref,
    proj_ref,
    pos_ref,
    table_ref,
    qkv_ref,
    lat_ref,
    embed_ref,
    up_ref,
    down_ref,
    rows_ref,
    sems,
):
    n_seq, n_tp, steps, seq_len = sizes
    samples, tok_dev, width = qkv_ref.shape[1:]
    count = n_seq * n_tp
    per_sample = count // samples
    heads_dev = width // HEAD_DIM // per_sample
    tok_seq, lat = own_hbm.shape[1:]
    units = slope_ref.shape[1]
    part = units // steps
    kept = keep_ref.shape[0] // part
    half = lax.axis_index("seq") % 2

    def up_copy(step):
        start = pl.multiple_of(half * units + step * part, LANES)
        return pltpu.make_async_copy(
            up_hbm.at[:, pl.ds(start, part)], up_ref.at[step], sems.at[6 + step]
        )

    def down_at(step):
        if step < kept:
            return keep_ref.at[pl.ds(step * part, part)]
        return down_ref.at[pl.ds((step - kept) * part, part)]

    def down_copy(step):
        start = pl.multiple_of(half * units + step * part, LANES)
        return pltpu.make_async_copy(
            down_hbm.at[pl.ds(start, part)],
            down_at(step),
            sems.at[6 + steps + step],
        )

    own_copy = pltpu.make_async_copy(own_hbm, lat_ref.at[half], sems.at[0])
    other_copy = pltpu.make_async_copy(other_hbm, lat_ref.at[1 - half], sems.at[1])
    embed_copy = pltpu.make_async_copy(embed_hbm, embed_ref, sems.at[2])
    qkv_copy = pltpu.make_async_copy(qkv_hbm, qkv_ref, sems.at[3])
    chunk = proj_ref.shape[1]
    flat = lax.axis_index("seq") * n_tp + lax.axis_index("tp")
    first_column = pl.multiple_of(lax.rem(flat, per_sample) * chunk, chunk)
    proj_copy = pltpu.make_async_copy(
        proj_hbm.at[:, pl.ds(first_column, chunk)], proj_ref, sems.at[6 + 2 * steps]
    )
    pos_copy = pltpu.make_async_copy(pos_hbm, pos_ref, sems.at[4])
    table_copy = pltpu.make_async_copy(table_hbm, table_ref, sems.at[5])
    for copy in (pos_copy, table_copy, own_copy, other_copy, qkv_copy, embed_copy):
        copy.start()
    for step in range(steps):
        up_copy(step).start()
    for step in range(steps):
        down_copy(step).start()
    proj_copy.start()

    pos_copy.wait()
    table_copy.wait()

    shape = (samples * tok_dev, LANES)
    row = lax.broadcasted_iota(jnp.int32, shape, 0)
    lane = lax.broadcasted_iota(jnp.int32, shape, 1)
    axis = jnp.broadcast_to(table_ref[1:2, :], shape)
    angles = jnp.zeros(shape, jnp.float32)
    for index in range(samples * tok_dev):
        sample, token = divmod(index, tok_dev)
        frame, line, column = (pos_ref[k, sample, token].astype(jnp.float32) for k in range(3))
        value = jnp.where(axis < 0.5, frame, jnp.where(axis < 1.5, line, column))
        angles = jnp.where(row == index, value, angles)
    angles = angles * jnp.broadcast_to(table_ref[0:1, :], shape)
    cosine = jnp.cos(angles)
    sine = jnp.sin(angles)
    sine = jnp.where(lane < HEAD_DIM // 2, -sine, sine)

    qkv_copy.wait()
    for sample in range(samples):
        cos_rows = cosine[sample * tok_dev : (sample + 1) * tok_dev]
        sin_rows = sine[sample * tok_dev : (sample + 1) * tok_dev]
        for head in range(width // HEAD_DIM):
            target = sample * per_sample + head // heads_dev
            span = slice(head * HEAD_DIM, (head + 1) * HEAD_DIM)
            for kind in range(3):
                group = 1 + kind * heads_dev + head % heads_dev
                values = qkv_ref[kind, sample, :, span]
                if kind < 2:
                    values = values.astype(jnp.float32)
                    values = values * cos_rows + pltpu.roll(values, HEAD_DIM // 2, 1) * sin_rows
                pay_ref[target, group] = values.astype(jnp.bfloat16)

    own_copy.wait()
    other_copy.wait()
    tok_pair = 2 * tok_seq
    sums = []
    for sample in range(samples):
        pieces = [lat_ref[0, sample], lat_ref[1, sample]]
        rows = jnp.concatenate(pieces, axis=0)
        rows_ref[sample * tok_pair : (sample + 1) * tok_pair] = jnp.concatenate([rows, rows], axis=1)
        sums.append(jnp.sum(rows.astype(jnp.float32), axis=0, keepdims=True))
    lat_sum = jnp.concatenate(sums, axis=0) * (1.0 / (2 * n_tp))
    lat_high = lat_sum.astype(jnp.bfloat16)
    lat_low = (lat_sum - lat_high.astype(jnp.float32)).astype(jnp.bfloat16)
    lat_rows = rows_ref[...]

    embed_copy.wait()
    embed = embed_ref[...]
    total = jnp.dot(
        jnp.concatenate([lat_high, lat_low], axis=0), embed, preferred_element_type=jnp.float32
    )
    parts = []
    for step in range(steps):
        up_copy(step).wait()
        joint = jnp.dot(embed, up_ref[step], preferred_element_type=jnp.float32)
        high = joint.astype(jnp.bfloat16)
        low = (joint - high.astype(jnp.float32)).astype(jnp.bfloat16)
        joint = jnp.concatenate([high, low], axis=0)
        span = slice(step * part, (step + 1) * part)
        joint_ref[:, span] = joint
        hidden = jnp.dot(lat_rows, joint, preferred_element_type=jnp.float32)
        cdf = 0.5 * (1.0 + lax.erf(hidden * 0.7071067811865476))
        pdf = jnp.exp(-0.5 * hidden * hidden) * 0.3989422804014327
        slope_ref[:, span] = (cdf + hidden * pdf).astype(jnp.bfloat16)
        act_sum = jnp.sum((hidden * cdf).reshape(samples, tok_pair, part), axis=1)
        high = act_sum.astype(jnp.bfloat16)
        low = (act_sum - high.astype(jnp.float32)).astype(jnp.bfloat16)
        parts.append(jnp.concatenate([high, low], axis=0))
    for step in range(steps):
        down_copy(step).wait()
        total = total + jnp.dot(
            parts[step],
            down_at(step)[...],
            preferred_element_type=jnp.float32,
        )
    proj_copy.wait()
    pool = (total[:samples] + total[samples:]) * (1.0 / seq_len)
    side = lax.broadcasted_iota(jnp.int32, (samples, LANES), 1) < LANES // 2
    for plane in range(n_seq // 2):
        for column in range(n_tp):
            first = (plane * 2 * n_tp + column) // 2
            second = (plane * 2 * n_tp + n_tp + column) // 2
            first = pool[:, first * LANES : (first + 1) * LANES]
            second = pool[:, second * LANES : (second + 1) * LANES]
            if column % 2 == 0:
                block = jnp.where(side, first, pltpu.roll(second, LANES // 2, 1))
            else:
                block = jnp.where(side, pltpu.roll(first, LANES // 2, 1), second)
            for core in range(2):
                target = (plane * 2 + core) * n_tp + column
                pay_ref[target, 0] = block.astype(jnp.bfloat16)


def forward(qkv, positions, own, other, embed_w, up_w, down_w, w_proj, n_seq, n_tp):
    samples, tok_dev, width = qkv.shape[1:]
    count = n_seq * n_tp
    groups = 1 + 3 * (width // HEAD_DIM // (count // samples))
    tok_seq, lat = own.shape[1:]
    units, features = (up_w.shape[1] // 2, up_w.shape[0])
    steps = units // 256
    rows = 2 * tok_seq * samples
    any_spec = pl.BlockSpec(memory_space=pl.ANY)
    vmem_spec = pl.BlockSpec(memory_space=pltpu.VMEM)
    return pl.pallas_call(
        functools.partial(forward_kernel, (n_seq, n_tp, steps, tok_dev * count)),
        out_shape=(
            jax.ShapeDtypeStruct((count, groups, tok_dev, LANES), jnp.bfloat16),
            jax.ShapeDtypeStruct((rows, units), jnp.bfloat16),
            jax.ShapeDtypeStruct((2 * lat, units), jnp.bfloat16),
            jax.ShapeDtypeStruct((KEPT * 256, features), jnp.bfloat16),
            jax.ShapeDtypeStruct((lat, width * samples // count), jnp.bfloat16),
        ),
        in_specs=[any_spec] * 9,
        out_specs=(vmem_spec,) * 5,
        scratch_shapes=[
            pltpu.SMEM(positions.shape, jnp.int32),
            pltpu.VMEM((8, LANES), jnp.float32),
            pltpu.VMEM(qkv.shape, jnp.bfloat16),
            pltpu.VMEM((2,) + own.shape, jnp.bfloat16),
            pltpu.VMEM(embed_w.shape, jnp.bfloat16),
            pltpu.VMEM((steps, features, 256), jnp.bfloat16),
            pltpu.VMEM((units - KEPT * 256, features), jnp.bfloat16),
            pltpu.VMEM((rows, 2 * lat), jnp.bfloat16),
            pltpu.SemaphoreType.DMA((7 + 2 * steps,)),
        ],
        compiler_params=pltpu.CompilerParams(vmem_limit_bytes=32 << 20),
        cost_estimate=pl.CostEstimate(
            flops=4 * features * units * 64, bytes_accessed=4 * features * units, transcendentals=0
        ),
        name="forward",
    )(*in_hbm(positions, jnp.asarray(lane_frequencies()), qkv, own), other, *in_hbm(embed_w, up_w, down_w, w_proj))


def backward_kernel(
    steps, second_ref, slope_ref, joint_ref, keep_ref, down_hbm, out_ref, dpool_ref, down_ref, sems
):
    count, groups, samples, _ = second_ref.shape
    units = slope_ref.shape[1]
    part = units // steps
    kept = keep_ref.shape[0] // part
    half = lax.axis_index("seq") % 2

    def down_copy(step):
        start = pl.multiple_of(half * units + step * part, LANES)
        return pltpu.make_async_copy(
            down_hbm.at[pl.ds(start, part)],
            down_ref.at[pl.ds((step - kept) * part, part)],
            sems.at[step - kept],
        )

    for step in range(kept, steps):
        down_copy(step).start()
    rows = slope_ref.shape[0] // samples
    side = lax.broadcasted_iota(jnp.int32, (samples, LANES), 1) < LANES // 2
    for pair in range(count // 2):
        first = second_ref[2 * pair, groups - 1].astype(jnp.float32)
        second = second_ref[2 * pair + 1, groups - 1].astype(jnp.float32)
        first = first + pltpu.roll(first, LANES // 2, 1)
        second = second + pltpu.roll(second, LANES // 2, 1)
        block = jnp.where(side, first, second)
        high = block.astype(jnp.bfloat16)
        low = (block - high.astype(jnp.float32)).astype(jnp.bfloat16)
        dpool_ref[:, pair * LANES : (pair + 1) * LANES] = jnp.concatenate([high, low], axis=0)
    dpool = dpool_ref[...]
    across = (((1,), (1,)), ((), ()))
    dx = None
    for step in range(steps):
        if step < kept:
            weights = keep_ref[step * part : (step + 1) * part]
        else:
            down_copy(step).wait()
            weights = down_ref[(step - kept) * part : (step - kept + 1) * part]
        dact = lax.dot_general(dpool, weights, across, preferred_element_type=jnp.float32)
        dact = dact[:samples] + dact[samples:]
        span = slice(step * part, (step + 1) * part)
        slope = slope_ref[:, span].astype(jnp.float32).reshape(samples, rows, part)
        dh1 = (slope * dact[:, None, :]).reshape(samples * rows, part).astype(jnp.bfloat16)
        term = lax.dot_general(dh1, joint_ref[:, span], across, preferred_element_type=jnp.float32)
        dx = term if dx is None else dx + term
    dx = dx + pltpu.roll(dx, LANES // 2, 1)
    side = lax.broadcasted_iota(jnp.int32, (rows, LANES), 1) < LANES // 2
    tok_dev = out_ref.shape[2]
    for pair in range(samples // 2):
        first = dx[2 * pair * rows : (2 * pair + 1) * rows]
        second = dx[(2 * pair + 1) * rows : (2 * pair + 2) * rows]
        both = jnp.where(side, first, second)
        for target in range(rows // tok_dev):
            out_ref[target, pair] = both[target * tok_dev : (target + 1) * tok_dev].astype(jnp.bfloat16)


def backward(second, slope, joint, keep, down, tok_dev):
    samples = second.shape[2]
    targets = slope.shape[0] // samples // tok_dev
    units, steps = (slope.shape[1], slope.shape[1] // 256)
    vmem_spec = pl.BlockSpec(memory_space=pltpu.VMEM)
    return pl.pallas_call(
        functools.partial(backward_kernel, steps),
        out_shape=(
            jax.ShapeDtypeStruct((targets, samples // 2, tok_dev, LANES), jnp.bfloat16),
            jax.ShapeDtypeStruct((2 * samples, down.shape[1]), jnp.bfloat16),
        ),
        in_specs=[vmem_spec] * 4 + [pl.BlockSpec(memory_space=pl.ANY)],
        out_specs=(vmem_spec,) * 2,
        scratch_shapes=[
            pltpu.VMEM((units - keep.shape[0], down.shape[1]), jnp.bfloat16),
            pltpu.SemaphoreType.DMA((steps - KEPT,)),
        ],
        compiler_params=pltpu.CompilerParams(vmem_limit_bytes=32 << 20),
        name="backward",
    )(second, slope, joint, keep, *in_hbm(down))


def pool_gradient_kernel(dpool_ref, embed_hbm, out_ref, embed_ref, sem):
    copy = pltpu.make_async_copy(embed_hbm, embed_ref, sem)
    copy.start()
    copy.wait()
    total = lax.dot_general(
        dpool_ref[...],
        embed_ref[...],
        (((1,), (1,)), ((), ())),
        preferred_element_type=jnp.float32,
    )
    half = total.shape[0] // 2
    out_ref[...] = total[:half] + total[half:]


def pool_gradient(dpool, embed_w):
    vmem_spec = pl.BlockSpec(memory_space=pltpu.VMEM)
    return pl.pallas_call(
        pool_gradient_kernel,
        out_shape=jax.ShapeDtypeStruct((dpool.shape[0] // 2, embed_w.shape[0]), jnp.float32),
        in_specs=[vmem_spec, pl.BlockSpec(memory_space=pl.ANY)],
        out_specs=vmem_spec,
        scratch_shapes=[pltpu.VMEM(embed_w.shape, jnp.bfloat16), pltpu.SemaphoreType.DMA],
        compiler_params=pltpu.CompilerParams(vmem_limit_bytes=32 << 20),
        cost_estimate=pl.CostEstimate(
            flops=2 * dpool.size * embed_w.shape[0],
            bytes_accessed=2 * embed_w.size,
            transcendentals=0,
        ),
        name="pool_gradient",
    )(dpool, *in_hbm(embed_w))


def per_device_fast(qkv, positions, w_proj, latents, embed_w, up_w, down_w, head_w, labels, timesteps):
    both = ("seq", "tp")
    n_seq, n_tp = (lax.axis_size("seq"), lax.axis_size("tp"))
    count = n_seq * n_tp
    seq_index = lax.axis_index("seq")
    half = seq_index % 2
    samples, tok_dev, width = qkv.shape[1:]
    seq_len = tok_dev * count
    lat = latents.shape[2]
    heads = width // HEAD_DIM
    per_sample = count // samples
    heads_dev = heads // per_sample
    rows_dev, classes = head_w.shape
    partner = [(i, i ^ n_tp) for i in range(count)]

    def in_order(own):
        other = lax.ppermute(own, both, partner)
        mine = jnp.broadcast_to(half == 0, own.shape)
        return jnp.stack([jnp.where(mine, own, other), jnp.where(mine, other, own)])

    other = lax.ppermute(latents, both, partner)
    head_pair = in_order(head_w).reshape(2 * rows_dev, classes)

    payload, slope, joint, keep, proj_mine = forward(
        qkv, positions, latents, other, embed_w, up_w, down_w, w_proj.T, n_seq, n_tp
    )
    moved = lax.all_to_all(payload, both, 0, 0, tiled=True)

    pooled = jnp.sum(moved[:, 0].astype(jnp.float32), axis=0)
    padded = -(-classes // 256) * 256
    terms = jnp.pad(split_dot(pooled, head_pair), ((0, 0), (0, padded - classes)))
    terms = lax.dynamic_slice_in_dim(terms, half * (padded // 2), padded // 2, 1)
    terms = jnp.broadcast_to(terms.astype(jnp.bfloat16)[None], (count,) + terms.shape)
    terms = lax.all_to_all(terms, both, 0, 0, tiled=True)

    views = moved[:, 1:].reshape(count, 3, heads_dev, tok_dev, HEAD_DIM)
    views = views.transpose(1, 2, 0, 3, 4).reshape(3, heads_dev, seq_len, HEAD_DIM)
    scores = jnp.einsum(
        "hqd,hkd->hqk", views[0], views[1], preferred_element_type=jnp.float32
    ) * HEAD_DIM ** (-0.5)
    weights = jnp.exp(scores - jnp.max(scores, axis=-1, keepdims=True))
    total = jnp.sum(weights, axis=-1)
    mixed = jnp.einsum(
        "hqk,hkd->hqd", weights.astype(jnp.bfloat16), views[2], preferred_element_type=jnp.float32
    )
    attended = (mixed / total[..., None]).astype(jnp.bfloat16)
    eps_terms = jnp.einsum(
        "hqd,lhd->ql",
        attended,
        proj_mine.reshape(lat, heads_dev, HEAD_DIM),
        preferred_element_type=jnp.float32,
    )
    eps_terms = split_two(eps_terms, 1).reshape(count, 1, tok_dev, 2 * lat)

    terms = terms.astype(jnp.float32).reshape(n_seq // 2, 2, n_tp, samples, padded // 2)
    logits = jnp.sum(terms, axis=(0, 2))
    logits = logits.transpose(1, 0, 2).reshape(samples, padded)[:, :classes]
    probs = jax.nn.softmax(logits, axis=-1)
    onehot = (labels[:, None] == jnp.arange(classes, dtype=jnp.int32)[None, :]).astype(jnp.float32)
    share = split_two(split_dot(onehot - probs, head_w, 1), 1)
    share = jnp.broadcast_to(share[None, None], (count, 1) + share.shape)
    second = lax.all_to_all(
        jnp.concatenate([eps_terms, share], axis=1), both, 0, 0, tiled=True
    )
    eps = second[:, 0].astype(jnp.float32).reshape(samples, per_sample, tok_dev, 2 * lat)
    eps = jnp.sum(eps, axis=1)
    eps = eps[..., :lat] + eps[..., lat:]
    eps = lax.optimization_barrier(eps)
    dx_terms, dpool = backward(second, slope, joint, keep, down_w, tok_dev)
    planes = [[first + k for k in range(2 * n_tp)] for first in range(0, count, 2 * n_tp)]
    dx_terms = lax.all_to_all(dx_terms, both, 0, 0, tiled=True, axis_index_groups=planes)
    dx = jnp.sum(dx_terms.astype(jnp.float32), axis=0)
    dx = dx.reshape(samples // 2, tok_dev, 2, lat).transpose(0, 2, 1, 3)
    dx = dx.reshape(samples, tok_dev, lat)
    dx = dx + pool_gradient(dpool, embed_w)[:, None, :]
    phase = (timesteps.astype(jnp.float32) / 1000.0 + 0.008) / 1.008 * (jnp.pi / 2)
    abar = jnp.cos(phase) ** 2
    scale = GUIDANCE * jnp.sqrt(1.0 - abar)
    return (eps - scale[:, None, None] * dx).astype(jnp.bfloat16)


def per_device(qkv, positions, w_proj, latents, embed_w, up_w, down_w, head_w, labels, timesteps):
    args = (qkv, positions, w_proj, latents, embed_w, up_w, down_w, head_w, labels, timesteps)
    n_seq = lax.axis_size("seq")
    count = n_seq * lax.axis_size("tp")
    samples, heads = (qkv.shape[1], qkv.shape[3] // HEAD_DIM)
    tok_dev, tok_seq, lat = (qkv.shape[2], latents.shape[1], latents.shape[2])
    even = count % samples == 0 and heads % max(1, count // samples) == 0
    even = even and n_seq % 2 == 0 and count // n_seq % 2 == 0 and samples == 4 and tok_dev == 4
    even = even and lat == 64 and head_w.shape[0] == 64 and tok_seq % 16 == 0
    even = even and up_w.shape[1] % 512 == 0 and tok_seq == tok_dev * (count // n_seq)
    if even and count * head_w.shape[0] == up_w.shape[0]:
        return per_device_fast(*args)
    return per_device_general(*args)


def solution(mesh):
    placed = (
        P(None, None, ("seq", "tp"), None),
        P(None, None, ("seq", "tp")),
        P(),
        P(None, "seq", None),
        P(),
        P(None, "tp"),
        P("tp", None),
        P(("seq", "tp"), None),
        P(),
        P(),
    )
    return jax.shard_map(
        per_device,
        mesh=mesh,
        in_specs=placed,
        out_specs=P(None, ("seq", "tp"), None),
        check_vma=False,
    )
```

```python
import functools

import jax
import jax.numpy as jnp
import numpy as np
from jax import lax
from jax.experimental import pallas as pl
from jax.experimental.pallas import tpu as pltpu
from jax.sharding import PartitionSpec as P

HEAD_DIM = 128


GUIDANCE = 0.1


def rope_angles(positions, head_dim):
    frame_width = head_dim // 8
    plane_width = (head_dim - frame_width) // 2
    pieces = []
    for axis, width in zip(range(3), (frame_width, plane_width, plane_width)):
        freqs = 10000.0 ** (-jnp.arange(0, width, 2, dtype=jnp.float32) / width)
        pieces.append(positions[axis][..., None] * freqs)
    return jnp.concatenate(pieces, axis=-1)


def rotate(values, angles):
    half = values.shape[-1] // 2
    floats = values.astype(jnp.float32)
    first = floats[..., :half]
    second = floats[..., half:]
    cosine = jnp.cos(angles)[:, :, None, :]
    sine = jnp.sin(angles)[:, :, None, :]
    turned = jnp.concatenate(
        [first * cosine - second * sine, first * sine + second * cosine], axis=-1
    )
    return turned.astype(jnp.bfloat16)


def gelu_slope(values):
    cdf = 0.5 * (1.0 + jax.scipy.special.erf(values * 0.7071067811865476))
    pdf = jnp.exp(-0.5 * values * values) * 0.3989422804014327
    return cdf + values * pdf


def pairs_first(array):
    samples, tokens = (array.shape[0], array.shape[1])
    return array.transpose(0, 2, 1, 3).reshape(samples * array.shape[2], tokens, HEAD_DIM)


def per_device_general(qkv, positions, w_proj, latents, embed_w, up_w, down_w, head_w, labels, timesteps):
    samples, tok_dev = (qkv.shape[1], qkv.shape[2])
    angles = rope_angles(positions.astype(jnp.float32), HEAD_DIM)
    heads = qkv.shape[3] // HEAD_DIM
    shaped = (samples, tok_dev, heads, HEAD_DIM)
    queries = rotate(qkv[0].reshape(shaped), angles)
    keys_tok = rotate(qkv[1].reshape(shaped), angles)
    values_tok = qkv[2].reshape(shaped)
    moved = lax.all_to_all(
        jnp.stack([pairs_first(queries), pairs_first(keys_tok), pairs_first(values_tok)]),
        "seq",
        split_axis=1,
        concat_axis=2,
        tiled=True,
    )
    query_pairs = moved[0]
    pair_count, query_count = (query_pairs.shape[0], query_pairs.shape[1])
    running = jnp.full((pair_count, query_count), -jnp.inf, jnp.float32)
    total = jnp.zeros((pair_count, query_count), jnp.float32)
    accum = jnp.zeros((pair_count, query_count, HEAD_DIM), jnp.float32)
    key_piece = lax.all_gather(moved[1], "tp", axis=1, tiled=True)
    value_piece = lax.all_gather(moved[2], "tp", axis=1, tiled=True)
    scores = jnp.einsum(
        "iqd,ikd->iqk", query_pairs, key_piece, preferred_element_type=jnp.float32
    ) * HEAD_DIM ** (-0.5)
    newest = jnp.max(scores, axis=-1)
    factor = jnp.exp(running - newest)
    weights = jnp.exp(scores - newest[..., None])
    total = total * factor + jnp.sum(weights, axis=-1)
    accum = accum * factor[..., None] + jnp.einsum(
        "iqk,ikd->iqd",
        weights.astype(jnp.bfloat16),
        value_piece,
        preferred_element_type=jnp.float32,
    )
    running, total, accum = (newest, total, accum)
    attended = (accum / total[..., None]).astype(jnp.bfloat16)
    returned = lax.all_to_all(attended, "seq", split_axis=1, concat_axis=0, tiled=True)
    returned = returned.reshape(samples, heads, tok_dev, HEAD_DIM).transpose(0, 2, 1, 3)
    returned = returned.reshape(samples, tok_dev, qkv.shape[3])
    eps = jnp.dot(returned, w_proj, preferred_element_type=jnp.float32)
    seq_len = latents.shape[1] * lax.axis_size("seq")
    tp_index = lax.axis_index("tp")
    emb = jnp.dot(latents, embed_w, preferred_element_type=jnp.float32).astype(jnp.bfloat16)
    hidden = jnp.dot(emb, up_w, preferred_element_type=jnp.float32)
    act = jax.nn.gelu(hidden, approximate=False).astype(jnp.bfloat16)
    branch = jnp.dot(act, down_w, preferred_element_type=jnp.float32)
    own_emb = lax.dynamic_slice_in_dim(emb, tp_index * tok_dev, tok_dev, 1).astype(jnp.float32)
    partial_pool = jnp.sum(branch, axis=1) + jnp.sum(own_emb, axis=1)
    head_rows = head_w.shape[0]
    flat_index = lax.axis_index("seq") * lax.axis_size("tp") + tp_index
    pooled = lax.psum(partial_pool, ("seq", "tp")) / seq_len
    pooled_share = lax.dynamic_slice_in_dim(pooled, flat_index * head_rows, head_rows, 1)
    head_float = head_w.astype(jnp.float32)
    logit_terms = jnp.dot(pooled_share, head_float, precision=lax.Precision.HIGHEST)
    logits = lax.psum(logit_terms, ("seq", "tp"))
    probs = jax.nn.softmax(logits, axis=-1)
    onehot = (labels[:, None] == jnp.arange(logits.shape[1], dtype=jnp.int32)[None, :]).astype(
        jnp.float32
    )
    grad_share = jnp.dot(onehot - probs, head_float.T, precision=lax.Precision.HIGHEST)
    dpool = lax.all_gather(grad_share, ("seq", "tp"), axis=1, tiled=True)
    dact = jnp.dot(dpool, down_w.astype(jnp.float32).T, precision=lax.Precision.HIGHEST)
    dh1 = (gelu_slope(hidden) * dact[:, None, :]).astype(jnp.bfloat16)
    demb = jnp.einsum("btf,cf->btc", dh1, up_w, preferred_element_type=jnp.float32)
    embed_float = embed_w.astype(jnp.float32)
    dx_terms = jnp.einsum("btc,lc->btl", demb, embed_float, precision=lax.Precision.HIGHEST)
    dx_mine = lax.psum_scatter(
        dx_terms.astype(jnp.bfloat16), "tp", scatter_dimension=1, tiled=True
    ).astype(jnp.float32)
    dx_pool = jnp.dot(dpool, embed_float.T, precision=lax.Precision.HIGHEST)
    dx_total = dx_mine + dx_pool[:, None, :]
    phase = (timesteps.astype(jnp.float32) / 1000.0 + 0.008) / 1.008 * (jnp.pi / 2)
    abar = jnp.cos(phase) ** 2
    scale = GUIDANCE * jnp.sqrt(1.0 - abar)
    return (eps - scale[:, None, None] * dx_total).astype(jnp.bfloat16)


def rounded(values):
    return lax.reduce_precision(values, exponent_bits=8, mantissa_bits=7)


def split_rows(values):
    high = rounded(values)
    middle = rounded(values - high)
    low = values - high - middle
    return jnp.concatenate([high, middle, low], axis=0).astype(jnp.bfloat16)


def split_dot(values, weights, contract=0):
    rows = values.shape[0]
    product = lax.dot_general(
        split_rows(values),
        weights,
        (((1,), (contract,)), ((), ())),
        preferred_element_type=jnp.float32,
    )
    return product[:rows] + product[rows : 2 * rows] + product[2 * rows :]


def split_two(values, axis):
    high = rounded(values)
    return jnp.concatenate([high, values - high], axis=axis).astype(jnp.bfloat16)


LANES = 128


KEPT = 2


def in_hbm(*arrays):
    return [pltpu.with_memory_space_constraint(array, pltpu.HBM) for array in arrays]


def lane_frequencies():
    frame_width = HEAD_DIM // 8
    plane_width = (HEAD_DIM - frame_width) // 2
    freqs, axes = [], []
    for axis, width in zip(range(3), (frame_width, plane_width, plane_width)):
        steps = np.arange(0, width, 2, dtype=np.float32) / np.float32(width)
        freqs.append(np.float32(10000.0) ** (-steps))
        axes.append(np.full(width // 2, axis, np.float32))
    freqs, axes = (np.concatenate(freqs), np.concatenate(axes))
    table = np.stack([np.tile(freqs, 2), np.tile(axes, 2)]).astype(np.float32)
    return np.pad(table, ((0, 6), (0, 0)))


def forward_kernel(
    sizes,
    pos_hbm,
    table_hbm,
    qkv_hbm,
    own_hbm,
    other_hbm,
    embed_hbm,
    up_hbm,
    down_hbm,
    proj_hbm,
    pay_ref,
    slope_ref,
    joint_ref,
    keep_ref,
    proj_ref,
    pos_ref,
    table_ref,
    qkv_ref,
    lat_ref,
    embed_ref,
    up_ref,
    down_ref,
    rows_ref,
    sems,
):
    n_seq, n_tp, steps, seq_len = sizes
    samples, tok_dev, width = qkv_ref.shape[1:]
    count = n_seq * n_tp
    per_sample = count // samples
    heads_dev = width // HEAD_DIM // per_sample
    tok_seq, lat = own_hbm.shape[1:]
    units = slope_ref.shape[1]
    part = units // steps
    kept = keep_ref.shape[0] // part
    half = lax.axis_index("seq") % 2

    def up_copy(step):
        start = pl.multiple_of(half * units + step * part, LANES)
        return pltpu.make_async_copy(
            up_hbm.at[:, pl.ds(start, part)], up_ref.at[step], sems.at[6 + step]
        )

    def down_at(step):
        if step < kept:
            return keep_ref.at[pl.ds(step * part, part)]
        return down_ref.at[pl.ds((step - kept) * part, part)]

    def down_copy(step):
        start = pl.multiple_of(half * units + step * part, LANES)
        return pltpu.make_async_copy(
            down_hbm.at[pl.ds(start, part)],
            down_at(step),
            sems.at[6 + steps + step],
        )

    own_copy = pltpu.make_async_copy(own_hbm, lat_ref.at[half], sems.at[0])
    other_copy = pltpu.make_async_copy(other_hbm, lat_ref.at[1 - half], sems.at[1])
    embed_copy = pltpu.make_async_copy(embed_hbm, embed_ref, sems.at[2])
    qkv_copy = pltpu.make_async_copy(qkv_hbm, qkv_ref, sems.at[3])
    chunk = proj_ref.shape[1]
    flat = lax.axis_index("seq") * n_tp + lax.axis_index("tp")
    first_column = pl.multiple_of(lax.rem(flat, per_sample) * chunk, chunk)
    proj_copy = pltpu.make_async_copy(
        proj_hbm.at[:, pl.ds(first_column, chunk)], proj_ref, sems.at[6 + 2 * steps]
    )
    pos_copy = pltpu.make_async_copy(pos_hbm, pos_ref, sems.at[4])
    table_copy = pltpu.make_async_copy(table_hbm, table_ref, sems.at[5])
    for copy in (pos_copy, table_copy, own_copy, other_copy, qkv_copy, embed_copy):
        copy.start()
    for step in range(steps):
        up_copy(step).start()
    for step in range(steps):
        down_copy(step).start()
    proj_copy.start()

    pos_copy.wait()
    table_copy.wait()

    shape = (samples * tok_dev, LANES)
    row = lax.broadcasted_iota(jnp.int32, shape, 0)
    lane = lax.broadcasted_iota(jnp.int32, shape, 1)
    axis = jnp.broadcast_to(table_ref[1:2, :], shape)
    angles = jnp.zeros(shape, jnp.float32)
    for index in range(samples * tok_dev):
        sample, token = divmod(index, tok_dev)
        frame, line, column = (pos_ref[k, sample, token].astype(jnp.float32) for k in range(3))
        value = jnp.where(axis < 0.5, frame, jnp.where(axis < 1.5, line, column))
        angles = jnp.where(row == index, value, angles)
    angles = angles * jnp.broadcast_to(table_ref[0:1, :], shape)
    cosine = jnp.cos(angles)
    sine = jnp.sin(angles)
    sine = jnp.where(lane < HEAD_DIM // 2, -sine, sine)

    def pack(sample):
        cos_rows = cosine[sample * tok_dev : (sample + 1) * tok_dev]
        sin_rows = sine[sample * tok_dev : (sample + 1) * tok_dev]
        for head in range(width // HEAD_DIM):
            target = sample * per_sample + head // heads_dev
            span = slice(head * HEAD_DIM, (head + 1) * HEAD_DIM)
            for kind in range(3):
                group = 1 + kind * heads_dev + head % heads_dev
                values = qkv_ref[kind, sample, :, span]
                if kind < 2:
                    values = values.astype(jnp.float32)
                    values = values * cos_rows + pltpu.roll(values, HEAD_DIM // 2, 1) * sin_rows
                pay_ref[target, group] = values.astype(jnp.bfloat16)

    qkv_copy.wait()
    own_copy.wait()
    other_copy.wait()
    tok_pair = 2 * tok_seq
    sums = []
    for sample in range(samples):
        pieces = [lat_ref[0, sample], lat_ref[1, sample]]
        rows = jnp.concatenate(pieces, axis=0)
        rows_ref[sample * tok_pair : (sample + 1) * tok_pair] = jnp.concatenate([rows, rows], axis=1)
        sums.append(jnp.sum(rows.astype(jnp.float32), axis=0, keepdims=True))
    lat_sum = jnp.concatenate(sums, axis=0) * (1.0 / (2 * n_tp))
    lat_high = lat_sum.astype(jnp.bfloat16)
    lat_low = (lat_sum - lat_high.astype(jnp.float32)).astype(jnp.bfloat16)
    lat_rows = rows_ref[...]

    embed_copy.wait()
    embed = embed_ref[...]
    total = jnp.dot(
        jnp.concatenate([lat_high, lat_low], axis=0), embed, preferred_element_type=jnp.float32
    )

    def activate(first, last):
        span = slice(first * part, last * part)
        hidden = jnp.dot(lat_rows, joint_ref[:, span], preferred_element_type=jnp.float32)
        cdf = 0.5 * (1.0 + lax.erf(hidden * 0.7071067811865476))
        pdf = jnp.exp(-0.5 * hidden * hidden) * 0.3989422804014327
        slope_ref[:, span] = (cdf + hidden * pdf).astype(jnp.bfloat16)
        act_sum = jnp.sum((hidden * cdf).reshape(samples, tok_pair, (last - first) * part), axis=1)
        high = act_sum.astype(jnp.bfloat16)
        low = (act_sum - high.astype(jnp.float32)).astype(jnp.bfloat16)
        return jnp.concatenate([high, low], axis=0)

    packed = 0
    for step in range(steps):
        up_copy(step).wait()
        joint = jnp.dot(embed, up_ref[step], preferred_element_type=jnp.float32)
        while packed * steps < samples * (step + 1):
            pack(packed)
            packed += 1
        if step == kept:
            acts = activate(0, kept)
        high = joint.astype(jnp.bfloat16)
        low = (joint - high.astype(jnp.float32)).astype(jnp.bfloat16)
        joint_ref[:, step * part : (step + 1) * part] = jnp.concatenate([high, low], axis=0)
    for step in range(kept):
        down_copy(step).wait()
    total = total + jnp.dot(acts, keep_ref[...], preferred_element_type=jnp.float32)
    acts = activate(kept, steps)
    for step in range(kept, steps):
        down_copy(step).wait()
    total = total + jnp.dot(acts, down_ref[...], preferred_element_type=jnp.float32)
    proj_copy.wait()
    pool = (total[:samples] + total[samples:]) * (1.0 / seq_len)
    side = lax.broadcasted_iota(jnp.int32, (samples, LANES), 1) < LANES // 2
    for plane in range(n_seq // 2):
        for column in range(n_tp):
            first = (plane * 2 * n_tp + column) // 2
            second = (plane * 2 * n_tp + n_tp + column) // 2
            first = pool[:, first * LANES : (first + 1) * LANES]
            second = pool[:, second * LANES : (second + 1) * LANES]
            if column % 2 == 0:
                block = jnp.where(side, first, pltpu.roll(second, LANES // 2, 1))
            else:
                block = jnp.where(side, pltpu.roll(first, LANES // 2, 1), second)
            for core in range(2):
                target = (plane * 2 + core) * n_tp + column
                pay_ref[target, 0] = block.astype(jnp.bfloat16)


def forward(qkv, positions, own, other, embed_w, up_w, down_w, w_proj, n_seq, n_tp):
    samples, tok_dev, width = qkv.shape[1:]
    count = n_seq * n_tp
    groups = 1 + 3 * (width // HEAD_DIM // (count // samples))
    tok_seq, lat = own.shape[1:]
    units, features = (up_w.shape[1] // 2, up_w.shape[0])
    steps = units // 256
    rows = 2 * tok_seq * samples
    any_spec = pl.BlockSpec(memory_space=pl.ANY)
    vmem_spec = pl.BlockSpec(memory_space=pltpu.VMEM)
    return pl.pallas_call(
        functools.partial(forward_kernel, (n_seq, n_tp, steps, tok_dev * count)),
        out_shape=(
            jax.ShapeDtypeStruct((count, groups, tok_dev, LANES), jnp.bfloat16),
            jax.ShapeDtypeStruct((rows, units), jnp.bfloat16),
            jax.ShapeDtypeStruct((2 * lat, units), jnp.bfloat16),
            jax.ShapeDtypeStruct((KEPT * 256, features), jnp.bfloat16),
            jax.ShapeDtypeStruct((lat, width * samples // count), jnp.bfloat16),
        ),
        in_specs=[any_spec] * 9,
        out_specs=(vmem_spec,) * 5,
        scratch_shapes=[
            pltpu.SMEM(positions.shape, jnp.int32),
            pltpu.VMEM((8, LANES), jnp.float32),
            pltpu.VMEM(qkv.shape, jnp.bfloat16),
            pltpu.VMEM((2,) + own.shape, jnp.bfloat16),
            pltpu.VMEM(embed_w.shape, jnp.bfloat16),
            pltpu.VMEM((steps, features, 256), jnp.bfloat16),
            pltpu.VMEM((units - KEPT * 256, features), jnp.bfloat16),
            pltpu.VMEM((rows, 2 * lat), jnp.bfloat16),
            pltpu.SemaphoreType.DMA((7 + 2 * steps,)),
        ],
        compiler_params=pltpu.CompilerParams(vmem_limit_bytes=32 << 20),
        cost_estimate=pl.CostEstimate(
            flops=4 * features * units * 64, bytes_accessed=4 * features * units, transcendentals=0
        ),
        name="forward",
    )(*in_hbm(positions, jnp.asarray(lane_frequencies()), qkv, own), other, *in_hbm(embed_w, up_w, down_w, w_proj))


def backward_kernel(
    steps, second_ref, slope_ref, joint_ref, keep_ref, down_hbm, out_ref, dpool_ref, down_ref, sems
):
    count, groups, samples, _ = second_ref.shape
    units = slope_ref.shape[1]
    part = units // steps
    kept = keep_ref.shape[0] // part
    half = lax.axis_index("seq") % 2

    def down_copy(step):
        start = pl.multiple_of(half * units + step * part, LANES)
        return pltpu.make_async_copy(
            down_hbm.at[pl.ds(start, part)],
            down_ref.at[pl.ds((step - kept) * part, part)],
            sems.at[step - kept],
        )

    for step in range(kept, steps):
        down_copy(step).start()
    rows = slope_ref.shape[0] // samples
    side = lax.broadcasted_iota(jnp.int32, (samples, LANES), 1) < LANES // 2
    for pair in range(count // 2):
        first = second_ref[2 * pair, groups - 1].astype(jnp.float32)
        second = second_ref[2 * pair + 1, groups - 1].astype(jnp.float32)
        first = first + pltpu.roll(first, LANES // 2, 1)
        second = second + pltpu.roll(second, LANES // 2, 1)
        block = jnp.where(side, first, second)
        high = block.astype(jnp.bfloat16)
        low = (block - high.astype(jnp.float32)).astype(jnp.bfloat16)
        dpool_ref[:, pair * LANES : (pair + 1) * LANES] = jnp.concatenate([high, low], axis=0)
    dpool = dpool_ref[...]
    across = (((1,), (1,)), ((), ()))

    def dx_part(weights, span):
        dact = lax.dot_general(dpool, weights, across, preferred_element_type=jnp.float32)
        dact = dact[:samples] + dact[samples:]
        size = span.stop - span.start
        slope = slope_ref[:, span].astype(jnp.float32).reshape(samples, rows, size)
        dh1 = (slope * dact[:, None, :]).reshape(samples * rows, size).astype(jnp.bfloat16)
        return lax.dot_general(dh1, joint_ref[:, span], across, preferred_element_type=jnp.float32)

    dx = dx_part(keep_ref[...], slice(0, kept * part))
    for step in range(kept, steps):
        down_copy(step).wait()
    dx = dx + dx_part(down_ref[...], slice(kept * part, steps * part))
    dx = dx + pltpu.roll(dx, LANES // 2, 1)
    side = lax.broadcasted_iota(jnp.int32, (rows, LANES), 1) < LANES // 2
    tok_dev = out_ref.shape[2]
    for pair in range(samples // 2):
        first = dx[2 * pair * rows : (2 * pair + 1) * rows]
        second = dx[(2 * pair + 1) * rows : (2 * pair + 2) * rows]
        both = jnp.where(side, first, second)
        for target in range(rows // tok_dev):
            out_ref[target, pair] = both[target * tok_dev : (target + 1) * tok_dev].astype(jnp.bfloat16)


def backward(second, slope, joint, keep, down, tok_dev):
    samples = second.shape[2]
    targets = slope.shape[0] // samples // tok_dev
    units, steps = (slope.shape[1], slope.shape[1] // 256)
    vmem_spec = pl.BlockSpec(memory_space=pltpu.VMEM)
    return pl.pallas_call(
        functools.partial(backward_kernel, steps),
        out_shape=(
            jax.ShapeDtypeStruct((targets, samples // 2, tok_dev, LANES), jnp.bfloat16),
            jax.ShapeDtypeStruct((2 * samples, down.shape[1]), jnp.bfloat16),
        ),
        in_specs=[vmem_spec] * 4 + [pl.BlockSpec(memory_space=pl.ANY)],
        out_specs=(vmem_spec,) * 2,
        scratch_shapes=[
            pltpu.VMEM((units - keep.shape[0], down.shape[1]), jnp.bfloat16),
            pltpu.SemaphoreType.DMA((steps - KEPT,)),
        ],
        compiler_params=pltpu.CompilerParams(vmem_limit_bytes=32 << 20),
        name="backward",
    )(second, slope, joint, keep, *in_hbm(down))


def pool_gradient_kernel(dpool_ref, embed_hbm, out_ref, embed_ref, sem):
    copy = pltpu.make_async_copy(embed_hbm, embed_ref, sem)
    copy.start()
    copy.wait()
    total = lax.dot_general(
        dpool_ref[...],
        embed_ref[...],
        (((1,), (1,)), ((), ())),
        preferred_element_type=jnp.float32,
    )
    half = total.shape[0] // 2
    out_ref[...] = total[:half] + total[half:]


def pool_gradient(dpool, embed_w):
    vmem_spec = pl.BlockSpec(memory_space=pltpu.VMEM)
    return pl.pallas_call(
        pool_gradient_kernel,
        out_shape=jax.ShapeDtypeStruct((dpool.shape[0] // 2, embed_w.shape[0]), jnp.float32),
        in_specs=[vmem_spec, pl.BlockSpec(memory_space=pl.ANY)],
        out_specs=vmem_spec,
        scratch_shapes=[pltpu.VMEM(embed_w.shape, jnp.bfloat16), pltpu.SemaphoreType.DMA],
        compiler_params=pltpu.CompilerParams(vmem_limit_bytes=32 << 20),
        cost_estimate=pl.CostEstimate(
            flops=2 * dpool.size * embed_w.shape[0],
            bytes_accessed=2 * embed_w.size,
            transcendentals=0,
        ),
        name="pool_gradient",
    )(dpool, *in_hbm(embed_w))


def per_device_fast(qkv, positions, w_proj, latents, embed_w, up_w, down_w, head_w, labels, timesteps):
    both = ("seq", "tp")
    n_seq, n_tp = (lax.axis_size("seq"), lax.axis_size("tp"))
    count = n_seq * n_tp
    seq_index = lax.axis_index("seq")
    half = seq_index % 2
    samples, tok_dev, width = qkv.shape[1:]
    seq_len = tok_dev * count
    lat = latents.shape[2]
    heads = width // HEAD_DIM
    per_sample = count // samples
    heads_dev = heads // per_sample
    rows_dev, classes = head_w.shape
    partner = [(i, i ^ n_tp) for i in range(count)]

    def in_order(own):
        other = lax.ppermute(own, both, partner)
        mine = jnp.broadcast_to(half == 0, own.shape)
        return jnp.stack([jnp.where(mine, own, other), jnp.where(mine, other, own)])

    other = lax.ppermute(latents, both, partner)
    head_pair = in_order(head_w).reshape(2 * rows_dev, classes)

    payload, slope, joint, keep, proj_mine = forward(
        qkv, positions, latents, other, embed_w, up_w, down_w, w_proj.T, n_seq, n_tp
    )
    moved = lax.all_to_all(payload, both, 0, 0, tiled=True)

    pooled = jnp.sum(moved[:, 0].astype(jnp.float32), axis=0)
    padded = -(-classes // 256) * 256
    terms = jnp.pad(split_dot(pooled, head_pair), ((0, 0), (0, padded - classes)))
    terms = lax.dynamic_slice_in_dim(terms, half * (padded // 2), padded // 2, 1)
    terms = jnp.broadcast_to(terms.astype(jnp.bfloat16)[None], (count,) + terms.shape)
    terms = lax.all_to_all(terms, both, 0, 0, tiled=True)

    views = moved[:, 1:].reshape(count, 3, heads_dev, tok_dev, HEAD_DIM)
    views = views.transpose(1, 2, 0, 3, 4).reshape(3, heads_dev, seq_len, HEAD_DIM)
    scores = jnp.einsum(
        "hqd,hkd->hqk", views[0], views[1], preferred_element_type=jnp.float32
    ) * HEAD_DIM ** (-0.5)
    weights = jnp.exp(scores - jnp.max(scores, axis=-1, keepdims=True))
    total = jnp.sum(weights, axis=-1)
    mixed = jnp.einsum(
        "hqk,hkd->hqd", weights.astype(jnp.bfloat16), views[2], preferred_element_type=jnp.float32
    )
    attended = (mixed / total[..., None]).astype(jnp.bfloat16)
    eps_terms = jnp.einsum(
        "hqd,lhd->ql",
        attended,
        proj_mine.reshape(lat, heads_dev, HEAD_DIM),
        preferred_element_type=jnp.float32,
    )
    eps_terms = split_two(eps_terms, 1).reshape(count, 1, tok_dev, 2 * lat)

    terms = terms.astype(jnp.float32).reshape(n_seq // 2, 2, n_tp, samples, padded // 2)
    logits = jnp.sum(terms, axis=(0, 2))
    logits = logits.transpose(1, 0, 2).reshape(samples, padded)[:, :classes]
    probs = jax.nn.softmax(logits, axis=-1)
    onehot = (labels[:, None] == jnp.arange(classes, dtype=jnp.int32)[None, :]).astype(jnp.float32)
    share = split_two(split_dot(onehot - probs, head_w, 1), 1)
    share = jnp.broadcast_to(share[None, None], (count, 1) + share.shape)
    second = lax.all_to_all(
        jnp.concatenate([eps_terms, share], axis=1), both, 0, 0, tiled=True
    )
    eps = second[:, 0].astype(jnp.float32).reshape(samples, per_sample, tok_dev, 2 * lat)
    eps = jnp.sum(eps, axis=1)
    eps = eps[..., :lat] + eps[..., lat:]
    eps = lax.optimization_barrier(eps)
    dx_terms, dpool = backward(second, slope, joint, keep, down_w, tok_dev)
    planes = [[first + k for k in range(2 * n_tp)] for first in range(0, count, 2 * n_tp)]
    dx_terms = lax.all_to_all(dx_terms, both, 0, 0, tiled=True, axis_index_groups=planes)
    dx = jnp.sum(dx_terms.astype(jnp.float32), axis=0)
    dx = dx.reshape(samples // 2, tok_dev, 2, lat).transpose(0, 2, 1, 3)
    dx = dx.reshape(samples, tok_dev, lat)
    dx = dx + pool_gradient(dpool, embed_w)[:, None, :]
    phase = (timesteps.astype(jnp.float32) / 1000.0 + 0.008) / 1.008 * (jnp.pi / 2)
    abar = jnp.cos(phase) ** 2
    scale = GUIDANCE * jnp.sqrt(1.0 - abar)
    return (eps - scale[:, None, None] * dx).astype(jnp.bfloat16)


def per_device(qkv, positions, w_proj, latents, embed_w, up_w, down_w, head_w, labels, timesteps):
    args = (qkv, positions, w_proj, latents, embed_w, up_w, down_w, head_w, labels, timesteps)
    n_seq = lax.axis_size("seq")
    count = n_seq * lax.axis_size("tp")
    samples, heads = (qkv.shape[1], qkv.shape[3] // HEAD_DIM)
    tok_dev, tok_seq, lat = (qkv.shape[2], latents.shape[1], latents.shape[2])
    even = count % samples == 0 and heads % max(1, count // samples) == 0
    even = even and n_seq % 2 == 0 and count // n_seq % 2 == 0 and samples == 4 and tok_dev == 4
    even = even and lat == 64 and head_w.shape[0] == 64 and tok_seq % 16 == 0
    even = even and up_w.shape[1] % 512 == 0 and tok_seq == tok_dev * (count // n_seq)
    if even and count * head_w.shape[0] == up_w.shape[0]:
        return per_device_fast(*args)
    return per_device_general(*args)


def solution(mesh):
    placed = (
        P(None, None, ("seq", "tp"), None),
        P(None, None, ("seq", "tp")),
        P(),
        P(None, "seq", None),
        P(),
        P(None, "tp"),
        P("tp", None),
        P(("seq", "tp"), None),
        P(),
        P(),
    )
    return jax.shard_map(
        per_device,
        mesh=mesh,
        in_specs=placed,
        out_specs=P(None, ("seq", "tp"), None),
        check_vma=False,
    )
```

```python
import functools

import jax
import jax.numpy as jnp
import numpy as np
from jax import lax
from jax.experimental import pallas as pl
from jax.experimental.pallas import tpu as pltpu
from jax.sharding import PartitionSpec as P

HEAD_DIM = 128


GUIDANCE = 0.1


def rope_angles(positions, head_dim):
    frame_width = head_dim // 8
    plane_width = (head_dim - frame_width) // 2
    pieces = []
    for axis, width in zip(range(3), (frame_width, plane_width, plane_width)):
        freqs = 10000.0 ** (-jnp.arange(0, width, 2, dtype=jnp.float32) / width)
        pieces.append(positions[axis][..., None] * freqs)
    return jnp.concatenate(pieces, axis=-1)


def rotate(values, angles):
    half = values.shape[-1] // 2
    floats = values.astype(jnp.float32)
    first = floats[..., :half]
    second = floats[..., half:]
    cosine = jnp.cos(angles)[:, :, None, :]
    sine = jnp.sin(angles)[:, :, None, :]
    turned = jnp.concatenate(
        [first * cosine - second * sine, first * sine + second * cosine], axis=-1
    )
    return turned.astype(jnp.bfloat16)


def gelu_slope(values):
    cdf = 0.5 * (1.0 + jax.scipy.special.erf(values * 0.7071067811865476))
    pdf = jnp.exp(-0.5 * values * values) * 0.3989422804014327
    return cdf + values * pdf


def pairs_first(array):
    samples, tokens = (array.shape[0], array.shape[1])
    return array.transpose(0, 2, 1, 3).reshape(samples * array.shape[2], tokens, HEAD_DIM)


def per_device_general(qkv, positions, w_proj, latents, embed_w, up_w, down_w, head_w, labels, timesteps):
    samples, tok_dev = (qkv.shape[1], qkv.shape[2])
    angles = rope_angles(positions.astype(jnp.float32), HEAD_DIM)
    heads = qkv.shape[3] // HEAD_DIM
    shaped = (samples, tok_dev, heads, HEAD_DIM)
    queries = rotate(qkv[0].reshape(shaped), angles)
    keys_tok = rotate(qkv[1].reshape(shaped), angles)
    values_tok = qkv[2].reshape(shaped)
    moved = lax.all_to_all(
        jnp.stack([pairs_first(queries), pairs_first(keys_tok), pairs_first(values_tok)]),
        "seq",
        split_axis=1,
        concat_axis=2,
        tiled=True,
    )
    query_pairs = moved[0]
    pair_count, query_count = (query_pairs.shape[0], query_pairs.shape[1])
    running = jnp.full((pair_count, query_count), -jnp.inf, jnp.float32)
    total = jnp.zeros((pair_count, query_count), jnp.float32)
    accum = jnp.zeros((pair_count, query_count, HEAD_DIM), jnp.float32)
    key_piece = lax.all_gather(moved[1], "tp", axis=1, tiled=True)
    value_piece = lax.all_gather(moved[2], "tp", axis=1, tiled=True)
    scores = jnp.einsum(
        "iqd,ikd->iqk", query_pairs, key_piece, preferred_element_type=jnp.float32
    ) * HEAD_DIM ** (-0.5)
    newest = jnp.max(scores, axis=-1)
    factor = jnp.exp(running - newest)
    weights = jnp.exp(scores - newest[..., None])
    total = total * factor + jnp.sum(weights, axis=-1)
    accum = accum * factor[..., None] + jnp.einsum(
        "iqk,ikd->iqd",
        weights.astype(jnp.bfloat16),
        value_piece,
        preferred_element_type=jnp.float32,
    )
    running, total, accum = (newest, total, accum)
    attended = (accum / total[..., None]).astype(jnp.bfloat16)
    returned = lax.all_to_all(attended, "seq", split_axis=1, concat_axis=0, tiled=True)
    returned = returned.reshape(samples, heads, tok_dev, HEAD_DIM).transpose(0, 2, 1, 3)
    returned = returned.reshape(samples, tok_dev, qkv.shape[3])
    eps = jnp.dot(returned, w_proj, preferred_element_type=jnp.float32)
    seq_len = latents.shape[1] * lax.axis_size("seq")
    tp_index = lax.axis_index("tp")
    emb = jnp.dot(latents, embed_w, preferred_element_type=jnp.float32).astype(jnp.bfloat16)
    hidden = jnp.dot(emb, up_w, preferred_element_type=jnp.float32)
    act = jax.nn.gelu(hidden, approximate=False).astype(jnp.bfloat16)
    branch = jnp.dot(act, down_w, preferred_element_type=jnp.float32)
    own_emb = lax.dynamic_slice_in_dim(emb, tp_index * tok_dev, tok_dev, 1).astype(jnp.float32)
    partial_pool = jnp.sum(branch, axis=1) + jnp.sum(own_emb, axis=1)
    head_rows = head_w.shape[0]
    flat_index = lax.axis_index("seq") * lax.axis_size("tp") + tp_index
    pooled = lax.psum(partial_pool, ("seq", "tp")) / seq_len
    pooled_share = lax.dynamic_slice_in_dim(pooled, flat_index * head_rows, head_rows, 1)
    head_float = head_w.astype(jnp.float32)
    logit_terms = jnp.dot(pooled_share, head_float, precision=lax.Precision.HIGHEST)
    logits = lax.psum(logit_terms, ("seq", "tp"))
    probs = jax.nn.softmax(logits, axis=-1)
    onehot = (labels[:, None] == jnp.arange(logits.shape[1], dtype=jnp.int32)[None, :]).astype(
        jnp.float32
    )
    grad_share = jnp.dot(onehot - probs, head_float.T, precision=lax.Precision.HIGHEST)
    dpool = lax.all_gather(grad_share, ("seq", "tp"), axis=1, tiled=True)
    dact = jnp.dot(dpool, down_w.astype(jnp.float32).T, precision=lax.Precision.HIGHEST)
    dh1 = (gelu_slope(hidden) * dact[:, None, :]).astype(jnp.bfloat16)
    demb = jnp.einsum("btf,cf->btc", dh1, up_w, preferred_element_type=jnp.float32)
    embed_float = embed_w.astype(jnp.float32)
    dx_terms = jnp.einsum("btc,lc->btl", demb, embed_float, precision=lax.Precision.HIGHEST)
    dx_mine = lax.psum_scatter(
        dx_terms.astype(jnp.bfloat16), "tp", scatter_dimension=1, tiled=True
    ).astype(jnp.float32)
    dx_pool = jnp.dot(dpool, embed_float.T, precision=lax.Precision.HIGHEST)
    dx_total = dx_mine + dx_pool[:, None, :]
    phase = (timesteps.astype(jnp.float32) / 1000.0 + 0.008) / 1.008 * (jnp.pi / 2)
    abar = jnp.cos(phase) ** 2
    scale = GUIDANCE * jnp.sqrt(1.0 - abar)
    return (eps - scale[:, None, None] * dx_total).astype(jnp.bfloat16)


def rounded(values):
    return lax.reduce_precision(values, exponent_bits=8, mantissa_bits=7)


def split_rows(values):
    high = rounded(values)
    middle = rounded(values - high)
    low = values - high - middle
    return jnp.concatenate([high, middle, low], axis=0).astype(jnp.bfloat16)


def split_dot(values, weights, contract=0):
    rows = values.shape[0]
    product = lax.dot_general(
        split_rows(values),
        weights,
        (((1,), (contract,)), ((), ())),
        preferred_element_type=jnp.float32,
    )
    return product[:rows] + product[rows : 2 * rows] + product[2 * rows :]


def split_two(values, axis):
    high = rounded(values)
    return jnp.concatenate([high, values - high], axis=axis).astype(jnp.bfloat16)


LANES = 128


KEPT = 2


def in_hbm(*arrays):
    return [pltpu.with_memory_space_constraint(array, pltpu.HBM) for array in arrays]


def lane_frequencies():
    frame_width = HEAD_DIM // 8
    plane_width = (HEAD_DIM - frame_width) // 2
    freqs, axes = [], []
    for axis, width in zip(range(3), (frame_width, plane_width, plane_width)):
        steps = np.arange(0, width, 2, dtype=np.float32) / np.float32(width)
        freqs.append(np.float32(10000.0) ** (-steps))
        axes.append(np.full(width // 2, axis, np.float32))
    freqs, axes = (np.concatenate(freqs), np.concatenate(axes))
    table = np.stack([np.tile(freqs, 2), np.tile(axes, 2)]).astype(np.float32)
    return np.pad(table, ((0, 6), (0, 0)))


def forward_kernel(
    sizes,
    pos_hbm,
    table_hbm,
    qkv_hbm,
    own_hbm,
    other_hbm,
    embed_hbm,
    up_hbm,
    down_hbm,
    proj_hbm,
    pay_ref,
    slope_ref,
    joint_ref,
    keep_ref,
    proj_ref,
    pos_ref,
    table_ref,
    qkv_ref,
    lat_ref,
    embed_ref,
    up_ref,
    down_ref,
    rows_ref,
    sems,
):
    n_seq, n_tp, steps, seq_len = sizes
    samples, tok_dev, width = qkv_ref.shape[1:]
    count = n_seq * n_tp
    per_sample = count // samples
    heads_dev = width // HEAD_DIM // per_sample
    tok_seq, lat = own_hbm.shape[1:]
    units = slope_ref.shape[1]
    part = units // steps
    kept = keep_ref.shape[0] // part
    half = lax.axis_index("seq") % 2

    def up_copy(step):
        start = pl.multiple_of(half * units + step * part, LANES)
        return pltpu.make_async_copy(
            up_hbm.at[:, pl.ds(start, part)], up_ref.at[step], sems.at[6 + step]
        )

    def down_at(step):
        if step < kept:
            return keep_ref.at[pl.ds(step * part, part)]
        return down_ref.at[pl.ds((step - kept) * part, part)]

    def down_copy(step):
        start = pl.multiple_of(half * units + step * part, LANES)
        return pltpu.make_async_copy(
            down_hbm.at[pl.ds(start, part)],
            down_at(step),
            sems.at[6 + steps + step],
        )

    own_copy = pltpu.make_async_copy(own_hbm, lat_ref.at[half], sems.at[0])
    other_copy = pltpu.make_async_copy(other_hbm, lat_ref.at[1 - half], sems.at[1])
    embed_copy = pltpu.make_async_copy(embed_hbm, embed_ref, sems.at[2])
    qkv_copy = pltpu.make_async_copy(qkv_hbm, qkv_ref, sems.at[3])
    chunk = proj_ref.shape[1]
    flat = lax.axis_index("seq") * n_tp + lax.axis_index("tp")
    first_column = pl.multiple_of(lax.rem(flat, per_sample) * chunk, chunk)
    proj_copy = pltpu.make_async_copy(
        proj_hbm.at[:, pl.ds(first_column, chunk)], proj_ref, sems.at[6 + 2 * steps]
    )
    pos_copy = pltpu.make_async_copy(pos_hbm, pos_ref, sems.at[4])
    table_copy = pltpu.make_async_copy(table_hbm, table_ref, sems.at[5])
    for copy in (pos_copy, table_copy, own_copy, other_copy, qkv_copy, embed_copy):
        copy.start()
    for step in range(steps):
        up_copy(step).start()
    for step in range(steps):
        down_copy(step).start()
    proj_copy.start()

    pos_copy.wait()
    table_copy.wait()

    shape = (samples * tok_dev, LANES)
    row = lax.broadcasted_iota(jnp.int32, shape, 0)
    lane = lax.broadcasted_iota(jnp.int32, shape, 1)
    axis = jnp.broadcast_to(table_ref[1:2, :], shape)
    angles = jnp.zeros(shape, jnp.float32)
    for index in range(samples * tok_dev):
        sample, token = divmod(index, tok_dev)
        frame, line, column = (pos_ref[k, sample, token].astype(jnp.float32) for k in range(3))
        value = jnp.where(axis < 0.5, frame, jnp.where(axis < 1.5, line, column))
        angles = jnp.where(row == index, value, angles)
    angles = angles * jnp.broadcast_to(table_ref[0:1, :], shape)
    cosine = jnp.cos(angles)
    sine = jnp.sin(angles)
    sine = jnp.where(lane < HEAD_DIM // 2, -sine, sine)

    def pack(sample):
        cos_rows = cosine[sample * tok_dev : (sample + 1) * tok_dev]
        sin_rows = sine[sample * tok_dev : (sample + 1) * tok_dev]
        for head in range(width // HEAD_DIM):
            target = sample * per_sample + head // heads_dev
            span = slice(head * HEAD_DIM, (head + 1) * HEAD_DIM)
            for kind in range(3):
                group = 1 + kind * heads_dev + head % heads_dev
                values = qkv_ref[kind, sample, :, span]
                if kind < 2:
                    values = values.astype(jnp.float32)
                    values = values * cos_rows + pltpu.roll(values, HEAD_DIM // 2, 1) * sin_rows
                pay_ref[target, group] = values.astype(jnp.bfloat16)

    qkv_copy.wait()
    own_copy.wait()
    other_copy.wait()
    tok_pair = 2 * tok_seq
    sums = []
    for sample in range(samples):
        pieces = [lat_ref[0, sample], lat_ref[1, sample]]
        rows = jnp.concatenate(pieces, axis=0)
        rows_ref[sample * tok_pair : (sample + 1) * tok_pair] = jnp.concatenate([rows, rows], axis=1)
        sums.append(jnp.sum(rows.astype(jnp.float32), axis=0, keepdims=True))
    lat_sum = jnp.concatenate(sums, axis=0) * (1.0 / (2 * n_tp))
    lat_high = lat_sum.astype(jnp.bfloat16)
    lat_low = (lat_sum - lat_high.astype(jnp.float32)).astype(jnp.bfloat16)
    lat_rows = rows_ref[...]

    embed_copy.wait()
    embed = embed_ref[...]
    total = jnp.dot(
        jnp.concatenate([lat_high, lat_low], axis=0), embed, preferred_element_type=jnp.float32
    )

    def activate(first, last):
        span = slice(first * part, last * part)
        hidden = jnp.dot(lat_rows, joint_ref[:, span], preferred_element_type=jnp.float32)
        cdf = 0.5 * (1.0 + lax.erf(hidden * 0.7071067811865476))
        pdf = jnp.exp(-0.5 * hidden * hidden) * 0.3989422804014327
        slope_ref[:, span] = (cdf + hidden * pdf).astype(jnp.bfloat16)
        act_sum = jnp.sum((hidden * cdf).reshape(samples, tok_pair, (last - first) * part), axis=1)
        high = act_sum.astype(jnp.bfloat16)
        low = (act_sum - high.astype(jnp.float32)).astype(jnp.bfloat16)
        return jnp.concatenate([high, low], axis=0)

    packed = 0
    for step in range(steps):
        up_copy(step).wait()
        joint = jnp.dot(embed, up_ref[step], preferred_element_type=jnp.float32)
        while packed * steps < samples * (step + 1):
            pack(packed)
            packed += 1
        if step == kept:
            acts = activate(0, kept)
        high = joint.astype(jnp.bfloat16)
        low = (joint - high.astype(jnp.float32)).astype(jnp.bfloat16)
        joint_ref[:, step * part : (step + 1) * part] = jnp.concatenate([high, low], axis=0)
    for step in range(kept):
        down_copy(step).wait()
    total = total + jnp.dot(acts, keep_ref[...], preferred_element_type=jnp.float32)
    acts = activate(kept, steps)
    for step in range(kept, steps):
        down_copy(step).wait()
    total = total + jnp.dot(acts, down_ref[...], preferred_element_type=jnp.float32)
    proj_copy.wait()
    pool = (total[:samples] + total[samples:]) * (1.0 / seq_len)
    side = lax.broadcasted_iota(jnp.int32, (samples, LANES), 1) < LANES // 2
    for plane in range(n_seq // 2):
        for column in range(n_tp):
            first = (plane * 2 * n_tp + column) // 2
            second = (plane * 2 * n_tp + n_tp + column) // 2
            first = pool[:, first * LANES : (first + 1) * LANES]
            second = pool[:, second * LANES : (second + 1) * LANES]
            if column % 2 == 0:
                block = jnp.where(side, first, pltpu.roll(second, LANES // 2, 1))
            else:
                block = jnp.where(side, pltpu.roll(first, LANES // 2, 1), second)
            for core in range(2):
                target = (plane * 2 + core) * n_tp + column
                pay_ref[target, 0] = block.astype(jnp.bfloat16)


def forward(qkv, positions, own, other, embed_w, up_w, down_w, w_proj, n_seq, n_tp):
    samples, tok_dev, width = qkv.shape[1:]
    count = n_seq * n_tp
    groups = 1 + 3 * (width // HEAD_DIM // (count // samples))
    tok_seq, lat = own.shape[1:]
    units, features = (up_w.shape[1] // 2, up_w.shape[0])
    steps = units // 256
    rows = 2 * tok_seq * samples
    any_spec = pl.BlockSpec(memory_space=pl.ANY)
    vmem_spec = pl.BlockSpec(memory_space=pltpu.VMEM)
    return pl.pallas_call(
        functools.partial(forward_kernel, (n_seq, n_tp, steps, tok_dev * count)),
        out_shape=(
            jax.ShapeDtypeStruct((count, groups, tok_dev, LANES), jnp.bfloat16),
            jax.ShapeDtypeStruct((rows, units), jnp.bfloat16),
            jax.ShapeDtypeStruct((2 * lat, units), jnp.bfloat16),
            jax.ShapeDtypeStruct((KEPT * 256, features), jnp.bfloat16),
            jax.ShapeDtypeStruct((lat, width * samples // count), jnp.bfloat16),
        ),
        in_specs=[any_spec] * 9,
        out_specs=(vmem_spec,) * 5,
        scratch_shapes=[
            pltpu.SMEM(positions.shape, jnp.int32),
            pltpu.VMEM((8, LANES), jnp.float32),
            pltpu.VMEM(qkv.shape, jnp.bfloat16),
            pltpu.VMEM((2,) + own.shape, jnp.bfloat16),
            pltpu.VMEM(embed_w.shape, jnp.bfloat16),
            pltpu.VMEM((steps, features, 256), jnp.bfloat16),
            pltpu.VMEM((units - KEPT * 256, features), jnp.bfloat16),
            pltpu.VMEM((rows, 2 * lat), jnp.bfloat16),
            pltpu.SemaphoreType.DMA((7 + 2 * steps,)),
        ],
        compiler_params=pltpu.CompilerParams(vmem_limit_bytes=32 << 20),
        cost_estimate=pl.CostEstimate(
            flops=4 * features * units * 64, bytes_accessed=4 * features * units, transcendentals=0
        ),
        name="forward",
    )(*in_hbm(positions, jnp.asarray(lane_frequencies()), qkv, own), other, *in_hbm(embed_w, up_w, down_w, w_proj))


def backward_kernel(
    steps, second_ref, slope_ref, joint_ref, keep_ref, down_hbm, out_ref, dpool_ref, down_ref, sems
):
    count, samples, _ = second_ref.shape
    units = slope_ref.shape[1]
    part = units // steps
    kept = keep_ref.shape[0] // part
    half = lax.axis_index("seq") % 2

    def down_copy(step):
        start = pl.multiple_of(half * units + step * part, LANES)
        return pltpu.make_async_copy(
            down_hbm.at[pl.ds(start, part)],
            down_ref.at[pl.ds((step - kept) * part, part)],
            sems.at[step - kept],
        )

    for step in range(kept, steps):
        down_copy(step).start()
    rows = slope_ref.shape[0] // samples
    side = lax.broadcasted_iota(jnp.int32, (samples, LANES), 1) < LANES // 2
    for pair in range(count // 2):
        first = second_ref[2 * pair].astype(jnp.float32)
        second = second_ref[2 * pair + 1].astype(jnp.float32)
        block = jnp.where(side, pltpu.roll(first, LANES // 2, 1), second)
        dpool_ref[:, pair * LANES : (pair + 1) * LANES] = block.astype(jnp.bfloat16)
    dpool = dpool_ref[...]
    across = (((1,), (1,)), ((), ()))

    def dx_part(weights, span):
        dact = lax.dot_general(dpool, weights, across, preferred_element_type=jnp.float32)
        size = span.stop - span.start
        slope = slope_ref[:, span].astype(jnp.float32).reshape(samples, rows, size)
        dh1 = (slope * dact[:, None, :]).reshape(samples * rows, size).astype(jnp.bfloat16)
        return lax.dot_general(dh1, joint_ref[:, span], across, preferred_element_type=jnp.float32)

    dx = dx_part(keep_ref[...], slice(0, kept * part))
    for step in range(kept, steps):
        down_copy(step).wait()
    dx = dx + dx_part(down_ref[...], slice(kept * part, steps * part))
    dx = dx + pltpu.roll(dx, LANES // 2, 1)
    side = lax.broadcasted_iota(jnp.int32, (rows, LANES), 1) < LANES // 2
    tok_dev = out_ref.shape[2]
    for pair in range(samples // 2):
        first = dx[2 * pair * rows : (2 * pair + 1) * rows]
        second = dx[(2 * pair + 1) * rows : (2 * pair + 2) * rows]
        both = jnp.where(side, first, second)
        for target in range(rows // tok_dev):
            out_ref[target, pair] = both[target * tok_dev : (target + 1) * tok_dev].astype(jnp.bfloat16)


def backward(second, slope, joint, keep, down, tok_dev):
    samples = second.shape[1]
    targets = slope.shape[0] // samples // tok_dev
    units, steps = (slope.shape[1], slope.shape[1] // 256)
    vmem_spec = pl.BlockSpec(memory_space=pltpu.VMEM)
    return pl.pallas_call(
        functools.partial(backward_kernel, steps),
        out_shape=(
            jax.ShapeDtypeStruct((targets, samples // 2, tok_dev, LANES), jnp.bfloat16),
            jax.ShapeDtypeStruct((samples, down.shape[1]), jnp.bfloat16),
        ),
        in_specs=[vmem_spec] * 4 + [pl.BlockSpec(memory_space=pl.ANY)],
        out_specs=(vmem_spec,) * 2,
        scratch_shapes=[
            pltpu.VMEM((units - keep.shape[0], down.shape[1]), jnp.bfloat16),
            pltpu.SemaphoreType.DMA((steps - KEPT,)),
        ],
        compiler_params=pltpu.CompilerParams(vmem_limit_bytes=32 << 20),
        name="backward",
    )(second, slope, joint, keep, *in_hbm(down))


def pool_gradient_kernel(dpool_ref, embed_hbm, out_ref, embed_ref, sem):
    copy = pltpu.make_async_copy(embed_hbm, embed_ref, sem)
    copy.start()
    copy.wait()
    out_ref[...] = lax.dot_general(
        dpool_ref[...],
        embed_ref[...],
        (((1,), (1,)), ((), ())),
        preferred_element_type=jnp.float32,
    )


def pool_gradient(dpool, embed_w):
    vmem_spec = pl.BlockSpec(memory_space=pltpu.VMEM)
    return pl.pallas_call(
        pool_gradient_kernel,
        out_shape=jax.ShapeDtypeStruct((dpool.shape[0], embed_w.shape[0]), jnp.float32),
        in_specs=[vmem_spec, pl.BlockSpec(memory_space=pl.ANY)],
        out_specs=vmem_spec,
        scratch_shapes=[pltpu.VMEM(embed_w.shape, jnp.bfloat16), pltpu.SemaphoreType.DMA],
        compiler_params=pltpu.CompilerParams(vmem_limit_bytes=32 << 20),
        cost_estimate=pl.CostEstimate(
            flops=2 * dpool.size * embed_w.shape[0],
            bytes_accessed=2 * embed_w.size,
            transcendentals=0,
        ),
        name="pool_gradient",
    )(dpool, *in_hbm(embed_w))


def per_device_fast(qkv, positions, w_proj, latents, embed_w, up_w, down_w, head_w, labels, timesteps):
    both = ("seq", "tp")
    n_seq, n_tp = (lax.axis_size("seq"), lax.axis_size("tp"))
    count = n_seq * n_tp
    seq_index = lax.axis_index("seq")
    half = seq_index % 2
    samples, tok_dev, width = qkv.shape[1:]
    seq_len = tok_dev * count
    lat = latents.shape[2]
    heads = width // HEAD_DIM
    per_sample = count // samples
    heads_dev = heads // per_sample
    rows_dev, classes = head_w.shape
    partner = [(i, i ^ n_tp) for i in range(count)]

    def in_order(own):
        other = lax.ppermute(own, both, partner)
        mine = jnp.broadcast_to(half == 0, own.shape)
        return jnp.stack([jnp.where(mine, own, other), jnp.where(mine, other, own)])

    other = lax.ppermute(latents, both, partner)
    head_pair = in_order(head_w).reshape(2 * rows_dev, classes)

    payload, slope, joint, keep, proj_mine = forward(
        qkv, positions, latents, other, embed_w, up_w, down_w, w_proj.T, n_seq, n_tp
    )
    moved = lax.all_to_all(payload, both, 0, 0, tiled=True)

    pooled = jnp.sum(moved[:, 0].astype(jnp.float32), axis=0)
    padded = -(-classes // 256) * 256
    terms = jnp.pad(split_dot(pooled, head_pair), ((0, 0), (0, padded - classes)))
    terms = lax.dynamic_slice_in_dim(terms, half * (padded // 2), padded // 2, 1)
    terms = jnp.broadcast_to(terms.astype(jnp.bfloat16)[None], (count,) + terms.shape)
    terms = lax.all_to_all(terms, both, 0, 0, tiled=True)

    views = moved[:, 1:].reshape(count, 3, heads_dev, tok_dev, HEAD_DIM)
    views = views.transpose(1, 2, 0, 3, 4).reshape(3, heads_dev, seq_len, HEAD_DIM)
    scores = jnp.einsum(
        "hqd,hkd->hqk", views[0], views[1], preferred_element_type=jnp.float32
    ) * HEAD_DIM ** (-0.5)
    weights = jnp.exp(scores - jnp.max(scores, axis=-1, keepdims=True))
    total = jnp.sum(weights, axis=-1)
    mixed = jnp.einsum(
        "hqk,hkd->hqd", weights.astype(jnp.bfloat16), views[2], preferred_element_type=jnp.float32
    )
    attended = (mixed / total[..., None]).astype(jnp.bfloat16)
    eps_terms = jnp.einsum(
        "hqd,lhd->ql",
        attended,
        proj_mine.reshape(lat, heads_dev, HEAD_DIM),
        preferred_element_type=jnp.float32,
    )
    eps_terms = eps_terms.reshape(count, tok_dev, lat)

    terms = terms.astype(jnp.float32).reshape(n_seq // 2, 2, n_tp, samples, padded // 2)
    logits = jnp.sum(terms, axis=(0, 2))
    logits = logits.transpose(1, 0, 2).reshape(samples, padded)[:, :classes]
    probs = jax.nn.softmax(logits, axis=-1)
    onehot = (labels[:, None] == jnp.arange(classes, dtype=jnp.int32)[None, :]).astype(jnp.float32)
    share = split_dot(onehot - probs, head_w, 1)
    share = jnp.broadcast_to(share[None], (count,) + share.shape)
    second = jnp.concatenate([eps_terms, share], axis=2).astype(jnp.bfloat16)
    second = lax.all_to_all(second, both, 0, 0, tiled=True)
    eps = second[..., :lat].astype(jnp.float32).reshape(samples, per_sample, tok_dev, lat)
    eps = jnp.sum(eps, axis=1)
    eps = lax.optimization_barrier(eps)
    dx_terms, dpool = backward(second, slope, joint, keep, down_w, tok_dev)
    planes = [[first + k for k in range(2 * n_tp)] for first in range(0, count, 2 * n_tp)]
    dx_terms = lax.all_to_all(dx_terms, both, 0, 0, tiled=True, axis_index_groups=planes)
    dx = jnp.sum(dx_terms.astype(jnp.float32), axis=0)
    dx = dx.reshape(samples // 2, tok_dev, 2, lat).transpose(0, 2, 1, 3)
    dx = dx.reshape(samples, tok_dev, lat)
    dx = dx + pool_gradient(dpool, embed_w)[:, None, :]
    phase = (timesteps.astype(jnp.float32) / 1000.0 + 0.008) / 1.008 * (jnp.pi / 2)
    abar = jnp.cos(phase) ** 2
    scale = GUIDANCE * jnp.sqrt(1.0 - abar)
    return (eps - scale[:, None, None] * dx).astype(jnp.bfloat16)


def per_device(qkv, positions, w_proj, latents, embed_w, up_w, down_w, head_w, labels, timesteps):
    args = (qkv, positions, w_proj, latents, embed_w, up_w, down_w, head_w, labels, timesteps)
    n_seq = lax.axis_size("seq")
    count = n_seq * lax.axis_size("tp")
    samples, heads = (qkv.shape[1], qkv.shape[3] // HEAD_DIM)
    tok_dev, tok_seq, lat = (qkv.shape[2], latents.shape[1], latents.shape[2])
    even = count % samples == 0 and heads % max(1, count // samples) == 0
    even = even and n_seq % 2 == 0 and count // n_seq % 2 == 0 and samples == 4 and tok_dev == 4
    even = even and lat == 64 and head_w.shape[0] == 64 and tok_seq % 16 == 0
    even = even and up_w.shape[1] % 512 == 0 and tok_seq == tok_dev * (count // n_seq)
    if even and count * head_w.shape[0] == up_w.shape[0]:
        return per_device_fast(*args)
    return per_device_general(*args)


def solution(mesh):
    placed = (
        P(None, None, ("seq", "tp"), None),
        P(None, None, ("seq", "tp")),
        P(),
        P(None, "seq", None),
        P(),
        P(None, "tp"),
        P("tp", None),
        P(("seq", "tp"), None),
        P(),
        P(),
    )
    return jax.shard_map(
        per_device,
        mesh=mesh,
        in_specs=placed,
        out_specs=P(None, ("seq", "tp"), None),
        check_vma=False,
    )
```

```python
import functools

import jax
import jax.numpy as jnp
import numpy as np
from jax import lax
from jax.experimental import pallas as pl
from jax.experimental.pallas import tpu as pltpu
from jax.sharding import PartitionSpec as P

HEAD_DIM = 128


GUIDANCE = 0.1


def rope_angles(positions, head_dim):
    frame_width = head_dim // 8
    plane_width = (head_dim - frame_width) // 2
    pieces = []
    for axis, width in zip(range(3), (frame_width, plane_width, plane_width)):
        freqs = 10000.0 ** (-jnp.arange(0, width, 2, dtype=jnp.float32) / width)
        pieces.append(positions[axis][..., None] * freqs)
    return jnp.concatenate(pieces, axis=-1)


def rotate(values, angles):
    half = values.shape[-1] // 2
    floats = values.astype(jnp.float32)
    first = floats[..., :half]
    second = floats[..., half:]
    cosine = jnp.cos(angles)[:, :, None, :]
    sine = jnp.sin(angles)[:, :, None, :]
    turned = jnp.concatenate(
        [first * cosine - second * sine, first * sine + second * cosine], axis=-1
    )
    return turned.astype(jnp.bfloat16)


def gelu_slope(values):
    cdf = 0.5 * (1.0 + jax.scipy.special.erf(values * 0.7071067811865476))
    pdf = jnp.exp(-0.5 * values * values) * 0.3989422804014327
    return cdf + values * pdf


def pairs_first(array):
    samples, tokens = (array.shape[0], array.shape[1])
    return array.transpose(0, 2, 1, 3).reshape(samples * array.shape[2], tokens, HEAD_DIM)


def per_device_general(qkv, positions, w_proj, latents, embed_w, up_w, down_w, head_w, labels, timesteps):
    samples, tok_dev = (qkv.shape[1], qkv.shape[2])
    angles = rope_angles(positions.astype(jnp.float32), HEAD_DIM)
    heads = qkv.shape[3] // HEAD_DIM
    shaped = (samples, tok_dev, heads, HEAD_DIM)
    queries = rotate(qkv[0].reshape(shaped), angles)
    keys_tok = rotate(qkv[1].reshape(shaped), angles)
    values_tok = qkv[2].reshape(shaped)
    moved = lax.all_to_all(
        jnp.stack([pairs_first(queries), pairs_first(keys_tok), pairs_first(values_tok)]),
        "seq",
        split_axis=1,
        concat_axis=2,
        tiled=True,
    )
    query_pairs = moved[0]
    pair_count, query_count = (query_pairs.shape[0], query_pairs.shape[1])
    running = jnp.full((pair_count, query_count), -jnp.inf, jnp.float32)
    total = jnp.zeros((pair_count, query_count), jnp.float32)
    accum = jnp.zeros((pair_count, query_count, HEAD_DIM), jnp.float32)
    key_piece = lax.all_gather(moved[1], "tp", axis=1, tiled=True)
    value_piece = lax.all_gather(moved[2], "tp", axis=1, tiled=True)
    scores = jnp.einsum(
        "iqd,ikd->iqk", query_pairs, key_piece, preferred_element_type=jnp.float32
    ) * HEAD_DIM ** (-0.5)
    newest = jnp.max(scores, axis=-1)
    factor = jnp.exp(running - newest)
    weights = jnp.exp(scores - newest[..., None])
    total = total * factor + jnp.sum(weights, axis=-1)
    accum = accum * factor[..., None] + jnp.einsum(
        "iqk,ikd->iqd",
        weights.astype(jnp.bfloat16),
        value_piece,
        preferred_element_type=jnp.float32,
    )
    running, total, accum = (newest, total, accum)
    attended = (accum / total[..., None]).astype(jnp.bfloat16)
    returned = lax.all_to_all(attended, "seq", split_axis=1, concat_axis=0, tiled=True)
    returned = returned.reshape(samples, heads, tok_dev, HEAD_DIM).transpose(0, 2, 1, 3)
    returned = returned.reshape(samples, tok_dev, qkv.shape[3])
    eps = jnp.dot(returned, w_proj, preferred_element_type=jnp.float32)
    seq_len = latents.shape[1] * lax.axis_size("seq")
    tp_index = lax.axis_index("tp")
    emb = jnp.dot(latents, embed_w, preferred_element_type=jnp.float32).astype(jnp.bfloat16)
    hidden = jnp.dot(emb, up_w, preferred_element_type=jnp.float32)
    act = jax.nn.gelu(hidden, approximate=False).astype(jnp.bfloat16)
    branch = jnp.dot(act, down_w, preferred_element_type=jnp.float32)
    own_emb = lax.dynamic_slice_in_dim(emb, tp_index * tok_dev, tok_dev, 1).astype(jnp.float32)
    partial_pool = jnp.sum(branch, axis=1) + jnp.sum(own_emb, axis=1)
    head_rows = head_w.shape[0]
    flat_index = lax.axis_index("seq") * lax.axis_size("tp") + tp_index
    pooled = lax.psum(partial_pool, ("seq", "tp")) / seq_len
    pooled_share = lax.dynamic_slice_in_dim(pooled, flat_index * head_rows, head_rows, 1)
    head_float = head_w.astype(jnp.float32)
    logit_terms = jnp.dot(pooled_share, head_float, precision=lax.Precision.HIGHEST)
    logits = lax.psum(logit_terms, ("seq", "tp"))
    probs = jax.nn.softmax(logits, axis=-1)
    onehot = (labels[:, None] == jnp.arange(logits.shape[1], dtype=jnp.int32)[None, :]).astype(
        jnp.float32
    )
    grad_share = jnp.dot(onehot - probs, head_float.T, precision=lax.Precision.HIGHEST)
    dpool = lax.all_gather(grad_share, ("seq", "tp"), axis=1, tiled=True)
    dact = jnp.dot(dpool, down_w.astype(jnp.float32).T, precision=lax.Precision.HIGHEST)
    dh1 = (gelu_slope(hidden) * dact[:, None, :]).astype(jnp.bfloat16)
    demb = jnp.einsum("btf,cf->btc", dh1, up_w, preferred_element_type=jnp.float32)
    embed_float = embed_w.astype(jnp.float32)
    dx_terms = jnp.einsum("btc,lc->btl", demb, embed_float, precision=lax.Precision.HIGHEST)
    dx_mine = lax.psum_scatter(
        dx_terms.astype(jnp.bfloat16), "tp", scatter_dimension=1, tiled=True
    ).astype(jnp.float32)
    dx_pool = jnp.dot(dpool, embed_float.T, precision=lax.Precision.HIGHEST)
    dx_total = dx_mine + dx_pool[:, None, :]
    phase = (timesteps.astype(jnp.float32) / 1000.0 + 0.008) / 1.008 * (jnp.pi / 2)
    abar = jnp.cos(phase) ** 2
    scale = GUIDANCE * jnp.sqrt(1.0 - abar)
    return (eps - scale[:, None, None] * dx_total).astype(jnp.bfloat16)


def rounded(values):
    return lax.reduce_precision(values, exponent_bits=8, mantissa_bits=7)


def split_rows(values):
    high = rounded(values)
    return jnp.concatenate([high, values - high], axis=0).astype(jnp.bfloat16)


def split_dot(values, weights, contract=0):
    rows = values.shape[0]
    product = lax.dot_general(
        split_rows(values),
        weights,
        (((1,), (contract,)), ((), ())),
        preferred_element_type=jnp.float32,
    )
    return product[:rows] + product[rows:]


def split_two(values, axis):
    high = rounded(values)
    return jnp.concatenate([high, values - high], axis=axis).astype(jnp.bfloat16)


LANES = 128


KEPT = 2


def in_hbm(*arrays):
    return [pltpu.with_memory_space_constraint(array, pltpu.HBM) for array in arrays]


def lane_frequencies():
    frame_width = HEAD_DIM // 8
    plane_width = (HEAD_DIM - frame_width) // 2
    freqs, axes = [], []
    for axis, width in zip(range(3), (frame_width, plane_width, plane_width)):
        steps = np.arange(0, width, 2, dtype=np.float32) / np.float32(width)
        freqs.append(np.float32(10000.0) ** (-steps))
        axes.append(np.full(width // 2, axis, np.float32))
    freqs, axes = (np.concatenate(freqs), np.concatenate(axes))
    table = np.stack([np.tile(freqs, 2), np.tile(axes, 2)]).astype(np.float32)
    return np.pad(table, ((0, 6), (0, 0)))


def forward_kernel(
    sizes,
    pos_hbm,
    table_hbm,
    qkv_hbm,
    own_hbm,
    other_hbm,
    embed_hbm,
    up_hbm,
    down_hbm,
    proj_hbm,
    pay_ref,
    slope_ref,
    joint_ref,
    keep_ref,
    proj_ref,
    pos_ref,
    table_ref,
    qkv_ref,
    lat_ref,
    embed_ref,
    up_ref,
    down_ref,
    rows_ref,
    sems,
):
    n_seq, n_tp, steps, seq_len = sizes
    samples, tok_dev, width = qkv_ref.shape[1:]
    count = n_seq * n_tp
    per_sample = count // samples
    heads_dev = width // HEAD_DIM // per_sample
    tok_seq, lat = own_hbm.shape[1:]
    units = slope_ref.shape[1]
    part = units // steps
    kept = keep_ref.shape[0] // part
    half = lax.axis_index("seq") % 2

    def up_copy(step):
        start = pl.multiple_of(half * units + step * part, LANES)
        return pltpu.make_async_copy(
            up_hbm.at[:, pl.ds(start, part)], up_ref.at[step], sems.at[6 + step]
        )

    def down_at(step):
        if step < kept:
            return keep_ref.at[pl.ds(step * part, part)]
        return down_ref.at[pl.ds((step - kept) * part, part)]

    def down_copy(step):
        start = pl.multiple_of(half * units + step * part, LANES)
        return pltpu.make_async_copy(
            down_hbm.at[pl.ds(start, part)],
            down_at(step),
            sems.at[6 + steps + step],
        )

    own_copy = pltpu.make_async_copy(own_hbm, lat_ref.at[half], sems.at[0])
    other_copy = pltpu.make_async_copy(other_hbm, lat_ref.at[1 - half], sems.at[1])
    embed_copy = pltpu.make_async_copy(embed_hbm, embed_ref, sems.at[2])
    qkv_copy = pltpu.make_async_copy(qkv_hbm, qkv_ref, sems.at[3])
    chunk = proj_ref.shape[1]
    flat = lax.axis_index("seq") * n_tp + lax.axis_index("tp")
    first_column = pl.multiple_of(lax.rem(flat, per_sample) * chunk, chunk)
    proj_copy = pltpu.make_async_copy(
        proj_hbm.at[:, pl.ds(first_column, chunk)], proj_ref, sems.at[6 + 2 * steps]
    )
    pos_copy = pltpu.make_async_copy(pos_hbm, pos_ref, sems.at[4])
    table_copy = pltpu.make_async_copy(table_hbm, table_ref, sems.at[5])
    for copy in (pos_copy, table_copy, own_copy, other_copy, qkv_copy, embed_copy):
        copy.start()
    for step in range(steps):
        up_copy(step).start()
    for step in range(steps):
        down_copy(step).start()
    proj_copy.start()

    pos_copy.wait()
    table_copy.wait()

    shape = (samples * tok_dev, LANES)
    row = lax.broadcasted_iota(jnp.int32, shape, 0)
    lane = lax.broadcasted_iota(jnp.int32, shape, 1)
    axis = jnp.broadcast_to(table_ref[1:2, :], shape)
    angles = jnp.zeros(shape, jnp.float32)
    for index in range(samples * tok_dev):
        sample, token = divmod(index, tok_dev)
        frame, line, column = (pos_ref[k, sample, token].astype(jnp.float32) for k in range(3))
        value = jnp.where(axis < 0.5, frame, jnp.where(axis < 1.5, line, column))
        angles = jnp.where(row == index, value, angles)
    angles = angles * jnp.broadcast_to(table_ref[0:1, :], shape)
    cosine = jnp.cos(angles)
    sine = jnp.sin(angles)
    sine = jnp.where(lane < HEAD_DIM // 2, -sine, sine)

    def pack(sample):
        cos_rows = cosine[sample * tok_dev : (sample + 1) * tok_dev]
        sin_rows = sine[sample * tok_dev : (sample + 1) * tok_dev]
        for head in range(width // HEAD_DIM):
            target = sample * per_sample + head // heads_dev
            span = slice(head * HEAD_DIM, (head + 1) * HEAD_DIM)
            for kind in range(3):
                group = 1 + kind * heads_dev + head % heads_dev
                values = qkv_ref[kind, sample, :, span]
                if kind < 2:
                    values = values.astype(jnp.float32)
                    values = values * cos_rows + pltpu.roll(values, HEAD_DIM // 2, 1) * sin_rows
                pay_ref[target, group] = values.astype(jnp.bfloat16)

    qkv_copy.wait()
    own_copy.wait()
    other_copy.wait()
    tok_pair = 2 * tok_seq
    sums = []
    for sample in range(samples):
        pieces = [lat_ref[0, sample], lat_ref[1, sample]]
        rows = jnp.concatenate(pieces, axis=0)
        rows_ref[sample * tok_pair : (sample + 1) * tok_pair] = jnp.concatenate([rows, rows], axis=1)
        sums.append(jnp.sum(rows.astype(jnp.float32), axis=0, keepdims=True))
    lat_sum = jnp.concatenate(sums, axis=0) * (1.0 / (2 * n_tp))
    lat_high = lat_sum.astype(jnp.bfloat16)
    lat_low = (lat_sum - lat_high.astype(jnp.float32)).astype(jnp.bfloat16)
    lat_rows = rows_ref[...]

    embed_copy.wait()
    embed = embed_ref[...]
    total = jnp.dot(
        jnp.concatenate([lat_high, lat_low], axis=0), embed, preferred_element_type=jnp.float32
    )

    def activate(first, last):
        span = slice(first * part, last * part)
        hidden = jnp.dot(lat_rows, joint_ref[:, span], preferred_element_type=jnp.float32)
        cdf = 0.5 * (1.0 + lax.erf(hidden * 0.7071067811865476))
        pdf = jnp.exp(-0.5 * hidden * hidden) * 0.3989422804014327
        slope_ref[:, span] = (cdf + hidden * pdf).astype(jnp.bfloat16)
        act_sum = jnp.sum((hidden * cdf).reshape(samples, tok_pair, (last - first) * part), axis=1)
        high = act_sum.astype(jnp.bfloat16)
        low = (act_sum - high.astype(jnp.float32)).astype(jnp.bfloat16)
        return jnp.concatenate([high, low], axis=0)

    packed = 0
    for step in range(steps):
        up_copy(step).wait()
        joint = jnp.dot(embed, up_ref[step], preferred_element_type=jnp.float32)
        while packed * steps < samples * (step + 1):
            pack(packed)
            packed += 1
        if step == kept:
            acts = activate(0, kept)
        high = joint.astype(jnp.bfloat16)
        low = (joint - high.astype(jnp.float32)).astype(jnp.bfloat16)
        joint_ref[:, step * part : (step + 1) * part] = jnp.concatenate([high, low], axis=0)
    for step in range(kept):
        down_copy(step).wait()
    total = total + jnp.dot(acts, keep_ref[...], preferred_element_type=jnp.float32)
    acts = activate(kept, steps)
    for step in range(kept, steps):
        down_copy(step).wait()
    total = total + jnp.dot(acts, down_ref[...], preferred_element_type=jnp.float32)
    proj_copy.wait()
    pool = (total[:samples] + total[samples:]) * (1.0 / seq_len)
    side = lax.broadcasted_iota(jnp.int32, (samples, LANES), 1) < LANES // 2
    for plane in range(n_seq // 2):
        for column in range(n_tp):
            first = (plane * 2 * n_tp + column) // 2
            second = (plane * 2 * n_tp + n_tp + column) // 2
            first = pool[:, first * LANES : (first + 1) * LANES]
            second = pool[:, second * LANES : (second + 1) * LANES]
            if column % 2 == 0:
                block = jnp.where(side, first, pltpu.roll(second, LANES // 2, 1))
            else:
                block = jnp.where(side, pltpu.roll(first, LANES // 2, 1), second)
            for core in range(2):
                target = (plane * 2 + core) * n_tp + column
                pay_ref[target, 0] = block.astype(jnp.bfloat16)


def forward(qkv, positions, own, other, embed_w, up_w, down_w, w_proj, n_seq, n_tp):
    samples, tok_dev, width = qkv.shape[1:]
    count = n_seq * n_tp
    groups = 1 + 3 * (width // HEAD_DIM // (count // samples))
    tok_seq, lat = own.shape[1:]
    units, features = (up_w.shape[1] // 2, up_w.shape[0])
    steps = units // 256
    rows = 2 * tok_seq * samples
    any_spec = pl.BlockSpec(memory_space=pl.ANY)
    vmem_spec = pl.BlockSpec(memory_space=pltpu.VMEM)
    return pl.pallas_call(
        functools.partial(forward_kernel, (n_seq, n_tp, steps, tok_dev * count)),
        out_shape=(
            jax.ShapeDtypeStruct((count, groups, tok_dev, LANES), jnp.bfloat16),
            jax.ShapeDtypeStruct((rows, units), jnp.bfloat16),
            jax.ShapeDtypeStruct((2 * lat, units), jnp.bfloat16),
            jax.ShapeDtypeStruct((KEPT * 256, features), jnp.bfloat16),
            jax.ShapeDtypeStruct((lat, width * samples // count), jnp.bfloat16),
        ),
        in_specs=[any_spec] * 9,
        out_specs=(vmem_spec,) * 5,
        scratch_shapes=[
            pltpu.SMEM(positions.shape, jnp.int32),
            pltpu.VMEM((8, LANES), jnp.float32),
            pltpu.VMEM(qkv.shape, jnp.bfloat16),
            pltpu.VMEM((2,) + own.shape, jnp.bfloat16),
            pltpu.VMEM(embed_w.shape, jnp.bfloat16),
            pltpu.VMEM((steps, features, 256), jnp.bfloat16),
            pltpu.VMEM((units - KEPT * 256, features), jnp.bfloat16),
            pltpu.VMEM((rows, 2 * lat), jnp.bfloat16),
            pltpu.SemaphoreType.DMA((7 + 2 * steps,)),
        ],
        compiler_params=pltpu.CompilerParams(vmem_limit_bytes=32 << 20),
        cost_estimate=pl.CostEstimate(
            flops=4 * features * units * 64, bytes_accessed=4 * features * units, transcendentals=0
        ),
        name="forward",
    )(*in_hbm(positions, jnp.asarray(lane_frequencies()), qkv, own), other, *in_hbm(embed_w, up_w, down_w, w_proj))


def backward_kernel(
    steps, second_ref, slope_ref, joint_ref, keep_ref, down_hbm, out_ref, dpool_ref, down_ref, sems
):
    count, samples, _ = second_ref.shape
    units = slope_ref.shape[1]
    part = units // steps
    kept = keep_ref.shape[0] // part
    half = lax.axis_index("seq") % 2

    def down_copy(step):
        start = pl.multiple_of(half * units + step * part, LANES)
        return pltpu.make_async_copy(
            down_hbm.at[pl.ds(start, part)],
            down_ref.at[pl.ds((step - kept) * part, part)],
            sems.at[step - kept],
        )

    for step in range(kept, steps):
        down_copy(step).start()
    rows = slope_ref.shape[0] // samples
    side = lax.broadcasted_iota(jnp.int32, (samples, LANES), 1) < LANES // 2
    for pair in range(count // 2):
        first = second_ref[2 * pair].astype(jnp.float32)
        second = second_ref[2 * pair + 1].astype(jnp.float32)
        block = jnp.where(side, pltpu.roll(first, LANES // 2, 1), second)
        dpool_ref[:, pair * LANES : (pair + 1) * LANES] = block.astype(jnp.bfloat16)
    dpool = dpool_ref[...]
    across = (((1,), (1,)), ((), ()))

    def dx_part(weights, span):
        dact = lax.dot_general(dpool, weights, across, preferred_element_type=jnp.float32)
        size = span.stop - span.start
        slope = slope_ref[:, span].astype(jnp.float32).reshape(samples, rows, size)
        dh1 = (slope * dact[:, None, :]).reshape(samples * rows, size).astype(jnp.bfloat16)
        return lax.dot_general(dh1, joint_ref[:, span], across, preferred_element_type=jnp.float32)

    dx = dx_part(keep_ref[...], slice(0, kept * part))
    for step in range(kept, steps):
        down_copy(step).wait()
    dx = dx + dx_part(down_ref[...], slice(kept * part, steps * part))
    dx = dx + pltpu.roll(dx, LANES // 2, 1)
    side = lax.broadcasted_iota(jnp.int32, (rows, LANES), 1) < LANES // 2
    tok_dev = out_ref.shape[2]
    for pair in range(samples // 2):
        first = dx[2 * pair * rows : (2 * pair + 1) * rows]
        second = dx[(2 * pair + 1) * rows : (2 * pair + 2) * rows]
        both = jnp.where(side, first, second)
        for target in range(rows // tok_dev):
            out_ref[target, pair] = both[target * tok_dev : (target + 1) * tok_dev].astype(jnp.bfloat16)


def backward(second, slope, joint, keep, down, tok_dev):
    samples = second.shape[1]
    targets = slope.shape[0] // samples // tok_dev
    units, steps = (slope.shape[1], slope.shape[1] // 256)
    vmem_spec = pl.BlockSpec(memory_space=pltpu.VMEM)
    return pl.pallas_call(
        functools.partial(backward_kernel, steps),
        out_shape=(
            jax.ShapeDtypeStruct((targets, samples // 2, tok_dev, LANES), jnp.bfloat16),
            jax.ShapeDtypeStruct((samples, down.shape[1]), jnp.bfloat16),
        ),
        in_specs=[vmem_spec] * 4 + [pl.BlockSpec(memory_space=pl.ANY)],
        out_specs=(vmem_spec,) * 2,
        scratch_shapes=[
            pltpu.VMEM((units - keep.shape[0], down.shape[1]), jnp.bfloat16),
            pltpu.SemaphoreType.DMA((steps - KEPT,)),
        ],
        compiler_params=pltpu.CompilerParams(vmem_limit_bytes=32 << 20),
        name="backward",
    )(second, slope, joint, keep, *in_hbm(down))


def pool_gradient_kernel(dpool_ref, embed_hbm, out_ref, embed_ref, sem):
    copy = pltpu.make_async_copy(embed_hbm, embed_ref, sem)
    copy.start()
    copy.wait()
    out_ref[...] = lax.dot_general(
        dpool_ref[...],
        embed_ref[...],
        (((1,), (1,)), ((), ())),
        preferred_element_type=jnp.float32,
    )


def pool_gradient(dpool, embed_w):
    vmem_spec = pl.BlockSpec(memory_space=pltpu.VMEM)
    return pl.pallas_call(
        pool_gradient_kernel,
        out_shape=jax.ShapeDtypeStruct((dpool.shape[0], embed_w.shape[0]), jnp.float32),
        in_specs=[vmem_spec, pl.BlockSpec(memory_space=pl.ANY)],
        out_specs=vmem_spec,
        scratch_shapes=[pltpu.VMEM(embed_w.shape, jnp.bfloat16), pltpu.SemaphoreType.DMA],
        compiler_params=pltpu.CompilerParams(vmem_limit_bytes=32 << 20),
        cost_estimate=pl.CostEstimate(
            flops=2 * dpool.size * embed_w.shape[0],
            bytes_accessed=2 * embed_w.size,
            transcendentals=0,
        ),
        name="pool_gradient",
    )(dpool, *in_hbm(embed_w))


def per_device_fast(qkv, positions, w_proj, latents, embed_w, up_w, down_w, head_w, labels, timesteps):
    both = ("seq", "tp")
    n_seq, n_tp = (lax.axis_size("seq"), lax.axis_size("tp"))
    count = n_seq * n_tp
    seq_index = lax.axis_index("seq")
    half = seq_index % 2
    samples, tok_dev, width = qkv.shape[1:]
    seq_len = tok_dev * count
    lat = latents.shape[2]
    heads = width // HEAD_DIM
    per_sample = count // samples
    heads_dev = heads // per_sample
    rows_dev, classes = head_w.shape
    partner = [(i, i ^ n_tp) for i in range(count)]

    def in_order(own):
        other = lax.ppermute(own, both, partner)
        mine = jnp.broadcast_to(half == 0, own.shape)
        return jnp.stack([jnp.where(mine, own, other), jnp.where(mine, other, own)])

    other = lax.ppermute(latents, both, partner)
    head_pair = in_order(head_w).reshape(2 * rows_dev, classes)

    payload, slope, joint, keep, proj_mine = forward(
        qkv, positions, latents, other, embed_w, up_w, down_w, w_proj.T, n_seq, n_tp
    )
    moved = lax.all_to_all(payload, both, 0, 0, tiled=True)

    pooled = jnp.sum(moved[:, 0].astype(jnp.float32), axis=0)
    padded = -(-classes // 256) * 256
    terms = jnp.pad(split_dot(pooled, head_pair), ((0, 0), (0, padded - classes)))
    terms = lax.dynamic_slice_in_dim(terms, half * (padded // 2), padded // 2, 1)
    terms = jnp.broadcast_to(terms.astype(jnp.bfloat16)[None], (count,) + terms.shape)
    terms = lax.all_to_all(terms, both, 0, 0, tiled=True)

    views = moved[:, 1:].reshape(count, 3, heads_dev, tok_dev, HEAD_DIM)
    views = views.transpose(1, 2, 0, 3, 4).reshape(3, heads_dev, seq_len, HEAD_DIM)
    scores = jnp.einsum(
        "hqd,hkd->hqk", views[0], views[1], preferred_element_type=jnp.float32
    ) * HEAD_DIM ** (-0.5)
    weights = jnp.exp(scores - jnp.max(scores, axis=-1, keepdims=True))
    total = jnp.sum(weights, axis=-1)
    mixed = jnp.einsum(
        "hqk,hkd->hqd", weights.astype(jnp.bfloat16), views[2], preferred_element_type=jnp.float32
    )
    attended = (mixed / total[..., None]).astype(jnp.bfloat16)
    eps_terms = jnp.einsum(
        "hqd,lhd->ql",
        attended,
        proj_mine.reshape(lat, heads_dev, HEAD_DIM),
        preferred_element_type=jnp.float32,
    )
    eps_terms = eps_terms.reshape(count, tok_dev, lat)

    terms = terms.astype(jnp.float32).reshape(n_seq // 2, 2, n_tp, samples, padded // 2)
    logits = jnp.sum(terms, axis=(0, 2))
    logits = logits.transpose(1, 0, 2).reshape(samples, padded)[:, :classes]
    probs = jax.nn.softmax(logits, axis=-1)
    onehot = (labels[:, None] == jnp.arange(classes, dtype=jnp.int32)[None, :]).astype(jnp.float32)
    share = split_dot(onehot - probs, head_w, 1)
    share = jnp.broadcast_to(share[None], (count,) + share.shape)
    second = jnp.concatenate([eps_terms, share], axis=2).astype(jnp.bfloat16)
    second = lax.all_to_all(second, both, 0, 0, tiled=True)
    eps = second[..., :lat].astype(jnp.float32).reshape(samples, per_sample, tok_dev, lat)
    eps = jnp.sum(eps, axis=1)
    eps = lax.optimization_barrier(eps)
    dx_terms, dpool = backward(second, slope, joint, keep, down_w, tok_dev)
    planes = [[first + k for k in range(2 * n_tp)] for first in range(0, count, 2 * n_tp)]
    dx_terms = lax.all_to_all(dx_terms, both, 0, 0, tiled=True, axis_index_groups=planes)
    dx = jnp.sum(dx_terms.astype(jnp.float32), axis=0)
    dx = dx.reshape(samples // 2, tok_dev, 2, lat).transpose(0, 2, 1, 3)
    dx = dx.reshape(samples, tok_dev, lat)
    dx = dx + pool_gradient(dpool, embed_w)[:, None, :]
    phase = (timesteps.astype(jnp.float32) / 1000.0 + 0.008) / 1.008 * (jnp.pi / 2)
    abar = jnp.cos(phase) ** 2
    scale = GUIDANCE * jnp.sqrt(1.0 - abar)
    return (eps - scale[:, None, None] * dx).astype(jnp.bfloat16)


def per_device(qkv, positions, w_proj, latents, embed_w, up_w, down_w, head_w, labels, timesteps):
    args = (qkv, positions, w_proj, latents, embed_w, up_w, down_w, head_w, labels, timesteps)
    n_seq = lax.axis_size("seq")
    count = n_seq * lax.axis_size("tp")
    samples, heads = (qkv.shape[1], qkv.shape[3] // HEAD_DIM)
    tok_dev, tok_seq, lat = (qkv.shape[2], latents.shape[1], latents.shape[2])
    even = count % samples == 0 and heads % max(1, count // samples) == 0
    even = even and n_seq % 2 == 0 and count // n_seq % 2 == 0 and samples == 4 and tok_dev == 4
    even = even and lat == 64 and head_w.shape[0] == 64 and tok_seq % 16 == 0
    even = even and up_w.shape[1] % 512 == 0 and tok_seq == tok_dev * (count // n_seq)
    if even and count * head_w.shape[0] == up_w.shape[0]:
        return per_device_fast(*args)
    return per_device_general(*args)


def solution(mesh):
    placed = (
        P(None, None, ("seq", "tp"), None),
        P(None, None, ("seq", "tp")),
        P(),
        P(None, "seq", None),
        P(),
        P(None, "tp"),
        P("tp", None),
        P(("seq", "tp"), None),
        P(),
        P(),
    )
    return jax.shard_map(
        per_device,
        mesh=mesh,
        in_specs=placed,
        out_specs=P(None, ("seq", "tp"), None),
        check_vma=False,
    )
```

```python
import functools

import jax
import jax.numpy as jnp
import numpy as np
from jax import lax
from jax.experimental import pallas as pl
from jax.experimental.pallas import tpu as pltpu
from jax.sharding import PartitionSpec as P

HEAD_DIM = 128


GUIDANCE = 0.1


def rope_angles(positions, head_dim):
    frame_width = head_dim // 8
    plane_width = (head_dim - frame_width) // 2
    pieces = []
    for axis, width in zip(range(3), (frame_width, plane_width, plane_width)):
        freqs = 10000.0 ** (-jnp.arange(0, width, 2, dtype=jnp.float32) / width)
        pieces.append(positions[axis][..., None] * freqs)
    return jnp.concatenate(pieces, axis=-1)


def rotate(values, angles):
    half = values.shape[-1] // 2
    floats = values.astype(jnp.float32)
    first = floats[..., :half]
    second = floats[..., half:]
    cosine = jnp.cos(angles)[:, :, None, :]
    sine = jnp.sin(angles)[:, :, None, :]
    turned = jnp.concatenate(
        [first * cosine - second * sine, first * sine + second * cosine], axis=-1
    )
    return turned.astype(jnp.bfloat16)


def gelu_slope(values):
    cdf = 0.5 * (1.0 + jax.scipy.special.erf(values * 0.7071067811865476))
    pdf = jnp.exp(-0.5 * values * values) * 0.3989422804014327
    return cdf + values * pdf


def pairs_first(array):
    samples, tokens = (array.shape[0], array.shape[1])
    return array.transpose(0, 2, 1, 3).reshape(samples * array.shape[2], tokens, HEAD_DIM)


def per_device_general(qkv, positions, w_proj, latents, embed_w, up_w, down_w, head_w, labels, timesteps):
    samples, tok_dev = (qkv.shape[1], qkv.shape[2])
    angles = rope_angles(positions.astype(jnp.float32), HEAD_DIM)
    heads = qkv.shape[3] // HEAD_DIM
    shaped = (samples, tok_dev, heads, HEAD_DIM)
    queries = rotate(qkv[0].reshape(shaped), angles)
    keys_tok = rotate(qkv[1].reshape(shaped), angles)
    values_tok = qkv[2].reshape(shaped)
    moved = lax.all_to_all(
        jnp.stack([pairs_first(queries), pairs_first(keys_tok), pairs_first(values_tok)]),
        "seq",
        split_axis=1,
        concat_axis=2,
        tiled=True,
    )
    query_pairs = moved[0]
    pair_count, query_count = (query_pairs.shape[0], query_pairs.shape[1])
    running = jnp.full((pair_count, query_count), -jnp.inf, jnp.float32)
    total = jnp.zeros((pair_count, query_count), jnp.float32)
    accum = jnp.zeros((pair_count, query_count, HEAD_DIM), jnp.float32)
    key_piece = lax.all_gather(moved[1], "tp", axis=1, tiled=True)
    value_piece = lax.all_gather(moved[2], "tp", axis=1, tiled=True)
    scores = jnp.einsum(
        "iqd,ikd->iqk", query_pairs, key_piece, preferred_element_type=jnp.float32
    ) * HEAD_DIM ** (-0.5)
    newest = jnp.max(scores, axis=-1)
    factor = jnp.exp(running - newest)
    weights = jnp.exp(scores - newest[..., None])
    total = total * factor + jnp.sum(weights, axis=-1)
    accum = accum * factor[..., None] + jnp.einsum(
        "iqk,ikd->iqd",
        weights.astype(jnp.bfloat16),
        value_piece,
        preferred_element_type=jnp.float32,
    )
    running, total, accum = (newest, total, accum)
    attended = (accum / total[..., None]).astype(jnp.bfloat16)
    returned = lax.all_to_all(attended, "seq", split_axis=1, concat_axis=0, tiled=True)
    returned = returned.reshape(samples, heads, tok_dev, HEAD_DIM).transpose(0, 2, 1, 3)
    returned = returned.reshape(samples, tok_dev, qkv.shape[3])
    eps = jnp.dot(returned, w_proj, preferred_element_type=jnp.float32)
    seq_len = latents.shape[1] * lax.axis_size("seq")
    tp_index = lax.axis_index("tp")
    emb = jnp.dot(latents, embed_w, preferred_element_type=jnp.float32).astype(jnp.bfloat16)
    hidden = jnp.dot(emb, up_w, preferred_element_type=jnp.float32)
    act = jax.nn.gelu(hidden, approximate=False).astype(jnp.bfloat16)
    branch = jnp.dot(act, down_w, preferred_element_type=jnp.float32)
    own_emb = lax.dynamic_slice_in_dim(emb, tp_index * tok_dev, tok_dev, 1).astype(jnp.float32)
    partial_pool = jnp.sum(branch, axis=1) + jnp.sum(own_emb, axis=1)
    head_rows = head_w.shape[0]
    flat_index = lax.axis_index("seq") * lax.axis_size("tp") + tp_index
    pooled = lax.psum(partial_pool, ("seq", "tp")) / seq_len
    pooled_share = lax.dynamic_slice_in_dim(pooled, flat_index * head_rows, head_rows, 1)
    head_float = head_w.astype(jnp.float32)
    logit_terms = jnp.dot(pooled_share, head_float, precision=lax.Precision.HIGHEST)
    logits = lax.psum(logit_terms, ("seq", "tp"))
    probs = jax.nn.softmax(logits, axis=-1)
    onehot = (labels[:, None] == jnp.arange(logits.shape[1], dtype=jnp.int32)[None, :]).astype(
        jnp.float32
    )
    grad_share = jnp.dot(onehot - probs, head_float.T, precision=lax.Precision.HIGHEST)
    dpool = lax.all_gather(grad_share, ("seq", "tp"), axis=1, tiled=True)
    dact = jnp.dot(dpool, down_w.astype(jnp.float32).T, precision=lax.Precision.HIGHEST)
    dh1 = (gelu_slope(hidden) * dact[:, None, :]).astype(jnp.bfloat16)
    demb = jnp.einsum("btf,cf->btc", dh1, up_w, preferred_element_type=jnp.float32)
    embed_float = embed_w.astype(jnp.float32)
    dx_terms = jnp.einsum("btc,lc->btl", demb, embed_float, precision=lax.Precision.HIGHEST)
    dx_mine = lax.psum_scatter(
        dx_terms.astype(jnp.bfloat16), "tp", scatter_dimension=1, tiled=True
    ).astype(jnp.float32)
    dx_pool = jnp.dot(dpool, embed_float.T, precision=lax.Precision.HIGHEST)
    dx_total = dx_mine + dx_pool[:, None, :]
    phase = (timesteps.astype(jnp.float32) / 1000.0 + 0.008) / 1.008 * (jnp.pi / 2)
    abar = jnp.cos(phase) ** 2
    scale = GUIDANCE * jnp.sqrt(1.0 - abar)
    return (eps - scale[:, None, None] * dx_total).astype(jnp.bfloat16)


def rounded(values):
    return lax.reduce_precision(values, exponent_bits=8, mantissa_bits=7)


def split_rows(values):
    high = rounded(values)
    return jnp.concatenate([high, values - high], axis=0).astype(jnp.bfloat16)


def split_dot(values, weights, contract=0):
    rows = values.shape[0]
    product = lax.dot_general(
        split_rows(values),
        weights,
        (((1,), (contract,)), ((), ())),
        preferred_element_type=jnp.float32,
    )
    return product[:rows] + product[rows:]


def split_two(values, axis):
    high = rounded(values)
    return jnp.concatenate([high, values - high], axis=axis).astype(jnp.bfloat16)


LANES = 128


KEPT = 2


def in_hbm(*arrays):
    return [pltpu.with_memory_space_constraint(array, pltpu.HBM) for array in arrays]


def lane_frequencies():
    frame_width = HEAD_DIM // 8
    plane_width = (HEAD_DIM - frame_width) // 2
    freqs, axes = [], []
    for axis, width in zip(range(3), (frame_width, plane_width, plane_width)):
        steps = np.arange(0, width, 2, dtype=np.float32) / np.float32(width)
        freqs.append(np.float32(10000.0) ** (-steps))
        axes.append(np.full(width // 2, axis, np.float32))
    freqs, axes = (np.concatenate(freqs), np.concatenate(axes))
    table = np.stack([np.tile(freqs, 2), np.tile(axes, 2)]).astype(np.float32)
    return np.pad(table, ((0, 6), (0, 0)))


def forward_kernel(
    sizes,
    pos_hbm,
    table_hbm,
    qkv_hbm,
    own_hbm,
    other_hbm,
    embed_hbm,
    up_hbm,
    down_hbm,
    proj_hbm,
    pay_ref,
    slope_ref,
    joint_ref,
    keep_ref,
    proj_ref,
    pos_ref,
    table_ref,
    qkv_ref,
    lat_ref,
    embed_ref,
    up_ref,
    down_ref,
    rows_ref,
    sems,
):
    n_seq, n_tp, steps, seq_len = sizes
    samples, tok_dev, width = qkv_ref.shape[1:]
    count = n_seq * n_tp
    per_sample = count // samples
    heads_dev = width // HEAD_DIM // per_sample
    tok_seq, lat = own_hbm.shape[1:]
    units = slope_ref.shape[1]
    part = units // steps
    kept = keep_ref.shape[0] // part
    half = lax.axis_index("seq") % 2

    def up_copy(step):
        start = pl.multiple_of(half * units + step * part, LANES)
        return pltpu.make_async_copy(
            up_hbm.at[:, pl.ds(start, part)], up_ref.at[step], sems.at[6 + step]
        )

    def down_at(step):
        if step < kept:
            return keep_ref.at[pl.ds(step * part, part)]
        return down_ref.at[pl.ds((step - kept) * part, part)]

    def down_copy(step):
        start = pl.multiple_of(half * units + step * part, LANES)
        return pltpu.make_async_copy(
            down_hbm.at[pl.ds(start, part)],
            down_at(step),
            sems.at[6 + steps + step],
        )

    own_copy = pltpu.make_async_copy(own_hbm, lat_ref.at[half], sems.at[0])
    other_copy = pltpu.make_async_copy(other_hbm, lat_ref.at[1 - half], sems.at[1])
    embed_copy = pltpu.make_async_copy(embed_hbm, embed_ref, sems.at[2])
    qkv_copy = pltpu.make_async_copy(qkv_hbm, qkv_ref, sems.at[3])
    chunk = proj_ref.shape[1]
    flat = lax.axis_index("seq") * n_tp + lax.axis_index("tp")
    first_column = pl.multiple_of(lax.rem(flat, per_sample) * chunk, chunk)
    proj_copy = pltpu.make_async_copy(
        proj_hbm.at[:, pl.ds(first_column, chunk)], proj_ref, sems.at[6 + 2 * steps]
    )
    pos_copy = pltpu.make_async_copy(pos_hbm, pos_ref, sems.at[4])
    table_copy = pltpu.make_async_copy(table_hbm, table_ref, sems.at[5])
    for copy in (pos_copy, table_copy, own_copy, other_copy, embed_copy, up_copy(0), qkv_copy):
        copy.start()
    for step in range(1, steps):
        up_copy(step).start()
    for step in range(steps):
        down_copy(step).start()
    proj_copy.start()

    pos_copy.wait()
    table_copy.wait()

    shape = (samples * tok_dev, LANES)
    row = lax.broadcasted_iota(jnp.int32, shape, 0)
    lane = lax.broadcasted_iota(jnp.int32, shape, 1)
    axis = jnp.broadcast_to(table_ref[1:2, :], shape)
    angles = jnp.zeros(shape, jnp.float32)
    for index in range(samples * tok_dev):
        sample, token = divmod(index, tok_dev)
        frame, line, column = (pos_ref[k, sample, token].astype(jnp.float32) for k in range(3))
        value = jnp.where(axis < 0.5, frame, jnp.where(axis < 1.5, line, column))
        angles = jnp.where(row == index, value, angles)
    angles = angles * jnp.broadcast_to(table_ref[0:1, :], shape)
    cosine = jnp.cos(angles)
    sine = jnp.sin(angles)
    sine = jnp.where(lane < HEAD_DIM // 2, -sine, sine)

    def pack(sample):
        cos_rows = cosine[sample * tok_dev : (sample + 1) * tok_dev]
        sin_rows = sine[sample * tok_dev : (sample + 1) * tok_dev]
        for head in range(width // HEAD_DIM):
            target = sample * per_sample + head // heads_dev
            span = slice(head * HEAD_DIM, (head + 1) * HEAD_DIM)
            for kind in range(3):
                group = 1 + kind * heads_dev + head % heads_dev
                values = qkv_ref[kind, sample, :, span]
                if kind < 2:
                    values = values.astype(jnp.float32)
                    values = values * cos_rows + pltpu.roll(values, HEAD_DIM // 2, 1) * sin_rows
                pay_ref[target, group] = values.astype(jnp.bfloat16)

    own_copy.wait()
    other_copy.wait()
    tok_pair = 2 * tok_seq
    sums = []
    for sample in range(samples):
        pieces = [lat_ref[0, sample], lat_ref[1, sample]]
        rows = jnp.concatenate(pieces, axis=0)
        rows_ref[sample * tok_pair : (sample + 1) * tok_pair] = jnp.concatenate([rows, rows], axis=1)
        sums.append(jnp.sum(rows.astype(jnp.float32), axis=0, keepdims=True))
    lat_sum = jnp.concatenate(sums, axis=0) * (1.0 / (2 * n_tp))
    lat_high = lat_sum.astype(jnp.bfloat16)
    lat_low = (lat_sum - lat_high.astype(jnp.float32)).astype(jnp.bfloat16)
    lat_rows = rows_ref[...]

    embed_copy.wait()
    embed = embed_ref[...]
    total = jnp.dot(
        jnp.concatenate([lat_high, lat_low], axis=0), embed, preferred_element_type=jnp.float32
    )

    def activate(first, last):
        span = slice(first * part, last * part)
        hidden = jnp.dot(lat_rows, joint_ref[:, span], preferred_element_type=jnp.float32)
        cdf = 0.5 * (1.0 + lax.erf(hidden * 0.7071067811865476))
        pdf = jnp.exp(-0.5 * hidden * hidden) * 0.3989422804014327
        slope_ref[:, span] = (cdf + hidden * pdf).astype(jnp.bfloat16)
        act_sum = jnp.sum((hidden * cdf).reshape(samples, tok_pair, (last - first) * part), axis=1)
        high = act_sum.astype(jnp.bfloat16)
        low = (act_sum - high.astype(jnp.float32)).astype(jnp.bfloat16)
        return jnp.concatenate([high, low], axis=0)

    packed = 0
    for step in range(steps):
        up_copy(step).wait()
        joint = jnp.dot(embed, up_ref[step], preferred_element_type=jnp.float32)
        if step == 0:
            qkv_copy.wait()
        while packed * steps < samples * (step + 1):
            pack(packed)
            packed += 1
        if step == kept:
            acts = activate(0, kept)
        high = joint.astype(jnp.bfloat16)
        low = (joint - high.astype(jnp.float32)).astype(jnp.bfloat16)
        joint_ref[:, step * part : (step + 1) * part] = jnp.concatenate([high, low], axis=0)
    for step in range(kept):
        down_copy(step).wait()
    total = total + jnp.dot(acts, keep_ref[...], preferred_element_type=jnp.float32)
    acts = activate(kept, steps)
    for step in range(kept, steps):
        down_copy(step).wait()
    total = total + jnp.dot(acts, down_ref[...], preferred_element_type=jnp.float32)
    proj_copy.wait()
    pool = (total[:samples] + total[samples:]) * (1.0 / seq_len)
    side = lax.broadcasted_iota(jnp.int32, (samples, LANES), 1) < LANES // 2
    for plane in range(n_seq // 2):
        for column in range(n_tp):
            first = (plane * 2 * n_tp + column) // 2
            second = (plane * 2 * n_tp + n_tp + column) // 2
            first = pool[:, first * LANES : (first + 1) * LANES]
            second = pool[:, second * LANES : (second + 1) * LANES]
            if column % 2 == 0:
                block = jnp.where(side, first, pltpu.roll(second, LANES // 2, 1))
            else:
                block = jnp.where(side, pltpu.roll(first, LANES // 2, 1), second)
            for core in range(2):
                target = (plane * 2 + core) * n_tp + column
                pay_ref[target, 0] = block.astype(jnp.bfloat16)


def forward(qkv, positions, own, other, embed_w, up_w, down_w, w_proj, n_seq, n_tp):
    samples, tok_dev, width = qkv.shape[1:]
    count = n_seq * n_tp
    groups = 1 + 3 * (width // HEAD_DIM // (count // samples))
    tok_seq, lat = own.shape[1:]
    units, features = (up_w.shape[1] // 2, up_w.shape[0])
    steps = units // 256
    rows = 2 * tok_seq * samples
    any_spec = pl.BlockSpec(memory_space=pl.ANY)
    vmem_spec = pl.BlockSpec(memory_space=pltpu.VMEM)
    return pl.pallas_call(
        functools.partial(forward_kernel, (n_seq, n_tp, steps, tok_dev * count)),
        out_shape=(
            jax.ShapeDtypeStruct((count, groups, tok_dev, LANES), jnp.bfloat16),
            jax.ShapeDtypeStruct((rows, units), jnp.bfloat16),
            jax.ShapeDtypeStruct((2 * lat, units), jnp.bfloat16),
            jax.ShapeDtypeStruct((KEPT * 256, features), jnp.bfloat16),
            jax.ShapeDtypeStruct((lat, width * samples // count), jnp.bfloat16),
        ),
        in_specs=[any_spec] * 9,
        out_specs=(vmem_spec,) * 5,
        scratch_shapes=[
            pltpu.SMEM(positions.shape, jnp.int32),
            pltpu.VMEM((8, LANES), jnp.float32),
            pltpu.VMEM(qkv.shape, jnp.bfloat16),
            pltpu.VMEM((2,) + own.shape, jnp.bfloat16),
            pltpu.VMEM(embed_w.shape, jnp.bfloat16),
            pltpu.VMEM((steps, features, 256), jnp.bfloat16),
            pltpu.VMEM((units - KEPT * 256, features), jnp.bfloat16),
            pltpu.VMEM((rows, 2 * lat), jnp.bfloat16),
            pltpu.SemaphoreType.DMA((7 + 2 * steps,)),
        ],
        compiler_params=pltpu.CompilerParams(vmem_limit_bytes=32 << 20),
        cost_estimate=pl.CostEstimate(
            flops=4 * features * units * 64, bytes_accessed=4 * features * units, transcendentals=0
        ),
        name="forward",
    )(*in_hbm(positions, jnp.asarray(lane_frequencies()), qkv, own), other, *in_hbm(embed_w, up_w, down_w, w_proj))


def backward_kernel(
    steps, second_ref, slope_ref, joint_ref, keep_ref, down_hbm, out_ref, dpool_ref, down_ref, sems
):
    count, samples, _ = second_ref.shape
    units = slope_ref.shape[1]
    part = units // steps
    kept = keep_ref.shape[0] // part
    half = lax.axis_index("seq") % 2

    def down_copy(step):
        start = pl.multiple_of(half * units + step * part, LANES)
        return pltpu.make_async_copy(
            down_hbm.at[pl.ds(start, part)],
            down_ref.at[pl.ds((step - kept) * part, part)],
            sems.at[step - kept],
        )

    for step in range(kept, steps):
        down_copy(step).start()
    rows = slope_ref.shape[0] // samples
    side = lax.broadcasted_iota(jnp.int32, (samples, LANES), 1) < LANES // 2
    for pair in range(count // 2):
        first = second_ref[2 * pair].astype(jnp.float32)
        second = second_ref[2 * pair + 1].astype(jnp.float32)
        block = jnp.where(side, pltpu.roll(first, LANES // 2, 1), second)
        dpool_ref[:, pair * LANES : (pair + 1) * LANES] = block.astype(jnp.bfloat16)
    dpool = dpool_ref[...]
    across = (((1,), (1,)), ((), ()))

    def dx_part(weights, span):
        dact = lax.dot_general(dpool, weights, across, preferred_element_type=jnp.float32)
        size = span.stop - span.start
        slope = slope_ref[:, span].astype(jnp.float32).reshape(samples, rows, size)
        dh1 = (slope * dact[:, None, :]).reshape(samples * rows, size).astype(jnp.bfloat16)
        return lax.dot_general(dh1, joint_ref[:, span], across, preferred_element_type=jnp.float32)

    dx = dx_part(keep_ref[...], slice(0, kept * part))
    for step in range(kept, steps):
        down_copy(step).wait()
    dx = dx + dx_part(down_ref[...], slice(kept * part, steps * part))
    dx = dx + pltpu.roll(dx, LANES // 2, 1)
    side = lax.broadcasted_iota(jnp.int32, (rows, LANES), 1) < LANES // 2
    tok_dev = out_ref.shape[2]
    for pair in range(samples // 2):
        first = dx[2 * pair * rows : (2 * pair + 1) * rows]
        second = dx[(2 * pair + 1) * rows : (2 * pair + 2) * rows]
        both = jnp.where(side, first, second)
        for target in range(rows // tok_dev):
            out_ref[target, pair] = both[target * tok_dev : (target + 1) * tok_dev].astype(jnp.bfloat16)


def backward(second, slope, joint, keep, down, tok_dev):
    samples = second.shape[1]
    targets = slope.shape[0] // samples // tok_dev
    units, steps = (slope.shape[1], slope.shape[1] // 256)
    vmem_spec = pl.BlockSpec(memory_space=pltpu.VMEM)
    return pl.pallas_call(
        functools.partial(backward_kernel, steps),
        out_shape=(
            jax.ShapeDtypeStruct((targets, samples // 2, tok_dev, LANES), jnp.bfloat16),
            jax.ShapeDtypeStruct((samples, down.shape[1]), jnp.bfloat16),
        ),
        in_specs=[vmem_spec] * 4 + [pl.BlockSpec(memory_space=pl.ANY)],
        out_specs=(vmem_spec,) * 2,
        scratch_shapes=[
            pltpu.VMEM((units - keep.shape[0], down.shape[1]), jnp.bfloat16),
            pltpu.SemaphoreType.DMA((steps - KEPT,)),
        ],
        compiler_params=pltpu.CompilerParams(vmem_limit_bytes=32 << 20),
        name="backward",
    )(second, slope, joint, keep, *in_hbm(down))


def pool_gradient_kernel(dpool_ref, embed_hbm, out_ref, embed_ref, sem):
    copy = pltpu.make_async_copy(embed_hbm, embed_ref, sem)
    copy.start()
    copy.wait()
    out_ref[...] = lax.dot_general(
        dpool_ref[...],
        embed_ref[...],
        (((1,), (1,)), ((), ())),
        preferred_element_type=jnp.float32,
    )


def pool_gradient(dpool, embed_w):
    vmem_spec = pl.BlockSpec(memory_space=pltpu.VMEM)
    return pl.pallas_call(
        pool_gradient_kernel,
        out_shape=jax.ShapeDtypeStruct((dpool.shape[0], embed_w.shape[0]), jnp.float32),
        in_specs=[vmem_spec, pl.BlockSpec(memory_space=pl.ANY)],
        out_specs=vmem_spec,
        scratch_shapes=[pltpu.VMEM(embed_w.shape, jnp.bfloat16), pltpu.SemaphoreType.DMA],
        compiler_params=pltpu.CompilerParams(vmem_limit_bytes=32 << 20),
        cost_estimate=pl.CostEstimate(
            flops=2 * dpool.size * embed_w.shape[0],
            bytes_accessed=2 * embed_w.size,
            transcendentals=0,
        ),
        name="pool_gradient",
    )(dpool, *in_hbm(embed_w))


def per_device_fast(qkv, positions, w_proj, latents, embed_w, up_w, down_w, head_w, labels, timesteps):
    both = ("seq", "tp")
    n_seq, n_tp = (lax.axis_size("seq"), lax.axis_size("tp"))
    count = n_seq * n_tp
    seq_index = lax.axis_index("seq")
    half = seq_index % 2
    samples, tok_dev, width = qkv.shape[1:]
    seq_len = tok_dev * count
    lat = latents.shape[2]
    heads = width // HEAD_DIM
    per_sample = count // samples
    heads_dev = heads // per_sample
    rows_dev, classes = head_w.shape
    partner = [(i, i ^ n_tp) for i in range(count)]

    def in_order(own):
        other = lax.ppermute(own, both, partner)
        mine = jnp.broadcast_to(half == 0, own.shape)
        return jnp.stack([jnp.where(mine, own, other), jnp.where(mine, other, own)])

    other = lax.ppermute(latents, both, partner)
    head_pair = in_order(head_w).reshape(2 * rows_dev, classes)

    payload, slope, joint, keep, proj_mine = forward(
        qkv, positions, latents, other, embed_w, up_w, down_w, w_proj.T, n_seq, n_tp
    )
    moved = lax.all_to_all(payload, both, 0, 0, tiled=True)

    pooled = jnp.sum(moved[:, 0].astype(jnp.float32), axis=0)
    padded = -(-classes // 256) * 256
    terms = jnp.pad(split_dot(pooled, head_pair), ((0, 0), (0, padded - classes)))
    terms = lax.dynamic_slice_in_dim(terms, half * (padded // 2), padded // 2, 1)
    terms = jnp.broadcast_to(terms.astype(jnp.bfloat16)[None], (count,) + terms.shape)
    terms = lax.all_to_all(terms, both, 0, 0, tiled=True)

    views = moved[:, 1:].reshape(count, 3, heads_dev, tok_dev, HEAD_DIM)
    views = views.transpose(1, 2, 0, 3, 4).reshape(3, heads_dev, seq_len, HEAD_DIM)
    scores = jnp.einsum(
        "hqd,hkd->hqk", views[0], views[1], preferred_element_type=jnp.float32
    ) * HEAD_DIM ** (-0.5)
    weights = jnp.exp(scores - jnp.max(scores, axis=-1, keepdims=True))
    total = jnp.sum(weights, axis=-1)
    mixed = jnp.einsum(
        "hqk,hkd->hqd", weights.astype(jnp.bfloat16), views[2], preferred_element_type=jnp.float32
    )
    attended = (mixed / total[..., None]).astype(jnp.bfloat16)
    eps_terms = jnp.einsum(
        "hqd,lhd->ql",
        attended,
        proj_mine.reshape(lat, heads_dev, HEAD_DIM),
        preferred_element_type=jnp.float32,
    )
    eps_terms = eps_terms.reshape(count, tok_dev, lat)

    terms = terms.astype(jnp.float32).reshape(n_seq // 2, 2, n_tp, samples, padded // 2)
    logits = jnp.sum(terms, axis=(0, 2))
    logits = logits.transpose(1, 0, 2).reshape(samples, padded)[:, :classes]
    probs = jax.nn.softmax(logits, axis=-1)
    onehot = (labels[:, None] == jnp.arange(classes, dtype=jnp.int32)[None, :]).astype(jnp.float32)
    share = split_dot(onehot - probs, head_w, 1)
    share = jnp.broadcast_to(share[None], (count,) + share.shape)
    second = jnp.concatenate([eps_terms, share], axis=2).astype(jnp.bfloat16)
    second = lax.all_to_all(second, both, 0, 0, tiled=True)
    eps = second[..., :lat].astype(jnp.float32).reshape(samples, per_sample, tok_dev, lat)
    eps = jnp.sum(eps, axis=1)
    eps = lax.optimization_barrier(eps)
    dx_terms, dpool = backward(second, slope, joint, keep, down_w, tok_dev)
    planes = [[first + k for k in range(2 * n_tp)] for first in range(0, count, 2 * n_tp)]
    dx_terms = lax.all_to_all(dx_terms, both, 0, 0, tiled=True, axis_index_groups=planes)
    dx = jnp.sum(dx_terms.astype(jnp.float32), axis=0)
    dx = dx.reshape(samples // 2, tok_dev, 2, lat).transpose(0, 2, 1, 3)
    dx = dx.reshape(samples, tok_dev, lat)
    dx = dx + pool_gradient(dpool, embed_w)[:, None, :]
    phase = (timesteps.astype(jnp.float32) / 1000.0 + 0.008) / 1.008 * (jnp.pi / 2)
    abar = jnp.cos(phase) ** 2
    scale = GUIDANCE * jnp.sqrt(1.0 - abar)
    return (eps - scale[:, None, None] * dx).astype(jnp.bfloat16)


def per_device(qkv, positions, w_proj, latents, embed_w, up_w, down_w, head_w, labels, timesteps):
    args = (qkv, positions, w_proj, latents, embed_w, up_w, down_w, head_w, labels, timesteps)
    n_seq = lax.axis_size("seq")
    count = n_seq * lax.axis_size("tp")
    samples, heads = (qkv.shape[1], qkv.shape[3] // HEAD_DIM)
    tok_dev, tok_seq, lat = (qkv.shape[2], latents.shape[1], latents.shape[2])
    even = count % samples == 0 and heads % max(1, count // samples) == 0
    even = even and n_seq % 2 == 0 and count // n_seq % 2 == 0 and samples == 4 and tok_dev == 4
    even = even and lat == 64 and head_w.shape[0] == 64 and tok_seq % 16 == 0
    even = even and up_w.shape[1] % 512 == 0 and tok_seq == tok_dev * (count // n_seq)
    if even and count * head_w.shape[0] == up_w.shape[0]:
        return per_device_fast(*args)
    return per_device_general(*args)


def solution(mesh):
    placed = (
        P(None, None, ("seq", "tp"), None),
        P(None, None, ("seq", "tp")),
        P(),
        P(None, "seq", None),
        P(),
        P(None, "tp"),
        P("tp", None),
        P(("seq", "tp"), None),
        P(),
        P(),
    )
    return jax.shard_map(
        per_device,
        mesh=mesh,
        in_specs=placed,
        out_specs=P(None, ("seq", "tp"), None),
        check_vma=False,
    )
```
